32 devices in a mesh: seq: 16 (over z, y, core), fsdp: 2 (over x).
Axes of the slice: x: 2, y: 2, z: 4, core: 2. Of those that a mesh axis runs over, the one named last changes fastest.
Arguments:
- patches: bfloat16 [2, 8192, 1024], P('fsdp', 'seq'), may hold values from -6 to 6
- pos_embed: bfloat16 [2, 8192, 1024], P('fsdp', 'seq'), may hold values from -4 to 4
- lengths: int32 [2, 8], P('fsdp'), may hold values from 1 to 2304, 8192 in all within a row
- out_grad: bfloat16 [2, 8192, 1024], P('fsdp', 'seq'), may hold values from -6 to 6
- ln1_gain: bfloat16 [1024], P('fsdp'), may hold values from 0.5 to 1.5
- ln1_bias: bfloat16 [1024], P('fsdp'), may hold values from -1 to 1
- w_qkv: bfloat16 [1024, 3072], P('fsdp'), may hold values from -0.1875 to 0.1875
- b_qv: bfloat16 [2048], P('fsdp'), may hold values from -1 to 1
- w_out: bfloat16 [1024, 1024], P('fsdp'), may hold values from -3 to 3
- b_out: bfloat16 [1024], P('fsdp'), may hold values from -1 to 1
- ln2_gain: bfloat16 [1024], P('fsdp'), may hold values from 0.5 to 1.5
- ln2_bias: bfloat16 [1024], P('fsdp'), may hold values from -1 to 1
- w_fc1: bfloat16 [1024, 4096], P('fsdp'), may hold values from -0.1875 to 0.1875
- b_fc1: bfloat16 [4096], P('fsdp'), may hold values from -1 to 1
- w_fc2: bfloat16 [4096, 1024], P('fsdp'), may hold values from -0.09375 to 0.09375
- b_fc2: bfloat16 [1024], P('fsdp'), may hold values from -1 to 1
Outputs:
- block_out: bfloat16 [2, 8192, 1024], P('fsdp', 'seq')
- patch_grad: float32 [2, 8192, 1024], P('fsdp', 'seq')
- ln1_gain_grad: float32 [1024], P('fsdp')
- ln1_bias_grad: float32 [1024], P('fsdp')
- w_qkv_grad: float32 [1024, 3072], P('fsdp')
- b_qv_grad: float32 [2048], P('fsdp')
- w_out_grad: float32 [1024, 1024], P('fsdp')
- b_out_grad: float32 [1024], P('fsdp')
- ln2_gain_grad: float32 [1024], P('fsdp')
- ln2_bias_grad: float32 [1024], P('fsdp')
- w_fc1_grad: float32 [1024, 4096], P('fsdp')
- b_fc1_grad: float32 [4096], P('fsdp')
- w_fc2_grad: float32 [4096, 1024], P('fsdp')
- b_fc2_grad: float32 [1024], P('fsdp')
The draws below stay inside these ranges and needn't reach their ends.
Inputs may be any that keep to these rules, and one draw needn't show every extreme that they name: The patches of pack b are its 8 images one after another in the order of lengths[b]; they add up to 8192, and in every pack one image has exactly 2304 patches.
All inputs are finite; a program needn't handle non-finite values.
Results may differ from the reference program's by a relative error of at most 0.0099.
Values may be sent and summed in bfloat16 or wider, within the bound.
No kernel may reach another device: no remote copies, remote signals or barrier semaphores. Data moves between devices by JAX's collectives and lax.ppermute only.
A program may use at most 320 MiB of HBM per device.

```python
import math
import jax
import jax.numpy as jnp
import numpy as np
from jax import lax

D = 1024
HEADS = 16
HEAD_DIM = 64
FF = 4096
TOK_DEV = 512
LONG = 2304
TOKENS = 8192
BATCHES = 2
IMAGES = 8


def block_levels(rng, shape, pieces, smallest, top_value):
    factor_of, own = 1.0, jax.random.fold_in(rng, 6)
    for dim, shards_of in pieces:
        steps = jnp.exp(jax.random.uniform(jax.random.fold_in(own, dim), (shards_of,), jnp.float32, smallest / len(pieces), top_value / len(pieces)))
        factor_of = factor_of * jnp.repeat(steps, shape[dim] // shards_of).reshape([-1 if axis == dim else 1 for axis in range(len(shape))])
    return factor_of


def length_profile(amount, total, bound, skew):
    portions = [(1 << 20) // math.isqrt(standing ** skew) + 1 for standing in range(2, amount + 1)]
    surplus, holding = total - bound - (amount - 1), [1] * (amount - 1)
    while surplus > 0:
        candidates = [i for i in range(amount - 1) if holding[i] < bound]
        mass, remaining = sum([portions[i] for i in candidates]), surplus
        for i in candidates:
            extra = min(bound - holding[i], max(1, remaining * portions[i] // mass), surplus)
            holding[i] = holding[i] + extra
            surplus = surplus - extra
    return np.array([bound] + holding)


def ragged(own_key, count, total, reach, skew):
    if count == 2:
        one = jax.random.randint(own_key, (), max(1, total - reach), min(reach, total - 1) + 1)
        return jnp.stack([one, total - one])
    sizes = jnp.asarray(length_profile(count, total, reach, skew), jnp.int32)
    pairs = (count - 1) // 2
    source_of, receiver = sizes[1:1 + 2 * pairs:2], sizes[2:2 + 2 * pairs:2]
    slack = jnp.minimum(source_of - 1, reach - receiver)
    passed = jax.random.randint(jax.random.fold_in(own_key, 1), (pairs,), 0, 1 << 20) % (slack + 1)
    sizes = sizes.at[1:1 + 2 * pairs:2].set(source_of - passed).at[2:2 + 2 * pairs:2].set(receiver + passed)
    return sizes[jax.random.permutation(jax.random.fold_in(own_key, 2), count)]


def bell_draw(own_key, dims, scale, most, split=(), kind=jnp.bfloat16):
    result = jax.random.normal(own_key, dims, jnp.float32) * scale
    if len(split) > 0:
        result = block_levels(own_key, dims, split, -0.22, 0.18) * result
    return jnp.clip(result, min=-most, max=most).astype(kind)


def setup_inputs(seed: int = 0) -> dict:
    arg_keys = jax.random.split(jax.random.key(seed), 17)
    return {
        "patches": bell_draw(arg_keys[0], (BATCHES, TOKENS, D), 1.0, 6.0, ((0, 2), (1, 16))),
        "pos_embed": bell_draw(arg_keys[1], (BATCHES, TOKENS, D), 0.5, 4.0, ((0, 2), (1, 16))),
        "lengths": jax.vmap(lambda own: ragged(own, IMAGES, TOKENS, LONG, 1))(jax.random.split(arg_keys[2], BATCHES)).reshape((BATCHES, IMAGES)).astype(jnp.int32),
        "out_grad": bell_draw(arg_keys[3], (BATCHES, TOKENS, D), 1.0, 6.0, ((0, 2), (1, 16))),
        "ln1_gain": jnp.clip(1.0 + 0.1 * jax.random.normal(arg_keys[4], (D,), jnp.float32), 0.5, 1.5).astype(jnp.bfloat16),
        "ln1_bias": bell_draw(arg_keys[5], (D,), 0.2, 1.0, ((0, 2),)),
        "w_qkv": bell_draw(arg_keys[6], (D, 3 * D), D ** -0.5, 0.1875, ((0, 2),)),
        "b_qv": bell_draw(arg_keys[7], (2 * D,), 0.2, 1.0, ((0, 2),)),
        "w_out": bell_draw(arg_keys[8], (D, D), (max(D // 256, 1)) ** -0.5, 3.0, ((0, 2),)),
        "b_out": bell_draw(arg_keys[9], (D,), 0.2, 1.0, ((0, 2),)),
        "ln2_gain": jnp.clip(1.0 + 0.1 * jax.random.normal(arg_keys[10], (D,), jnp.float32), 0.5, 1.5).astype(jnp.bfloat16),
        "ln2_bias": bell_draw(arg_keys[11], (D,), 0.2, 1.0, ((0, 2),)),
        "w_fc1": bell_draw(arg_keys[12], (D, FF), D ** -0.5, 0.1875, ((0, 2),)),
        "b_fc1": bell_draw(arg_keys[13], (FF,), 0.2, 1.0, ((0, 2),)),
        "w_fc2": bell_draw(arg_keys[14], (FF, D), FF ** -0.5, 0.09375, ((0, 2),)),
        "b_fc2": bell_draw(arg_keys[15], (D,), 0.2, 1.0, ((0, 2),)),
    }


NORM_EPS = 1e-06
MASKED = -1e+30

@jax.custom_vjp
def low(v):
    return lax.optimization_barrier(v.astype(jnp.bfloat16)).astype(jnp.float32)

@jax.custom_vjp
def low_back(v):
    return v

def low_keep(v):
    return (low(v), None)

def low_pass(kept, grad):
    return (grad,)

def back_keep(v):
    return (v, None)

def back_low(kept, grad):
    return (low(grad),)
low.defvjp(low_keep, low_pass)
low_back.defvjp(back_keep, back_low)

def matmul(first_mat, second_mat):
    return jnp.dot(first_mat, second_mat, precision=lax.Precision.HIGHEST)

def layer_norm(hidden, gain_vec, offset_vec):
    centre = hidden - lax.optimization_barrier(jnp.mean(hidden, axis=-1, keepdims=True))
    spread = lax.optimization_barrier(jnp.mean(centre * centre, axis=-1, keepdims=True))
    return centre * lax.rsqrt(spread + NORM_EPS) * gain_vec + offset_vec

def segment_ids(lengths):
    image_ends = jnp.cumsum(lengths).astype(jnp.int32)
    places = jnp.arange(TOKENS, dtype=jnp.int32)
    return lax.optimization_barrier(jnp.sum((places[:, None] >= image_ends[None, :]).astype(jnp.int32), axis=1)).astype(jnp.int32)

def attend(queries, keys, values, segments):
    key_reach = (LONG + TOK_DEV - 2) // TOK_DEV
    margin = key_reach * TOK_DEV
    window_len = (2 * key_reach + 1) * TOK_DEV
    keys_pad = jnp.pad(keys, ((margin, margin), (0, 0)))
    values_pad = jnp.pad(values, ((margin, margin), (0, 0)))
    segs_pad = jnp.pad(segments, (margin, margin), constant_values=-1)
    score_scale = HEAD_DIM ** (-0.5)

    def attend_block(first_row):
        query_rows = lax.dynamic_slice_in_dim(queries, first_row, TOK_DEV, 0).reshape(TOK_DEV, HEADS, HEAD_DIM)
        near_keys = lax.dynamic_slice_in_dim(keys_pad, first_row, window_len, 0).reshape(window_len, HEADS, HEAD_DIM)
        near_values = lax.dynamic_slice_in_dim(values_pad, first_row, window_len, 0).reshape(window_len, HEADS, HEAD_DIM)
        own_segs = lax.dynamic_slice_in_dim(segments, first_row, TOK_DEV, 0)
        near_segs = lax.dynamic_slice_in_dim(segs_pad, first_row, window_len, 0)
        same_image = own_segs[:, None] == near_segs[None, :]
        scores = low_back(jnp.einsum('qhd,khd->hqk', query_rows, near_keys, precision=lax.Precision.HIGHEST) * score_scale)
        scores = jnp.where(same_image[None], scores, MASKED)
        weights = low(jax.nn.softmax(scores, axis=-1))
        attended = jnp.einsum('hqk,khd->qhd', weights, near_values, precision=lax.Precision.HIGHEST)
        return low(low_back(attended.reshape(TOK_DEV, HEADS * HEAD_DIM)))
    starts = jnp.arange(TOKENS // TOK_DEV, dtype=jnp.int32) * TOK_DEV
    return lax.map(jax.checkpoint(attend_block), starts).reshape(TOKENS, HEADS * HEAD_DIM)

def forward(patch_rows, pos_rows, weight_set, segments):
    ln1_gain, ln1_bias, w_qkv, b_qv, w_out, b_out, ln2_gain, ln2_bias, w_fc1, b_fc1, w_fc2, b_fc2 = weight_set
    hidden = patch_rows + pos_rows
    normed = low(layer_norm(hidden, ln1_gain, ln1_bias))
    joined = matmul(normed, w_qkv)
    queries = low(low_back(joined[:, :D] + b_qv[:D]))
    keys = low(low_back(joined[:, D:2 * D]))
    values = low(low_back(joined[:, 2 * D:] + b_qv[D:]))
    attended = attend(queries, keys, values, segments)
    branch = low_back(matmul(attended, w_out) + b_out)
    middle = hidden + branch
    normed_two = low(layer_norm(middle, ln2_gain, ln2_bias))
    inner_sum = low_back(matmul(normed_two, w_fc1) + b_fc1)
    active = low(jax.nn.gelu(inner_sum, approximate=True))
    return middle + low_back(matmul(active, w_fc2) + b_fc2)

def add_arrays(first_arr, second_arr):
    return first_arr + second_arr

def reference(patches, pos_embed, lengths, out_grad, ln1_gain, ln1_bias, w_qkv, b_qv, w_out, b_out, ln2_gain, ln2_bias, w_fc1, b_fc1, w_fc2, b_fc2):
    weight_set = tuple((weight_arg.astype(jnp.float32) for weight_arg in (ln1_gain, ln1_bias, w_qkv, b_qv, w_out, b_out, ln2_gain, ln2_bias, w_fc1, b_fc1, w_fc2, b_fc2)))
    segments = jax.vmap(segment_ids)(lengths)

    def pack_step(grad_total, pack_item):
        pack_patches, pack_pos, pack_segs, pack_cot = pack_item

        def run_block(patch_rows, weight_arg):
            return forward(patch_rows, pack_pos, weight_arg, pack_segs)
        block_out, pullback = jax.vjp(run_block, pack_patches, weight_set)
        patch_grad, weight_grads = pullback(pack_cot)
        grad_total = jax.tree.map(add_arrays, grad_total, weight_grads)
        return (grad_total, (block_out.astype(jnp.bfloat16), patch_grad))
    zero_grads = jax.tree.map(jnp.zeros_like, weight_set)
    grad_total, (block_out, patch_grad) = lax.scan(pack_step, zero_grads, (patches.astype(jnp.float32), pos_embed.astype(jnp.float32), segments, out_grad.astype(jnp.float32)))
    grad_scale = 1.0 / (BATCHES * math.sqrt(TOKENS))
    scaled = tuple((grad_sum * grad_scale for grad_sum in grad_total))
    return (block_out, patch_grad, scaled[0], scaled[1], scaled[2], scaled[3], scaled[4], scaled[5], scaled[6], scaled[7], scaled[8], scaled[9], scaled[10], scaled[11])
```

```python
import math
from functools import partial

import jax
import jax.numpy as jnp
from jax import lax
from jax.experimental import pallas as pl
from jax.experimental.pallas import tpu as pltpu
from jax.sharding import Mesh, PartitionSpec as P

HEADS = 16
LONG = 2304
NORM_EPS = 1e-06
HEAD_DIM = 64
BLOCK = 512
FAR = 1e30
QB = 512
KB = 512


def rows_dot(a, b):
    return lax.dot_general(a, b, (((1,), (0,)), ((), ())), preferred_element_type=jnp.float32)


def membership(ends_ref, count, first, width):
    place = first + lax.broadcasted_iota(jnp.int32, (16, width), 1)
    row = lax.broadcasted_iota(jnp.int32, (16, width), 0)
    low = jnp.zeros((16, width), jnp.int32)
    high = jnp.zeros((16, width), jnp.int32)
    for i in range(count):
        begin = ends_ref[i - 1] if i > 0 else 0
        low = jnp.where(row == i, begin, low)
        high = jnp.where(row == i, ends_ref[i], high)
    return jnp.where((place >= low) & (place < high), 1.0, 0.0)


def image_span(ends_ref, count, first, last):
    low = jnp.int32(0)
    high = ends_ref[count - 1]
    for i in range(count - 1):
        end = ends_ref[i]
        low = jnp.where(end <= first, end, low)
    for i in range(count - 2, -1, -1):
        end = ends_ref[i]
        high = jnp.where(end > last, end, high)
    return low, high


def split3(x):
    top = x.astype(jnp.bfloat16)
    rest = x - top.astype(jnp.float32)
    mid = rest.astype(jnp.bfloat16)
    low = (rest - mid.astype(jnp.float32)).astype(jnp.bfloat16)
    return [top.astype(jnp.float32), mid.astype(jnp.float32), low.astype(jnp.float32)]


def forward_kernel(count, shift, ends_ref, base_ref, q_ref, k_ref, v_ref, o_ref, log_ref, qa, kn, va):
    q_blocks = q_ref.shape[0]
    k_blocks = k_ref.shape[0]
    key_count = k_blocks * BLOCK
    base = base_ref[0]

    @pl.loop(0, k_blocks)
    def _(i):
        at = pl.ds(pl.multiple_of(i * BLOCK, BLOCK), BLOCK)
        away = (membership(ends_ref, count, base - shift + i * BLOCK, BLOCK) - 1.0) * FAR
        both = jnp.concatenate([k_ref[i].astype(jnp.float32), away], axis=0)
        kn[at, :] = both.T.astype(jnp.bfloat16)
        va[:, at] = jnp.concatenate(
            [v_ref[i].astype(jnp.float32), jnp.ones((16, BLOCK), jnp.float32)], axis=0
        ).astype(jnp.bfloat16)

    @pl.loop(0, q_blocks)
    def _(i):
        at = pl.ds(pl.multiple_of(i * BLOCK, BLOCK), BLOCK)
        inside = membership(ends_ref, count, base + i * BLOCK, BLOCK)
        qa[:, at] = jnp.concatenate(
            [q_ref[i].astype(jnp.float32) * (HEAD_DIM ** -0.5), inside], axis=0
        ).astype(jnp.bfloat16)

    per = BLOCK // QB

    @pl.loop(0, q_blocks * per)
    def _(i):
        q_part = qa[:, pl.ds(pl.multiple_of(i * QB, QB), QB)]
        first = base + i * QB
        low, high = image_span(ends_ref, count, first, first + QB - 1)
        low = jnp.maximum(low - base + shift, 0) // KB
        high = jnp.minimum(high - base + shift + KB - 1, key_count) // KB

        def step(j, carry):
            top, acc = carry
            at = pl.ds(pl.multiple_of(j * KB, KB), KB)
            scores = rows_dot(kn[at, :], q_part)
            new_top = jnp.maximum(top, jnp.max(scores, axis=0, keepdims=True))
            weights = jnp.exp(scores - new_top)
            acc = acc * jnp.exp(top - new_top) + rows_dot(va[:, at], weights.astype(jnp.bfloat16))
            return new_top, acc

        top, acc = lax.fori_loop(
            low,
            high,
            step,
            (jnp.full((1, QB), -3e38, jnp.float32), jnp.zeros((HEAD_DIM + 16, QB), jnp.float32)),
        )
        total = acc[HEAD_DIM : HEAD_DIM + 1]
        o_ref[i // per, :, pl.ds(pl.multiple_of((i % per) * QB, QB), QB)] = (
            acc[:HEAD_DIM] / total
        ).astype(jnp.bfloat16)
        log_ref[:, pl.ds(pl.multiple_of(i * QB, QB), QB)] = top + jnp.log(total)


def backward_kernel(
    count, shift, ends_ref, base_ref, q_ref, k_ref, v_ref, o_ref, do_ref, log_ref,
    dq_ref, dk_ref, dv_ref, qa, da, kn, vn, qn, dn, ks, sums,
):
    q_blocks = q_ref.shape[0]
    k_blocks = k_ref.shape[0]
    key_count = k_blocks * BLOCK
    base = base_ref[0]
    scale = HEAD_DIM ** -0.5
    sums[...] = jnp.zeros_like(sums)

    @pl.loop(0, k_blocks)
    def _(i):
        at = pl.ds(pl.multiple_of(i * BLOCK, BLOCK), BLOCK)
        away = (membership(ends_ref, count, base - shift + i * BLOCK, BLOCK) - 1.0) * FAR
        ones = jnp.ones((16, BLOCK), jnp.float32)
        keys = k_ref[i].astype(jnp.float32)
        kn[at, :] = jnp.concatenate([keys, away, ones], axis=0).T.astype(jnp.bfloat16)
        vn[at, :] = jnp.concatenate([v_ref[i].astype(jnp.float32), ones], axis=0).T.astype(jnp.bfloat16)
        ks[:, at] = (keys * scale).astype(jnp.bfloat16)

    @pl.loop(0, q_blocks)
    def _(i):
        at = pl.ds(pl.multiple_of(i * BLOCK, BLOCK), BLOCK)
        inside = membership(ends_ref, count, base + i * BLOCK, BLOCK)
        pad = jnp.zeros((13, BLOCK), jnp.float32)
        scaled = q_ref[i].astype(jnp.float32) * scale
        qn[at, :] = scaled.T.astype(jnp.bfloat16)
        qa[:, at] = jnp.concatenate(
            [scaled, inside] + split3(-log_ref[:, at]) + [pad], axis=0
        ).astype(jnp.bfloat16)
        grads = do_ref[i].astype(jnp.float32)
        row_dot = jnp.sum(grads * o_ref[i].astype(jnp.float32), axis=0, keepdims=True)
        dn[at, :] = grads.T.astype(jnp.bfloat16)
        da[:, at] = jnp.concatenate([grads] + split3(-row_dot) + [pad], axis=0).astype(jnp.bfloat16)

    per = BLOCK // QB

    @pl.loop(0, q_blocks * per)
    def _(i):
        q_at = pl.ds(pl.multiple_of(i * QB, QB), QB)
        q_part = qa[:, q_at]
        d_part = da[:, q_at]
        q_rows = qn[q_at, :]
        d_rows = dn[q_at, :]
        first = base + i * QB
        low, high = image_span(ends_ref, count, first, first + QB - 1)
        low = jnp.maximum(low - base + shift, 0) // KB
        high = jnp.minimum(high - base + shift + KB - 1, key_count) // KB

        def step(j, dq):
            at = pl.ds(pl.multiple_of(j * KB, KB), KB)
            probs = jnp.exp(rows_dot(kn[at, :], q_part))
            score_grad = (probs * rows_dot(vn[at, :], d_part)).astype(jnp.bfloat16)
            sums[at, 0:HEAD_DIM] += rows_dot(score_grad, q_rows)
            sums[at, HEAD_DIM : 2 * HEAD_DIM] += rows_dot(probs.astype(jnp.bfloat16), d_rows)
            return dq + rows_dot(ks[:, at], score_grad)

        dq = lax.fori_loop(low, high, step, jnp.zeros((HEAD_DIM, QB), jnp.float32))
        dq_ref[i // per, :, pl.ds(pl.multiple_of((i % per) * QB, QB), QB)] = dq.astype(jnp.bfloat16)

    @pl.loop(0, k_blocks)
    def _(i):
        at = pl.ds(pl.multiple_of(i * BLOCK, BLOCK), BLOCK)
        both = sums[at, :].T
        dk_ref[i] = both[:HEAD_DIM].astype(dk_ref.dtype)
        dv_ref[i] = both[HEAD_DIM:].astype(dv_ref.dtype)


def vmem_spec():
    return pl.BlockSpec(memory_space=pltpu.VMEM)


def smem_spec():
    return pl.BlockSpec(memory_space=pltpu.SMEM)


def attention_forward(ends, base, q, k, v, shift):
    blocks, k_blocks = q.shape[0], k.shape[0]
    tokens, keys = blocks * BLOCK, k_blocks * BLOCK
    pairs = tokens * 2048
    return pl.pallas_call(
        partial(forward_kernel, ends.shape[0], shift),
        out_shape=(
            jax.ShapeDtypeStruct((blocks, HEAD_DIM, BLOCK), jnp.bfloat16),
            jax.ShapeDtypeStruct((1, tokens), jnp.float32),
        ),
        in_specs=[smem_spec(), smem_spec(), vmem_spec(), vmem_spec(), vmem_spec()],
        out_specs=(vmem_spec(), vmem_spec()),
        scratch_shapes=[
            pltpu.VMEM((HEAD_DIM + 16, tokens), jnp.bfloat16),
            pltpu.VMEM((keys, HEAD_DIM + 16), jnp.bfloat16),
            pltpu.VMEM((HEAD_DIM + 16, keys), jnp.bfloat16),
        ],
        compiler_params=pltpu.CompilerParams(vmem_limit_bytes=56 * 1024 * 1024),
        cost_estimate=pl.CostEstimate(flops=pairs * 4 * 64, bytes_accessed=tokens * 512, transcendentals=pairs),
    )(ends, base, q, k, v)


def attention_backward(ends, base, q, k, v, o, do, log, shift, kv_dtype):
    blocks, k_blocks = q.shape[0], k.shape[0]
    tokens, keys = blocks * BLOCK, k_blocks * BLOCK
    pairs = tokens * 2048
    return pl.pallas_call(
        partial(backward_kernel, ends.shape[0], shift),
        out_shape=(
            jax.ShapeDtypeStruct((blocks, HEAD_DIM, BLOCK), jnp.bfloat16),
            jax.ShapeDtypeStruct((k_blocks, HEAD_DIM, BLOCK), kv_dtype),
            jax.ShapeDtypeStruct((k_blocks, HEAD_DIM, BLOCK), kv_dtype),
        ),
        in_specs=[smem_spec(), smem_spec()] + [vmem_spec()] * 6,
        out_specs=(vmem_spec(), vmem_spec(), vmem_spec()),
        scratch_shapes=[
            pltpu.VMEM((HEAD_DIM + 32, tokens), jnp.bfloat16),
            pltpu.VMEM((HEAD_DIM + 16, tokens), jnp.bfloat16),
            pltpu.VMEM((keys, HEAD_DIM + 32), jnp.bfloat16),
            pltpu.VMEM((keys, HEAD_DIM + 16), jnp.bfloat16),
            pltpu.VMEM((tokens, HEAD_DIM), jnp.bfloat16),
            pltpu.VMEM((tokens, HEAD_DIM), jnp.bfloat16),
            pltpu.VMEM((HEAD_DIM, keys), jnp.bfloat16),
            pltpu.VMEM((keys, 2 * HEAD_DIM), jnp.float32),
        ],
        compiler_params=pltpu.CompilerParams(vmem_limit_bytes=56 * 1024 * 1024),
        cost_estimate=pl.CostEstimate(flops=pairs * 10 * 64, bytes_accessed=tokens * 1024, transcendentals=pairs),
    )(ends, base, q, k, v, o, do, log)


SEQ = ("z", "y", "c")
SWAP = ((0, 1), (1, 0))


def norm_forward(hidden, gain_vec, offset_vec):
    centre = hidden - jnp.mean(hidden, axis=-1, keepdims=True)
    spread = jnp.mean(centre * centre, axis=-1, keepdims=True)
    inv_std = lax.rsqrt(spread + NORM_EPS)
    scaled = centre * inv_std
    return (scaled * gain_vec + offset_vec, scaled, inv_std)


def norm_backward(grad_out, scaled, inv_std, gain_vec):
    gain_grad = jnp.sum(grad_out * scaled, axis=0)
    offset_grad = jnp.sum(grad_out, axis=0)
    grad_scaled = grad_out * gain_vec
    grad_in = inv_std * (
        grad_scaled
        - jnp.mean(grad_scaled, axis=-1, keepdims=True)
        - scaled * jnp.mean(grad_scaled * scaled, axis=-1, keepdims=True)
    )
    return (gain_grad, offset_grad, grad_in)


def dot(a, b, a_dim, b_dim):
    return lax.dot_general(
        a, b, (((a_dim,), (b_dim,)), ((), ())), preferred_element_type=jnp.float32
    )


def pick(x, i, axis=0):
    return lax.dynamic_index_in_dim(x, i, axis, keepdims=False)


def swap(x, axis):
    return lax.ppermute(x, axis, SWAP)


def in_order(own, other, position):
    return jnp.where(position == 0, jnp.stack([own, other]), jnp.stack([other, own]))


def join_fsdp(shard):
    if lax.axis_size("f") != 2:
        return lax.all_gather(shard, "f", axis=0, tiled=True)
    rows = shard.shape[0] // 2
    core = lax.axis_index("c")
    part = swap(lax.dynamic_slice_in_dim(shard, core * rows, rows, 0), "f")
    other = in_order(part, swap(part, "c"), core).reshape(shard.shape)
    return in_order(shard, other, lax.axis_index("f")).reshape((-1,) + shard.shape[1:])


def join_small(shard):
    if lax.axis_size("f") != 2:
        return lax.all_gather(shard, "f", axis=0, tiled=False)
    return in_order(shard, swap(shard, "f"), lax.axis_index("f"))


def halve(x, axis):
    here = lax.axis_index(axis)
    got = swap(pick(x, 1 - here), axis)
    return pick(x, here).astype(jnp.float32) + got.astype(jnp.float32)


def scatter_sum(x, axis):
    count, here = lax.axis_size(axis), lax.axis_index(axis)
    total = pick(x, here).astype(jnp.float32)
    for step in range(1, count):
        piece = pick(x, lax.rem(here + step, count))
        got = lax.ppermute(piece, axis, [(i, (i + step) % count) for i in range(count)])
        total = total + got.astype(jnp.float32)
    return total


def spread_parts(x, axis):
    count, here = lax.axis_size(axis), lax.axis_index(axis)
    out = jnp.zeros((count,) + x.shape, x.dtype)
    out = lax.dynamic_update_index_in_dim(out, x, here, 0)
    for step in range(1, count):
        got = lax.ppermute(x, axis, [(i, (i + step) % count) for i in range(count)])
        out = lax.dynamic_update_index_in_dim(out, got, lax.rem(here - step + count, count), 0)
    return out


def reduce_weight(grad, scale):
    parts, planes = lax.axis_size("f"), lax.axis_size("z")
    rows, cols = grad.shape
    low = jnp.bfloat16
    x = grad.reshape(parts, 2, -1, cols).transpose(1, 0, 2, 3).astype(low)
    x = halve(x, "c").astype(low)
    if parts == 2:
        x = halve(x, "f").astype(low)
    else:
        x = lax.psum_scatter(x, "f", scatter_dimension=0, tiled=False)
    x = x.reshape(2, -1, cols)
    x = halve(x, "y").astype(low)
    x = x.reshape(planes, -1, cols)
    x = scatter_sum(x, "z")
    if lax.axis_size("g") > 1:
        x = lax.psum(x, "g")
    x = (x * scale).astype(low)
    x = spread_parts(x, "z").reshape(-1, cols)
    x = in_order(x, swap(x, "y"), lax.axis_index("y")).reshape(-1, cols)
    x = in_order(x, swap(x, "c"), lax.axis_index("c")).reshape(-1, cols)
    return x.astype(jnp.float32)


def body(
    patches, pos_embed, lengths, out_grad,
    ln1_gain, ln1_bias, w_qkv, b_qv, w_out, b_out,
    ln2_gain, ln2_bias, w_fc1, b_fc1, w_fc2, b_fc2,
):
    f32, low = jnp.float32, jnp.bfloat16
    rows, width = patches.shape[1:]
    groups, parts = lax.axis_size("g"), lax.axis_size("f")
    head = lax.axis_index(SEQ)
    group = lax.axis_index("g")
    shard_index = lax.axis_index("f")
    scale = 1.0 / (parts * math.sqrt(rows * HEADS * groups))

    small = (ln1_gain, ln1_bias, b_qv, b_out, ln2_gain, ln2_bias, b_fc1, b_fc2)
    packed = join_small(jnp.concatenate(small))
    vectors, at = [], 0
    for vec in small:
        size = vec.shape[0]
        vectors.append(packed[:, at : at + size].reshape(-1).astype(f32))
        at += size
    gain_one, bias_one, qv_bias, out_bias, gain_two, bias_two, fc1_bias, fc2_bias = vectors

    shard_rows = w_qkv.shape[0]
    head_cols = lax.dynamic_slice_in_dim(
        w_qkv.reshape(shard_rows, 3, HEADS, HEAD_DIM), head, 1, 2
    ).reshape(shard_rows, 3 * HEAD_DIM)
    head_full = join_small(head_cols).reshape(width, 3 * HEAD_DIM)
    head_bias = jnp.concatenate(
        [
            lax.dynamic_slice_in_dim(qv_bias, head * HEAD_DIM, HEAD_DIM),
            jnp.zeros((HEAD_DIM,), f32),
            lax.dynamic_slice_in_dim(qv_bias, width + head * HEAD_DIM, HEAD_DIM),
        ]
    )

    hidden = patches[0].astype(f32) + pos_embed[0].astype(f32)
    normed_pre, scaled_one, inv_one = norm_forward(hidden, gain_one, bias_one)
    normed = normed_pre.astype(low)
    normed_all = lax.all_gather(normed, SEQ, axis=0, tiled=True)

    qkv_full = join_fsdp(w_qkv)
    out_full = join_fsdp(w_out)
    fc1_full = join_fsdp(w_fc1)
    fc2_full = join_fsdp(w_fc2)

    qkv = lax.dot_general(
        head_full, normed_all.reshape(HEADS, rows, width), (((0,), (2,)), ((), ())),
        preferred_element_type=f32,
    )
    qkv = (qkv + head_bias[:, None, None]).astype(low).transpose(1, 0, 2)
    q, k, v = (qkv[:, i * HEAD_DIM : (i + 1) * HEAD_DIM] for i in range(3))
    ends = jnp.cumsum(lengths[0]).astype(jnp.int32)
    base = (group * (rows * HEADS)).astype(jnp.int32).reshape(1)
    shift, margin = 0, 0
    up = [(i, i + 1) for i in range(groups - 1)]
    down = [(i + 1, i) for i in range(groups - 1)]
    if groups > 1:
        margin = -(-LONG // rows)
        shift = margin * rows
        both = jnp.stack([k, v])
        before = lax.ppermute(both[:, HEADS - margin :], "g", up)
        after = lax.ppermute(both[:, :margin], "g", down)
        k, v = jnp.concatenate([before, both, after], axis=1)
    attended, log_total = attention_forward(ends, base, q, k, v, shift)
    mixed = lax.all_to_all(attended, SEQ, 0, 0, tiled=True).reshape(width, rows)

    branch = dot(mixed, out_full, 0, 0) + out_bias
    middle = hidden + branch
    normed_two_pre, scaled_two, inv_two = norm_forward(middle, gain_two, bias_two)
    normed_two = normed_two_pre.astype(low)
    inner_sum = dot(normed_two, fc1_full, 1, 0) + fc1_bias
    active, gelu_pull = jax.vjp(partial(jax.nn.gelu, approximate=True), inner_sum)
    active_low = active.astype(low)
    block_out = middle + (dot(active_low, fc2_full, 1, 0) + fc2_bias)

    out_cot = out_grad[0]
    cot_full = out_cot.astype(f32)
    active_grad = dot(out_cot, fc2_full, 1, 1)
    inner_grad = gelu_pull(active_grad)[0].astype(low)
    norm_two_grad = dot(inner_grad, fc1_full, 1, 1)
    gain_two_grad, bias_two_grad, middle_from_norm = norm_backward(
        norm_two_grad, scaled_two, inv_two, gain_two
    )
    middle_grad = cot_full + middle_from_norm
    branch_grad = middle_grad.astype(low)
    mixed_grad = dot(out_full, branch_grad, 1, 1).astype(low)
    attended_grad = lax.all_to_all(
        mixed_grad.reshape(HEADS, HEAD_DIM, rows), SEQ, 0, 0, tiled=True
    )

    fc2_grad = reduce_weight(dot(active_low, out_cot, 0, 0), scale)
    fc1_grad = reduce_weight(dot(normed_two, inner_grad, 0, 0), scale)
    out_weight_grad = reduce_weight(dot(mixed, branch_grad, 1, 0), scale)

    dq, dk, dv = attention_backward(
        ends, base, q, k, v, attended, attended_grad, log_total, shift, f32 if groups > 1 else low
    )
    if groups > 1:
        both = jnp.stack([dk, dv])
        inner = both[:, margin : margin + HEADS]
        before = lax.ppermute(both[:, :margin], "g", down)
        after = lax.ppermute(both[:, margin + HEADS :], "g", up)
        inner = inner.at[:, HEADS - margin :].add(before).at[:, :margin].add(after)
        dk, dv = inner.astype(low)
    head_grad = jnp.concatenate([dq, dk, dv], axis=1)
    token_grad = lax.all_to_all(head_grad, SEQ, 0, 0, tiled=True)

    weight_part = lax.dot_general(
        normed_all.reshape(HEADS, rows, width), head_grad, (((0, 1), (0, 2)), ((), ())),
        preferred_element_type=f32,
    ).reshape(parts, shard_rows, 3 * HEAD_DIM)
    if parts == 2:
        weight_part = halve(weight_part, "f")
    else:
        weight_part = lax.psum_scatter(weight_part, "f", scatter_dimension=0, tiled=False)
    if groups > 1:
        weight_part = lax.psum(weight_part, "g")
    weight_all = lax.all_gather((weight_part * scale).astype(low), SEQ, axis=0, tiled=False)
    qkv_weight_grad = (
        weight_all.reshape(HEADS, shard_rows, 3, HEAD_DIM)
        .transpose(1, 2, 0, 3)
        .reshape(shard_rows, 3 * width)
        .astype(f32)
    )

    token_grad = (
        token_grad.reshape(HEADS, 3, HEAD_DIM, rows).transpose(1, 0, 2, 3).reshape(3 * width, rows)
    )
    token_sums = jnp.sum(token_grad.astype(f32), axis=1)
    norm_one_grad = dot(token_grad, qkv_full, 0, 1)
    gain_one_grad, bias_one_grad, hidden_from_norm = norm_backward(
        norm_one_grad, scaled_one, inv_one, gain_one
    )
    patch_grad = middle_grad + hidden_from_norm

    vectors = (
        gain_one_grad,
        bias_one_grad,
        jnp.concatenate([token_sums[:width], token_sums[2 * width :]]),
        jnp.sum(branch_grad.astype(f32), axis=0),
        gain_two_grad,
        bias_two_grad,
        jnp.sum(inner_grad.astype(f32), axis=0),
        jnp.sum(cot_full, axis=0),
    )
    total = lax.psum(
        jnp.concatenate([vec.reshape(parts, -1) for vec in vectors], axis=1) * scale,
        ("g",) + SEQ + ("f",),
    )
    total = pick(total, shard_index)
    sums, at = [], 0
    for vec in vectors:
        size = vec.shape[0] // parts
        sums.append(total[at : at + size])
        at += size
    return (
        block_out.astype(low)[None],
        patch_grad[None],
        sums[0],
        sums[1],
        qkv_weight_grad,
        sums[2],
        out_weight_grad,
        sums[3],
        sums[4],
        sums[5],
        fc1_grad,
        sums[6],
        fc2_grad,
        sums[7],
    )


def solution(mesh):
    seq, parts = mesh.shape["seq"], mesh.shape["fsdp"]
    fine = Mesh(mesh.devices.reshape(seq // HEADS, HEADS // 4, 2, 2, parts), ("g", "z", "y", "c", "f"))
    rows = P("f", ("g",) + SEQ, None)
    vec, mat = P("f"), P("f", None)
    in_specs = (rows, rows, mat, rows, vec, vec, mat, vec, mat, vec, vec, vec, mat, vec, mat, vec)
    out_specs = (rows, rows, vec, vec, mat, vec, mat, vec, vec, vec, mat, vec, mat, vec)
    return jax.shard_map(body, mesh=fine, in_specs=in_specs, out_specs=out_specs, check_vma=False)
```

```python
import math
from functools import partial

import jax
import jax.numpy as jnp
from jax import lax
from jax.experimental import pallas as pl
from jax.experimental.pallas import tpu as pltpu
from jax.sharding import Mesh, PartitionSpec as P

HEADS = 16
LONG = 2304
NORM_EPS = 1e-06
CHUNKS = 4
HEAD_DIM = 64
BLOCK = 512
FAR = 1e30
QB = 512
KB = 512
CALM_SCORE = 60.0
FORWARD_COST = 50_000_000_000
BACKWARD_COST = 75_000_000_000


def rows_dot(a, b):
    return lax.dot_general(a, b, (((1,), (0,)), ((), ())), preferred_element_type=jnp.float32)


def membership(ends_ref, count, first, width):
    place = first + lax.broadcasted_iota(jnp.int32, (16, width), 1)
    row = lax.broadcasted_iota(jnp.int32, (16, width), 0)
    low = jnp.zeros((16, width), jnp.int32)
    high = jnp.zeros((16, width), jnp.int32)
    for i in range(count):
        begin = ends_ref[i - 1] if i > 0 else 0
        low = jnp.where(row == i, begin, low)
        high = jnp.where(row == i, ends_ref[i], high)
    return jnp.where((place >= low) & (place < high), 1.0, 0.0)


def image_span(ends_ref, count, first, last):
    low = jnp.int32(0)
    high = ends_ref[count - 1]
    for i in range(count - 1):
        end = ends_ref[i]
        low = jnp.where(end <= first, end, low)
    for i in range(count - 2, -1, -1):
        end = ends_ref[i]
        high = jnp.where(end > last, end, high)
    return low, high


def split3(x):
    top = x.astype(jnp.bfloat16)
    rest = x - top.astype(jnp.float32)
    mid = rest.astype(jnp.bfloat16)
    low = (rest - mid.astype(jnp.float32)).astype(jnp.bfloat16)
    return [top.astype(jnp.float32), mid.astype(jnp.float32), low.astype(jnp.float32)]


def parts_of(ref):
    return [ref.at[:, i * HEAD_DIM : (i + 1) * HEAD_DIM, :] for i in range(ref.shape[1] // HEAD_DIM)]


def forward_kernel(count, shift, ends_ref, base_ref, own_ref, *refs):
    q_ref, k_ref, v_ref = parts_of(own_ref)
    if shift:
        k_ref, v_ref = parts_of(refs[0])
        refs = refs[1:]
    o_ref, log_ref, qa, kn, va, peak = refs
    peak[...] = jnp.zeros_like(peak)
    q_blocks = q_ref.shape[0]
    k_blocks = k_ref.shape[0]
    key_count = k_blocks * BLOCK
    base = base_ref[0]

    @pl.loop(0, k_blocks)
    def _(i):
        at = pl.ds(pl.multiple_of(i * BLOCK, BLOCK), BLOCK)
        away = (membership(ends_ref, count, base - shift + i * BLOCK, BLOCK) - 1.0) * FAR
        keys = k_ref[i].astype(jnp.float32)
        peak[1:2] = jnp.maximum(peak[1:2], jnp.sum(keys * keys, axis=0, keepdims=True))
        both = jnp.concatenate([keys, away], axis=0)
        kn[at, :] = both.T.astype(jnp.bfloat16)
        va[:, at] = jnp.concatenate(
            [v_ref[i].astype(jnp.float32), jnp.ones((16, BLOCK), jnp.float32)], axis=0
        ).astype(jnp.bfloat16)

    @pl.loop(0, q_blocks)
    def _(i):
        at = pl.ds(pl.multiple_of(i * BLOCK, BLOCK), BLOCK)
        inside = membership(ends_ref, count, base + i * BLOCK, BLOCK)
        asked = q_ref[i].astype(jnp.float32)
        peak[0:1] = jnp.maximum(peak[0:1], jnp.sum(asked * asked, axis=0, keepdims=True))
        qa[:, at] = jnp.concatenate(
            [asked * (HEAD_DIM ** -0.5), inside], axis=0
        ).astype(jnp.bfloat16)

    per = BLOCK // QB
    calm = CALM_SCORE * HEAD_DIM ** 0.5
    peaks = [jnp.max(peak[i : i + 1]) for i in range(2)]

    def span(i):
        first = base + i * QB
        low, high = image_span(ends_ref, count, first, first + QB - 1)
        low = jnp.maximum(low - base + shift, 0) // KB
        return low, jnp.minimum(high - base + shift + KB - 1, key_count) // KB

    def finish(i, top, acc):
        total = acc[HEAD_DIM : HEAD_DIM + 1]
        o_ref[i // per, :, pl.ds(pl.multiple_of((i % per) * QB, QB), QB)] = (
            acc[:HEAD_DIM] / total
        ).astype(jnp.bfloat16)
        log_ref[:, pl.ds(pl.multiple_of(i * QB, QB), QB)] = top + jnp.log(total)

    small = peaks[0] * peaks[1] <= calm * calm

    @pl.when(small)
    def _():
        @pl.loop(0, q_blocks * per)
        def _(i):
            q_part = qa[:, pl.ds(pl.multiple_of(i * QB, QB), QB)]

            def step(j, acc):
                at = pl.ds(pl.multiple_of(j * KB, KB), KB)
                weights = jnp.exp(rows_dot(kn[at, :], q_part)).astype(jnp.bfloat16)
                return acc + rows_dot(va[:, at], weights)

            acc = lax.fori_loop(*span(i), step, jnp.zeros((HEAD_DIM + 16, QB), jnp.float32))
            finish(i, 0.0, acc)

    @pl.when(jnp.logical_not(small))
    def _():
        @pl.loop(0, q_blocks * per)
        def _(i):
            q_part = qa[:, pl.ds(pl.multiple_of(i * QB, QB), QB)]

            def step(j, carry):
                top, acc = carry
                at = pl.ds(pl.multiple_of(j * KB, KB), KB)
                scores = rows_dot(kn[at, :], q_part)
                new_top = jnp.maximum(top, jnp.max(scores, axis=0, keepdims=True))
                weights = jnp.exp(scores - new_top).astype(jnp.bfloat16)
                acc = acc * jnp.exp(top - new_top) + rows_dot(va[:, at], weights)
                return new_top, acc

            start = (
                jnp.full((1, QB), -3e38, jnp.float32),
                jnp.zeros((HEAD_DIM + 16, QB), jnp.float32),
            )
            finish(i, *lax.fori_loop(*span(i), step, start))


def backward_kernel(count, shift, first_block, chunk, last, ends_ref, base_ref, own_ref, *refs):
    q_ref, k_ref, v_ref = parts_of(own_ref)
    if shift:
        k_ref, v_ref = parts_of(refs[0])
        refs = refs[1:]
    o_ref, do_ref, log_ref, *refs = refs
    if first_block > 0:
        sums_in, _, *refs = refs
    grad_ref, *refs = refs
    sums_out = None
    if shift:
        window_ref, *refs = refs
    if not last:
        sums_out, *refs = refs
    qa, da, kn, vn, qn, dn, ks, sums, dq_part, sums_sem, dq_sem, *refs = refs
    k_blocks = k_ref.shape[0]
    key_count = k_blocks * BLOCK
    base = base_ref[0]
    scale = HEAD_DIM ** -0.5
    start = base + first_block * BLOCK
    low, high = image_span(ends_ref, count, start, start + chunk * BLOCK - 1)
    low = jnp.maximum(low - base + shift, 0) // BLOCK
    high = jnp.minimum(high - base + shift + BLOCK - 1, key_count) // BLOCK
    held_low, held_high = (0, k_blocks) if last or first_block == 0 else (low, high)

    def block_at(i):
        return pl.ds(pl.multiple_of(i * BLOCK, BLOCK), BLOCK)

    if first_block > 0:

        @pl.loop(held_low, held_high)
        def _(i):
            pltpu.make_async_copy(sums_in.at[block_at(i)], sums.at[block_at(i)], sums_sem.at[i]).start()

    else:
        sums[...] = jnp.zeros_like(sums)

    @pl.loop(low, high)
    def _(i):
        at = block_at(i)
        away = (membership(ends_ref, count, base - shift + i * BLOCK, BLOCK) - 1.0) * FAR
        ones = jnp.ones((16, BLOCK), jnp.float32)
        keys = k_ref[i].astype(jnp.float32)
        kn[at, :] = jnp.concatenate([keys, away, ones], axis=0).T.astype(jnp.bfloat16)
        vn[at, :] = jnp.concatenate([v_ref[i].astype(jnp.float32), ones], axis=0).T.astype(jnp.bfloat16)
        ks[:, at] = (keys * scale).astype(jnp.bfloat16)

    @pl.loop(0, chunk)
    def _(i):
        at = block_at(i)
        block = first_block + i
        inside = membership(ends_ref, count, base + block * BLOCK, BLOCK)
        pad = jnp.zeros((13, BLOCK), jnp.float32)
        scaled = q_ref[block].astype(jnp.float32) * scale
        qn[at, :] = scaled.T.astype(jnp.bfloat16)
        qa[:, at] = jnp.concatenate(
            [scaled, inside] + split3(-log_ref[:, block_at(block)]) + [pad], axis=0
        ).astype(jnp.bfloat16)
        grads = do_ref[block].astype(jnp.float32)
        row_dot = jnp.sum(grads * o_ref[block].astype(jnp.float32), axis=0, keepdims=True)
        dn[at, :] = grads.T.astype(jnp.bfloat16)
        da[:, at] = jnp.concatenate([grads] + split3(-row_dot) + [pad], axis=0).astype(jnp.bfloat16)

    if first_block > 0:

        @pl.loop(held_low, held_high)
        def _(i):
            pltpu.make_async_copy(sums_in.at[block_at(i)], sums.at[block_at(i)], sums_sem.at[i]).wait()

    @pl.loop(0, chunk)
    def _(i):
        q_at = block_at(i)
        q_part = qa[:, q_at]
        d_part = da[:, q_at]
        q_rows = qn[q_at, :]
        d_rows = dn[q_at, :]
        first = start + i * BLOCK
        key_low, key_high = image_span(ends_ref, count, first, first + BLOCK - 1)
        key_low = jnp.maximum(key_low - base + shift, 0) // BLOCK
        key_high = jnp.minimum(key_high - base + shift + BLOCK - 1, key_count) // BLOCK

        def step(j, dq):
            at = block_at(j)
            probs = jnp.exp(rows_dot(kn[at, :], q_part))
            score_grad = (probs * rows_dot(vn[at, :], d_part)).astype(jnp.bfloat16)
            sums[at, 0:HEAD_DIM] += rows_dot(score_grad, q_rows)
            sums[at, HEAD_DIM : 2 * HEAD_DIM] += rows_dot(probs.astype(jnp.bfloat16), d_rows)
            return dq + rows_dot(ks[:, at], score_grad)

        dq = lax.fori_loop(key_low, key_high, step, jnp.zeros((HEAD_DIM, BLOCK), jnp.float32))
        dq_part[i] = dq.astype(jnp.bfloat16)

    def query_copy(i):
        return pltpu.make_async_copy(
            dq_part.at[i], grad_ref.at[first_block + i, 0:HEAD_DIM], dq_sem.at[i]
        )

    for i in range(chunk):
        query_copy(i).start()
    if not last:

        @pl.loop(held_low, held_high)
        def _(i):
            pltpu.make_async_copy(sums.at[block_at(i)], sums_out.at[block_at(i)], sums_sem.at[i]).start()

        @pl.loop(held_low, held_high)
        def _(i):
            pltpu.make_async_copy(sums.at[block_at(i)], sums_out.at[block_at(i)], sums_sem.at[i]).wait()

    elif shift:

        @pl.loop(0, k_blocks)
        def _(i):
            window_ref[i] = sums[block_at(i), :].T

    else:
        kv_part, kv_sem = refs

        def key_copy(i):
            return pltpu.make_async_copy(
                kv_part.at[i], grad_ref.at[i, HEAD_DIM : 3 * HEAD_DIM], kv_sem.at[i]
            )

        @pl.loop(0, k_blocks)
        def _(i):
            kv_part[i] = sums[block_at(i), :].T.astype(jnp.bfloat16)
            key_copy(i).start()

        @pl.loop(0, k_blocks)
        def _(i):
            key_copy(i).wait()

    for i in range(chunk):
        query_copy(i).wait()


def vmem_spec():
    return pl.BlockSpec(memory_space=pltpu.VMEM)


def smem_spec():
    return pl.BlockSpec(memory_space=pltpu.SMEM)


def attention_forward(ends, base, own, window, shift):
    blocks = own.shape[0]
    tokens, keys = blocks * BLOCK, blocks * BLOCK + 2 * shift
    arrays = [own] + ([window] if shift else [])
    return pl.pallas_call(
        partial(forward_kernel, ends.shape[0], shift),
        out_shape=(
            jax.ShapeDtypeStruct((blocks, HEAD_DIM, BLOCK), jnp.bfloat16),
            jax.ShapeDtypeStruct((1, tokens), jnp.float32),
        ),
        in_specs=[smem_spec(), smem_spec()] + [vmem_spec()] * len(arrays),
        out_specs=(vmem_spec(), vmem_spec()),
        scratch_shapes=[
            pltpu.VMEM((HEAD_DIM + 16, tokens), jnp.bfloat16),
            pltpu.VMEM((keys, HEAD_DIM + 16), jnp.bfloat16),
            pltpu.VMEM((HEAD_DIM + 16, keys), jnp.bfloat16),
            pltpu.VMEM((8, BLOCK), jnp.float32),
        ],
        compiler_params=pltpu.CompilerParams(vmem_limit_bytes=48 * 1024 * 1024),
        cost_estimate=pl.CostEstimate(
            flops=FORWARD_COST, bytes_accessed=tokens * 512, transcendentals=0
        ),
    )(ends, base, *arrays)


def attention_backward(ends, base, own, window, o, do, log, shift, first_block, chunk, carried):
    blocks = own.shape[0]
    tokens, keys = chunk * BLOCK, blocks * BLOCK + 2 * shift
    last = first_block + chunk == blocks
    low, f32 = jnp.bfloat16, jnp.float32
    arrays = [own] + ([window] if shift else []) + [o, do, log]
    in_specs = [smem_spec(), smem_spec()] + [vmem_spec()] * len(arrays)
    out_shape = [jax.ShapeDtypeStruct((blocks, HEAD_DIM if shift else 3 * HEAD_DIM, BLOCK), low)]
    out_specs = [any_spec()]
    aliases = {}
    if carried is not None:
        place_at = 2 + len(arrays)
        arrays += list(carried)
        in_specs += [any_spec(), any_spec()]
        aliases = {place_at + 1: 0}
        if not last:
            aliases[place_at] = 1
    if shift:
        out_shape.append(jax.ShapeDtypeStruct((keys // BLOCK, 2 * HEAD_DIM, BLOCK), f32))
        out_specs.append(vmem_spec())
    if not last:
        out_shape.append(jax.ShapeDtypeStruct((keys, 2 * HEAD_DIM), f32))
        out_specs.append(any_spec())
    scratch = [
        pltpu.VMEM((HEAD_DIM + 32, tokens), low),
        pltpu.VMEM((HEAD_DIM + 16, tokens), low),
        pltpu.VMEM((keys, HEAD_DIM + 32), low),
        pltpu.VMEM((keys, HEAD_DIM + 16), low),
        pltpu.VMEM((tokens, HEAD_DIM), low),
        pltpu.VMEM((tokens, HEAD_DIM), low),
        pltpu.VMEM((HEAD_DIM, keys), low),
        pltpu.VMEM((keys, 2 * HEAD_DIM), f32),
        pltpu.VMEM((chunk, HEAD_DIM, BLOCK), low),
        pltpu.SemaphoreType.DMA((keys // BLOCK,)),
        pltpu.SemaphoreType.DMA((chunk,)),
    ]
    if last and not shift:
        scratch += [
            pltpu.VMEM((blocks, 2 * HEAD_DIM, BLOCK), low),
            pltpu.SemaphoreType.DMA((blocks,)),
        ]
    return pl.pallas_call(
        partial(backward_kernel, ends.shape[0], shift, first_block, chunk, last),
        out_shape=out_shape,
        in_specs=in_specs,
        out_specs=out_specs,
        scratch_shapes=scratch,
        input_output_aliases=aliases,
        compiler_params=pltpu.CompilerParams(vmem_limit_bytes=50 * 1024 * 1024),
        cost_estimate=pl.CostEstimate(
            flops=BACKWARD_COST * chunk // blocks, bytes_accessed=tokens * 1024, transcendentals=0
        ),
    )(ends, base, *arrays)


def any_spec():
    return pl.BlockSpec(memory_space=pl.ANY)


def block_rows(rows, cols):
    while rows * cols > 512 * 1024 and rows % 16 == 0:
        rows //= 2
    return rows


def take_kernel(at_ref, in_ref, out_ref):
    out_ref[...] = in_ref[...]


def take(x, index, count):
    rows, cols = x.shape[0] // count, x.shape[1]
    size = block_rows(rows, cols)
    steps = rows // size
    return pl.pallas_call(
        take_kernel,
        out_shape=jax.ShapeDtypeStruct((rows, cols), x.dtype),
        grid_spec=pltpu.PrefetchScalarGridSpec(
            num_scalar_prefetch=1,
            grid=(steps,),
            in_specs=[pl.BlockSpec((size, cols), lambda j, at_ref: (at_ref[0] * steps + j, 0))],
            out_specs=pl.BlockSpec((size, cols), lambda j, at_ref: (j, 0)),
        ),
        cost_estimate=pl.CostEstimate(
            flops=0, bytes_accessed=2 * rows * cols * x.dtype.itemsize, transcendentals=0
        ),
    )(index.astype(jnp.int32).reshape(1), x)


def place_kernel(owner, row_ref, col_ref, *refs):
    out_ref = refs[-1]
    for i, piece in enumerate(owner):

        @pl.when(pl.program_id(0) == i)
        def _(piece=piece):
            out_ref[...] = refs[piece][...].astype(out_ref.dtype)


def place(pieces, row_at, col_at, dtype, rows, shape):
    cols = pieces[0].shape[1]
    owner = [n for n, piece in enumerate(pieces) for _ in range(piece.shape[0] // rows)]
    count = len(owner)
    size = block_rows(rows, cols)
    steps = rows // size

    def piece_map(piece):
        turns = [i for i in range(count) if owner[i] == piece]
        first, last = turns[0], turns[-1]

        def index(s, j, row_ref, col_ref):
            inside = j + (s - first) * steps
            end = (last - first + 1) * steps - 1
            return (jnp.where(s < first, 0, jnp.where(s > last, end, inside)), 0)

        return index

    return pl.pallas_call(
        partial(place_kernel, owner),
        out_shape=jax.ShapeDtypeStruct(shape, dtype),
        grid_spec=pltpu.PrefetchScalarGridSpec(
            num_scalar_prefetch=2,
            grid=(count, steps),
            in_specs=[pl.BlockSpec((size, cols), piece_map(i)) for i in range(len(pieces))],
            out_specs=pl.BlockSpec(
                (size, cols), lambda s, j, row_ref, col_ref: (row_ref[s] * steps + j, col_ref[s])
            ),
        ),
        cost_estimate=pl.CostEstimate(
            flops=0,
            bytes_accessed=count * rows * cols * (2 + jnp.dtype(dtype).itemsize),
            transcendentals=0,
        ),
    )(row_at, col_at, *pieces)


def project_kernel(count, place_ref, w_ref, bias_ref, *refs):
    blocks, out_ref, made, sem = refs[:count], refs[-3], refs[-2], refs[-1]

    def copy(i):
        return pltpu.make_async_copy(made.at[i], out_ref.at[place_ref[i]], sem.at[i])

    for i in range(count):
        part = lax.dot_general(
            w_ref[...], blocks[i][...], (((1,), (1,)), ((), ())), preferred_element_type=jnp.float32
        )
        made[i] = (part + bias_ref[...]).astype(jnp.bfloat16)
        copy(i).start()
    for i in range(count):
        copy(i).wait()


def project(so_far, places, w, bias, blocks):
    count = len(blocks)
    rows, width = blocks[0].shape
    cols = w.shape[0]
    arrays = [w, bias, *blocks] + ([] if so_far is None else [so_far])
    specs = [vmem_spec()] * (2 + count) + ([] if so_far is None else [any_spec()])
    return pl.pallas_call(
        partial(project_kernel, count),
        out_shape=jax.ShapeDtypeStruct((HEADS, cols, rows), jnp.bfloat16),
        in_specs=[smem_spec()] + specs,
        out_specs=any_spec(),
        scratch_shapes=[
            pltpu.VMEM((count, cols, rows), jnp.bfloat16),
            pltpu.SemaphoreType.DMA((count,)),
        ],
        input_output_aliases={} if so_far is None else {3 + count: 0},
        compiler_params=pltpu.CompilerParams(vmem_limit_bytes=24 * 1024 * 1024),
        cost_estimate=pl.CostEstimate(
            flops=4 * count * rows * width * cols, bytes_accessed=count * rows * width * 2, transcendentals=0
        ),
    )(jnp.stack(places).astype(jnp.int32), *arrays)


SLOTS = 4


def head_weight_kernel(count, place_ref, grad_ref, *refs):
    blocks, (out_ref, held, sem) = refs[:count], refs[count:]

    def copy(b):
        return pltpu.make_async_copy(blocks[b], held.at[b % SLOTS], sem.at[b % SLOTS])

    for b in range(SLOTS - 1):
        copy(b).start()
    out_ref[...] = jnp.zeros_like(out_ref)

    @pl.loop(0, count)
    def _(i):
        slot = lax.rem(i, SLOTS)
        pltpu.make_async_copy(blocks[0], held.at[slot], sem.at[slot]).wait()
        for b in range(SLOTS - 1, count):

            @pl.when(i + SLOTS - 1 == b)
            def _(b=b):
                copy(b).start()

        out_ref[...] += rows_dot(grad_ref[place_ref[i]], held[slot])


def head_weight(places, grad, blocks):
    count = len(blocks)
    rows, width = blocks[0].shape
    cols = grad.shape[1]
    return pl.pallas_call(
        partial(head_weight_kernel, count),
        out_shape=jax.ShapeDtypeStruct((cols, width), jnp.float32),
        in_specs=[smem_spec(), vmem_spec()] + [any_spec()] * count,
        out_specs=vmem_spec(),
        scratch_shapes=[
            pltpu.VMEM((SLOTS, rows, width), jnp.bfloat16),
            pltpu.SemaphoreType.DMA((SLOTS,)),
        ],
        compiler_params=pltpu.CompilerParams(vmem_limit_bytes=24 * 1024 * 1024),
        cost_estimate=pl.CostEstimate(
            flops=4 * count * rows * width * cols, bytes_accessed=count * rows * width * 2, transcendentals=0
        ),
    )(jnp.stack(places).astype(jnp.int32), grad, *blocks)


def place_of_head(head):
    return (head % 2) * (HEADS // 2) + (head // 2 % 2) * (HEADS // 4) + head // 4


def weave_kernel(heads_ref, out_ref):
    heads = heads_ref.shape[0]
    for part in range(3):
        for pair in range(heads // 2):
            rows = slice(part * HEAD_DIM, (part + 1) * HEAD_DIM)
            both = [heads_ref[place_of_head(2 * pair + i), rows] for i in range(2)]
            both = jnp.concatenate(both, axis=0)
            at = (part * heads + 2 * pair) * HEAD_DIM
            out_ref[:, at : at + 2 * HEAD_DIM] = both.astype(jnp.float32).T


def weave(heads):
    count, cols, rows = heads.shape
    size = 128
    return pl.pallas_call(
        weave_kernel,
        out_shape=jax.ShapeDtypeStruct((rows, count * cols), jnp.float32),
        grid=(rows // size,),
        in_specs=[pl.BlockSpec((count, cols, size), lambda i: (0, 0, i))],
        out_specs=pl.BlockSpec((size, count * cols), lambda i: (i, 0)),
        cost_estimate=pl.CostEstimate(
            flops=0, bytes_accessed=6 * count * cols * rows, transcendentals=0
        ),
    )(heads)


SEQ = ("z", "y", "c")
SWAP = ((0, 1), (1, 0))


def norm_forward(hidden, gain_vec, offset_vec):
    centre = hidden - jnp.mean(hidden, axis=-1, keepdims=True)
    spread = jnp.mean(centre * centre, axis=-1, keepdims=True)
    inv_std = lax.rsqrt(spread + NORM_EPS)
    scaled = centre * inv_std
    return (scaled * gain_vec + offset_vec, scaled, inv_std)


def norm_backward(grad_out, scaled, inv_std, gain_vec):
    gain_grad = jnp.sum(grad_out * scaled, axis=0)
    offset_grad = jnp.sum(grad_out, axis=0)
    grad_scaled = grad_out * gain_vec
    grad_in = inv_std * (
        grad_scaled
        - jnp.mean(grad_scaled, axis=-1, keepdims=True)
        - scaled * jnp.mean(grad_scaled * scaled, axis=-1, keepdims=True)
    )
    return (gain_grad, offset_grad, grad_in)


def dot(a, b, a_dim, b_dim):
    return lax.dot_general(
        a, b, (((a_dim,), (b_dim,)), ((), ())), preferred_element_type=jnp.float32
    )


def tie(x, *others):
    others = [other for other in others if other is not None]
    return lax.optimization_barrier((x, *others))[0] if others else x


def linear(start, first, a, second, b):
    start, first, second = (jnp.array(x, jnp.int32) for x in (start, first, second))
    return start + first * a + second * b


def pick(x, i, axis=0):
    return lax.dynamic_index_in_dim(x, i, axis, keepdims=False)


def swap(x, axis):
    return lax.ppermute(x, axis, SWAP)


def in_order(own, other, position):
    return jnp.where(position == 0, jnp.stack([own, other]), jnp.stack([other, own]))


def fetch_fsdp(shard, pieces, *others):
    if lax.axis_size("f") != 2:
        return [lax.all_gather(shard, "f", axis=0, tiled=True)]
    rows = shard.shape[0] // (2 * pieces)
    first = lax.axis_index("c") * pieces
    shard = tie(shard, *others)
    return [swap(take(shard, first + i, 2 * pieces), "f") for i in range(pieces)]


def share_cores(fetched, *others):
    if lax.axis_size("f") != 2:
        return fetched
    return fetched + [swap(tie(piece, *others), "c") for piece in fetched]


def join_fsdp(shard, pieces, *others):
    if lax.axis_size("f") != 2:
        return pieces[0]
    core, here = lax.axis_index("c"), lax.axis_index("f")
    count = len(pieces) // 2
    step = range(count)
    at = linear(
        (*range(2 * count), *(2 * count + i for i in step), *(3 * count + i for i in step)),
        (2 * count,) * (2 * count) + (-2 * count,) * (2 * count),
        here,
        (0,) * (2 * count) + (count,) * count + (-count,) * count,
        core,
    )
    rows, cols = shard.shape
    return place(
        [tie(shard, *others), *pieces], at, jnp.zeros_like(at), shard.dtype, rows // (2 * count), (2 * rows, cols)
    )


def join_small(shard):
    if lax.axis_size("f") != 2:
        return lax.all_gather(shard, "f", axis=0, tiled=False)
    return in_order(shard, swap(shard, "f"), lax.axis_index("f"))


def halve(x, axis, pairs=SWAP, here=None):
    here = lax.axis_index(axis) if here is None else here
    got = lax.ppermute(pick(x, 1 - here), axis, pairs)
    return pick(x, here).astype(jnp.float32) + got.astype(jnp.float32)


def plane_pairs(bit):
    return [(i, i ^ bit) for i in range(4)]


class WeightSum:
    def __init__(self, left, right, scale, left_dim=0):
        self.left, self.right, self.scale, self.left_dim = left, right, scale, left_dim
        self.size = left.shape[1 - left_dim] // lax.axis_size("f")
        self.cols = right.shape[1] // 2

    def term(self, c, f):
        left = lax.dynamic_slice_in_dim(self.left, f * self.size, self.size, 1 - self.left_dim)
        right = lax.dynamic_slice_in_dim(self.right, c * self.cols, self.cols, 1)
        return dot(left, right, self.left_dim, 0)

    def other_core(self, *others):
        low = jnp.bfloat16
        self.right = tie(self.right, *others)
        core = lax.axis_index("c")
        parts, here = lax.axis_size("f"), lax.axis_index("f")
        order = [1 - here, here] if parts == 2 else range(parts)
        sent = [self.term(1 - core, f).astype(low) for f in order]
        self.got = [swap(part, "c") for part in sent]
        return sent[-1]

    def other_f(self, *others):
        low, f32 = jnp.bfloat16, jnp.float32
        self.right = tie(self.right, *others)
        core, parts, here = lax.axis_index("c"), lax.axis_size("f"), lax.axis_index("f")
        if parts == 2:
            sent = (self.term(core, 1 - here) + self.got[0].astype(f32)).astype(low)
            self.far = swap(sent, "f")
            return sent
        total = [(self.term(core, f) + self.got[f].astype(f32)).astype(low) for f in range(parts)]
        self.total = lax.psum_scatter(jnp.stack(total), "f", scatter_dimension=0, tiled=False)
        return self.total

    def half(self, x, axis, pairs, here):
        x = x.reshape(2, -1, self.cols)
        sent = pick(x, 1 - here)
        self.kept, self.coming = pick(x, here), lax.ppermute(sent, axis, pairs)
        return sent

    def near_y(self, *others):
        low, f32 = jnp.bfloat16, jnp.float32
        core, parts, here = lax.axis_index("c"), lax.axis_size("f"), lax.axis_index("f")
        if parts == 2:
            self.right = tie(self.right, *others)
            x = self.term(core, here) + self.got[1].astype(f32) + self.far.astype(f32)
        else:
            x = self.total
        return self.half(x.astype(low), "y", SWAP, lax.axis_index("y"))

    def added(self, *others):
        coming = tie(self.coming, *others)
        return self.kept.astype(jnp.float32) + coming.astype(jnp.float32)

    def near_z(self, *others):
        x = self.added(*others).astype(jnp.bfloat16)
        return self.half(x, "z", plane_pairs(1), lax.rem(lax.axis_index("z"), 2))

    def far_z(self, *others):
        x = self.added(*others).astype(jnp.bfloat16)
        return self.half(x, "z", plane_pairs(2), lax.axis_index("z") // 2)

    def back_far_z(self, *others):
        x = self.added(*others)
        if lax.axis_size("g") > 1:
            x = lax.psum(x, "g")
        self.x = (x * self.scale).astype(jnp.bfloat16)
        self.coming = lax.ppermute(self.x, "z", plane_pairs(2))
        return self.x

    def back_near_z(self, *others):
        coming = tie(self.coming, *others)
        self.x = in_order(self.x, coming, lax.axis_index("z") // 2).reshape(-1, self.cols)
        self.coming = lax.ppermute(self.x, "z", plane_pairs(1))
        return self.x

    def back_y(self, *others):
        coming = tie(self.coming, *others)
        x = in_order(self.x, coming, lax.rem(lax.axis_index("z"), 2)).reshape(-1, self.cols)
        near = swap(x, "y")
        self.pieces = [x, near, swap(x, "c"), swap(near, "c")]
        return x

    def result(self, *others):
        y, c = lax.axis_index("y"), lax.axis_index("c")
        pieces = [tie(self.pieces[0], *others)] + self.pieces[1:]
        row_at = linear((0, 1, 0, 1), (1, -1, 1, -1), y, (0, 0, 0, 0), c)
        col_at = linear((0, 0, 1, 1), (0, 0, 0, 0), y, (1, 1, -1, -1), c)
        rows, cols = pieces[0].shape
        return place(pieces, row_at, col_at, jnp.float32, rows, (2 * rows, 2 * cols))


class VectorSum:
    def __init__(self, vectors, scale):
        self.sizes = [vec.shape[0] // lax.axis_size("f") for vec in vectors]
        self.x = jnp.concatenate([vec.reshape(lax.axis_size("f"), -1) for vec in vectors], axis=1) * scale

    def core(self, *others):
        self.x = tie(self.x, *others)
        self.coming = swap(self.x, "c")
        return self.x

    def other_f(self, *others):
        x = self.x + tie(self.coming, *others)
        if lax.axis_size("f") == 2:
            here = lax.axis_index("f")
            self.x, sent = pick(x, here), pick(x, 1 - here)
            self.coming = swap(sent, "f")
            return sent
        self.x = lax.psum_scatter(x, "f", scatter_dimension=0, tiled=False)
        self.coming = jnp.zeros_like(self.x)
        return self.x

    def hop(self, axis, pairs, others):
        self.x = self.x + tie(self.coming, *others)
        self.coming = lax.ppermute(self.x, axis, pairs)
        return self.x

    def near_y(self, *others):
        return self.hop("y", SWAP, others)

    def near_z(self, *others):
        return self.hop("z", plane_pairs(1), others)

    def far_z(self, *others):
        return self.hop("z", plane_pairs(2), others)

    def result(self, *others):
        self.total = self.x + tie(self.coming, *others)
        if lax.axis_size("g") > 1:
            self.total = lax.psum(self.total, "g")
        return self.total

    def vectors(self):
        at = 0
        for size in self.sizes:
            yield self.total[at : at + size]
            at += size


def arrivals(count):
    table = []
    for z in range(count):
        hops = []
        for t in range(1, count):
            if z - t >= 0:
                hops.append(("up", t))
            if z + t < count:
                hops.append(("down", t))
        table.append(hops)
    return table


def gather_group(x, use, beside):
    z, y, c = (lax.axis_index(axis) for axis in SEQ)
    count = lax.axis_size("z")
    table = arrivals(count)
    up, down = x, x
    hops = {}
    block, plane = x, z
    state, crossing = None, []
    for t in range(1, count + 1):
        first = plane * 4
        if t < count:
            up = lax.ppermute(up, "z", [(i, i + 1) for i in range(t - 1, count - 1)])
            down = lax.ppermute(down, "z", [(i, i - 1) for i in range(1, count - t + 1)])
        near = swap(block, "y")
        across = swap(block, "c")
        up, down, near, across, crossing, state, _ = lax.optimization_barrier(
            (up, down, near, across, crossing, state, beside[t - 1] if t <= len(beside) else [])
        )
        items = [(block, first + 2 * y + c), (across, first + 2 * y + 1 - c)]
        items += [(near, first + 2 * (1 - y) + c), *crossing]
        state = use(state, [item[0] for item in items], [item[1] for item in items])
        crossing = [(swap(near, "c"), first + 2 * (1 - y) + 1 - c)]
        if t < count:
            hops["up", t], hops["down", t] = up, down
            names = sorted({table[i][t - 1] for i in range(count)})
            block, plane = None, z
            for name in names:
                here = [i for i in range(count) if table[i][t - 1] == name]
                chosen = (z >= here[0]) & (z <= here[-1])
                block = hops[name] if block is None else jnp.where(chosen, hops[name], block)
                plane = jnp.where(chosen, z + (-name[1] if name[0] == "up" else name[1]), plane)
    return use(state, [item[0] for item in crossing], [item[1] for item in crossing])


def body(
    patches, pos_embed, lengths, out_grad,
    ln1_gain, ln1_bias, w_qkv, b_qv, w_out, b_out,
    ln2_gain, ln2_bias, w_fc1, b_fc1, w_fc2, b_fc2,
):
    f32, low = jnp.float32, jnp.bfloat16
    rows, width = patches.shape[1:]
    groups, parts = lax.axis_size("g"), lax.axis_size("f")
    head = lax.axis_index(SEQ)
    group = lax.axis_index("g")
    shard_index = lax.axis_index("f")
    scale = 1.0 / (parts * math.sqrt(rows * HEADS * groups))

    gain_one, bias_one, qv_bias = (
        join_small(vec).reshape(-1).astype(f32) for vec in (ln1_gain, ln1_bias, b_qv)
    )
    hidden = patches[0].astype(f32) + pos_embed[0].astype(f32)
    normed_pre, scaled_one, inv_one = norm_forward(hidden, gain_one, bias_one)
    normed = normed_pre.astype(low)

    shard_rows = w_qkv.shape[0]
    head_cols = lax.dynamic_slice_in_dim(
        w_qkv.reshape(shard_rows, 3, HEADS, HEAD_DIM), head, 1, 2
    ).reshape(shard_rows, 3 * HEAD_DIM)
    head_full = join_small(head_cols).reshape(width, 3 * HEAD_DIM).T
    head_bias = jnp.concatenate(
        [
            lax.dynamic_slice_in_dim(qv_bias, head * HEAD_DIM, HEAD_DIM),
            jnp.zeros((HEAD_DIM,), f32),
            lax.dynamic_slice_in_dim(qv_bias, width + head * HEAD_DIM, HEAD_DIM),
        ]
    )[:, None]

    kept_blocks, kept_places = [], []

    def add_blocks(qkv, blocks, places):
        kept_blocks.extend(blocks)
        kept_places.extend(places)
        return project(qkv, places, head_full, head_bias, blocks)

    out_part = fetch_fsdp(w_out, 1, normed)
    fc1_part = fetch_fsdp(w_fc1, 2, normed)
    fc2_part = fetch_fsdp(w_fc2, 2, normed)
    beside = [out_part, fc1_part[:1], fc1_part[1:], fc2_part[:1]]
    qkv = gather_group(normed, add_blocks, beside)
    out_part, fc1_part = share_cores(out_part), share_cores(fc1_part)
    ends = jnp.cumsum(lengths[0]).astype(jnp.int32)
    base = (group * (rows * HEADS)).astype(jnp.int32).reshape(1)
    shift, window = 0, None
    up = [(i, i + 1) for i in range(groups - 1)]
    down = [(i + 1, i) for i in range(groups - 1)]
    if groups > 1:
        margin = -(-LONG // rows)
        shift = margin * rows
        both = qkv[:, HEAD_DIM:]
        before = lax.ppermute(both[HEADS - margin :], "g", up)
        after = lax.ppermute(both[:margin], "g", down)
        window = jnp.concatenate([before, both, after], axis=0)
    attended, log_total = attention_forward(
        ends, base, qkv, window, shift
    )
    qkv_part = fetch_fsdp(w_qkv, 1, attended)
    fc2_part = share_cores(fc2_part, attended)
    out_full = join_fsdp(w_out, out_part, attended)
    fc1_full = join_fsdp(w_fc1, fc1_part, attended)
    fc2_full = join_fsdp(w_fc2, fc2_part, attended)
    small = (b_out, ln2_gain, ln2_bias, b_fc1, b_fc2)
    packed = join_small(tie(jnp.concatenate(small), normed))
    vectors, at = [], 0
    for vec in small:
        size = vec.shape[0]
        vectors.append(packed[:, at : at + size].reshape(-1).astype(f32))
        at += size
    out_bias, gain_two, bias_two, fc1_bias, fc2_bias = vectors
    mixed = lax.all_to_all(attended, SEQ, 0, 0, tiled=True).reshape(width, rows)

    branch = dot(mixed, out_full, 0, 0) + out_bias
    middle = hidden + tie(branch, fc2_full)
    normed_two_pre, scaled_two, inv_two = norm_forward(middle, gain_two, bias_two)
    normed_two = normed_two_pre.astype(low)
    inner_sum = dot(normed_two, fc1_full, 1, 0) + fc1_bias
    active, gelu_pull = jax.vjp(partial(jax.nn.gelu, approximate=True), inner_sum)
    active_low = active.astype(low)

    out_cot = out_grad[0]
    cot_full = out_cot.astype(f32)
    qkv_part = share_cores(qkv_part, active_low)
    fc2_sum = WeightSum(active_low, out_cot, scale)
    token = fc2_sum.other_core()
    block_out = middle + (dot(tie(active_low, token), fc2_full, 1, 0) + fc2_bias)
    token = fc2_sum.other_f(block_out)
    active_grad = dot(tie(out_cot, token), fc2_full, 1, 1)
    inner_grad = gelu_pull(active_grad)[0].astype(low)
    fc1_sum = WeightSum(normed_two, inner_grad, scale)
    norm_two_grad = dot(inner_grad, fc1_full, 1, 1)
    gain_two_grad, bias_two_grad, middle_from_norm = norm_backward(
        norm_two_grad, scaled_two, inv_two, gain_two
    )
    middle_grad = cot_full + middle_from_norm
    branch_grad = middle_grad.astype(low)
    out_sum = WeightSum(mixed, branch_grad, scale, 1)
    mixed_grad = dot(out_full, branch_grad, 1, 1).astype(low)
    attended_grad = lax.all_to_all(
        mixed_grad.reshape(HEADS, HEAD_DIM, rows), SEQ, 0, 0, tiled=True
    )
    early = VectorSum(
        (
            jnp.sum(branch_grad.astype(f32), axis=0),
            gain_two_grad,
            bias_two_grad,
            jnp.sum(inner_grad.astype(f32), axis=0),
            jnp.sum(cot_full, axis=0),
        ),
        scale,
    )
    token = fc1_sum.other_core(mixed_grad)
    early.core(mixed_grad)
    token = early.other_f(token)
    token = fc1_sum.other_f(token)
    token = out_sum.other_core(token)
    token = fc2_sum.near_y(token)
    tokens = [out_sum.other_f(token)]

    chunk = HEADS if groups > 1 else HEADS // CHUNKS
    plan = {
        0: [fc2_sum.near_z, early.near_y],
        1: [fc2_sum.far_z, fc1_sum.near_y, early.near_z],
        2: [fc2_sum.back_far_z, fc1_sum.near_z, out_sum.near_y, early.far_z],
        3: [fc2_sum.back_near_z, fc1_sum.far_z, out_sum.near_z, early.result],
    }
    carried = None
    for step in range(HEADS // chunk):
        results = attention_backward(
            ends, tie(base, *tokens), qkv, window, attended, attended_grad, log_total, shift,
            step * chunk, chunk, carried,
        )
        carried = results[::-1]
        tokens = [move(results[0]) for move in plan.pop(step)]
    for left in plan.values():
        for move in left:
            move(results[0])
    head_grad, *window_grad = results
    if groups > 1:
        both = window_grad[0]
        inner = both[margin : margin + HEADS]
        before = lax.ppermute(both[:margin], "g", down)
        after = lax.ppermute(both[margin + HEADS :], "g", up)
        inner = inner.at[HEADS - margin :].add(before).at[:margin].add(after)
        head_grad = jnp.concatenate([head_grad, inner.astype(low)], axis=1)
    token_grad = lax.all_to_all(head_grad, SEQ, 0, 0, tiled=True)

    weight_part = head_weight(kept_places, head_grad, kept_blocks)
    qkv_full = join_fsdp(w_qkv, qkv_part, weight_part)
    weight_part = weight_part.reshape(3 * HEAD_DIM, parts, shard_rows).transpose(1, 0, 2)
    if parts == 2:
        weight_part = halve(weight_part, "f")
    else:
        weight_part = lax.psum_scatter(weight_part, "f", scatter_dimension=0, tiled=False)
    if groups > 1:
        weight_part = lax.psum(weight_part, "g")

    weight_part = (weight_part * scale).astype(low)
    fc2_sum.back_y(weight_part)
    fc1_sum.back_far_z(weight_part)
    out_sum.far_z(weight_part)
    fc1_sum.back_near_z()
    out_sum.back_far_z()
    fc2_grad = fc2_sum.result()

    token_grad = (
        tie(token_grad, fc2_grad).reshape(HEADS, 3, HEAD_DIM, rows).transpose(1, 0, 2, 3).reshape(3 * width, rows)
    )
    norm_one_grad = dot(token_grad, qkv_full, 0, 1)
    gain_one_grad, bias_one_grad, hidden_from_norm = norm_backward(
        norm_one_grad, scaled_one, inv_one, gain_one
    )
    patch_grad = middle_grad + hidden_from_norm

    head_sums = jnp.sum(head_grad.astype(f32), axis=(0, 2))
    qv_grad = jnp.zeros((2 * width,), f32)
    qv_grad = lax.dynamic_update_slice(qv_grad, head_sums[:HEAD_DIM], (head * HEAD_DIM,))
    qv_grad = lax.dynamic_update_slice(
        qv_grad, head_sums[2 * HEAD_DIM :], (width + head * HEAD_DIM,)
    )
    late = VectorSum((gain_one_grad, bias_one_grad, qv_grad), scale)
    token = late.core()
    hops = [
        lax.ppermute(tie(weight_part, token), "z", [(i, (i + k) % 4) for i in range(4)]) for k in range(1, 4)
    ]
    token = late.other_f(token)
    fc1_sum.back_y(token)
    out_sum.back_near_z(token)
    plane = lax.axis_index("z")
    planes = jnp.zeros((4,) + weight_part.shape, low)
    for k, piece in enumerate([weight_part] + hops):
        planes = lax.dynamic_update_index_in_dim(planes, piece, lax.rem(plane + 4 - k, 4), 0)
    planes = in_order(planes, swap(planes, "y"), lax.axis_index("y"))
    late.near_y(planes)
    out_sum.back_y(planes)
    planes = in_order(planes, swap(planes, "c"), lax.axis_index("c"))
    late.near_z(planes)
    qkv_weight_grad = weave(planes.reshape((HEADS,) + weight_part.shape))
    late.far_z(qkv_weight_grad)
    fc1_grad, out_weight_grad = fc1_sum.result(), out_sum.result()
    late.result(fc1_grad)
    ln1_gain_sum, ln1_bias_sum, qv_sum = late.vectors()
    out_bias_sum, ln2_gain_sum, ln2_bias_sum, fc1_bias_sum, fc2_bias_sum = early.vectors()
    return (
        block_out.astype(low)[None],
        patch_grad[None],
        ln1_gain_sum,
        ln1_bias_sum,
        qkv_weight_grad,
        qv_sum,
        out_weight_grad,
        out_bias_sum,
        ln2_gain_sum,
        ln2_bias_sum,
        fc1_grad,
        fc1_bias_sum,
        fc2_grad,
        fc2_bias_sum,
    )


def solution(mesh):
    seq, parts = mesh.shape["seq"], mesh.shape["fsdp"]
    fine = Mesh(mesh.devices.reshape(seq // HEADS, HEADS // 4, 2, 2, parts), ("g", "z", "y", "c", "f"))
    rows = P("f", ("g",) + SEQ, None)
    vec, mat = P("f"), P("f", None)
    in_specs = (rows, rows, mat, rows, vec, vec, mat, vec, mat, vec, vec, vec, mat, vec, mat, vec)
    out_specs = (rows, rows, vec, vec, mat, vec, mat, vec, vec, vec, mat, vec, mat, vec)
    return jax.shard_map(body, mesh=fine, in_specs=in_specs, out_specs=out_specs, check_vma=False)
```

```python
import math
from functools import partial

import jax
import jax.numpy as jnp
from jax import lax
from jax.experimental import pallas as pl
from jax.experimental.pallas import tpu as pltpu
from jax.sharding import Mesh, PartitionSpec as P

HEADS = 16
LONG = 2304
NORM_EPS = 1e-06
CHUNKS = (2, 3, 3, 3, 3, 2)
HEAD_DIM = 64
BLOCK = 512
FAR = 1e30
QB = 512
KB = 512
CALM_SCORE = 60.0
FORWARD_COST = 50_000_000_000
BACKWARD_COST = 75_000_000_000


def rows_dot(a, b):
    return lax.dot_general(a, b, (((1,), (0,)), ((), ())), preferred_element_type=jnp.float32)


def membership(ends_ref, count, first, width):
    place = first + lax.broadcasted_iota(jnp.int32, (16, width), 1)
    row = lax.broadcasted_iota(jnp.int32, (16, width), 0)
    low = jnp.zeros((16, width), jnp.int32)
    high = jnp.zeros((16, width), jnp.int32)
    for i in range(count):
        begin = ends_ref[i - 1] if i > 0 else 0
        low = jnp.where(row == i, begin, low)
        high = jnp.where(row == i, ends_ref[i], high)
    return jnp.where((place >= low) & (place < high), 1.0, 0.0)


def image_span(ends_ref, count, first, last):
    low = jnp.int32(0)
    high = ends_ref[count - 1]
    for i in range(count - 1):
        end = ends_ref[i]
        low = jnp.where(end <= first, end, low)
    for i in range(count - 2, -1, -1):
        end = ends_ref[i]
        high = jnp.where(end > last, end, high)
    return low, high


def split3(x):
    top = x.astype(jnp.bfloat16)
    rest = x - top.astype(jnp.float32)
    mid = rest.astype(jnp.bfloat16)
    low = (rest - mid.astype(jnp.float32)).astype(jnp.bfloat16)
    return [top.astype(jnp.float32), mid.astype(jnp.float32), low.astype(jnp.float32)]


def parts_of(ref):
    return [ref.at[:, i * HEAD_DIM : (i + 1) * HEAD_DIM, :] for i in range(ref.shape[1] // HEAD_DIM)]


def forward_kernel(count, shift, ends_ref, base_ref, own_ref, *refs):
    q_ref, k_ref, v_ref = parts_of(own_ref)
    if shift:
        k_ref, v_ref = parts_of(refs[0])
        refs = refs[1:]
    o_ref, log_ref, qa, kn, va, peak = refs
    peak[...] = jnp.zeros_like(peak)
    q_blocks = q_ref.shape[0]
    k_blocks = k_ref.shape[0]
    key_count = k_blocks * BLOCK
    base = base_ref[0]

    @pl.loop(0, k_blocks)
    def _(i):
        at = pl.ds(pl.multiple_of(i * BLOCK, BLOCK), BLOCK)
        away = (membership(ends_ref, count, base - shift + i * BLOCK, BLOCK) - 1.0) * FAR
        keys = k_ref[i].astype(jnp.float32)
        peak[1:2] = jnp.maximum(peak[1:2], jnp.sum(keys * keys, axis=0, keepdims=True))
        both = jnp.concatenate([keys, away], axis=0)
        kn[at, :] = both.T.astype(jnp.bfloat16)
        va[:, at] = jnp.concatenate(
            [v_ref[i].astype(jnp.float32), jnp.ones((16, BLOCK), jnp.float32)], axis=0
        ).astype(jnp.bfloat16)

    @pl.loop(0, q_blocks)
    def _(i):
        at = pl.ds(pl.multiple_of(i * BLOCK, BLOCK), BLOCK)
        inside = membership(ends_ref, count, base + i * BLOCK, BLOCK)
        asked = q_ref[i].astype(jnp.float32)
        peak[0:1] = jnp.maximum(peak[0:1], jnp.sum(asked * asked, axis=0, keepdims=True))
        qa[:, at] = jnp.concatenate(
            [asked * (HEAD_DIM ** -0.5), inside], axis=0
        ).astype(jnp.bfloat16)

    per = BLOCK // QB
    calm = CALM_SCORE * HEAD_DIM ** 0.5
    peaks = [jnp.max(peak[i : i + 1]) for i in range(2)]

    def span(i):
        first = base + i * QB
        low, high = image_span(ends_ref, count, first, first + QB - 1)
        low = jnp.maximum(low - base + shift, 0) // KB
        return low, jnp.minimum(high - base + shift + KB - 1, key_count) // KB

    def finish(i, top, acc):
        total = acc[HEAD_DIM : HEAD_DIM + 1]
        o_ref[i // per, :, pl.ds(pl.multiple_of((i % per) * QB, QB), QB)] = (
            acc[:HEAD_DIM] / total
        ).astype(jnp.bfloat16)
        log_ref[:, pl.ds(pl.multiple_of(i * QB, QB), QB)] = top + jnp.log(total)

    small = peaks[0] * peaks[1] <= calm * calm

    @pl.when(small)
    def _():
        @pl.loop(0, q_blocks * per)
        def _(i):
            q_part = qa[:, pl.ds(pl.multiple_of(i * QB, QB), QB)]

            def step(j, acc):
                at = pl.ds(pl.multiple_of(j * KB, KB), KB)
                weights = jnp.exp(rows_dot(kn[at, :], q_part)).astype(jnp.bfloat16)
                return acc + rows_dot(va[:, at], weights)

            acc = lax.fori_loop(*span(i), step, jnp.zeros((HEAD_DIM + 16, QB), jnp.float32))
            finish(i, 0.0, acc)

    @pl.when(jnp.logical_not(small))
    def _():
        @pl.loop(0, q_blocks * per)
        def _(i):
            q_part = qa[:, pl.ds(pl.multiple_of(i * QB, QB), QB)]

            def step(j, carry):
                top, acc = carry
                at = pl.ds(pl.multiple_of(j * KB, KB), KB)
                scores = rows_dot(kn[at, :], q_part)
                new_top = jnp.maximum(top, jnp.max(scores, axis=0, keepdims=True))
                weights = jnp.exp(scores - new_top).astype(jnp.bfloat16)
                acc = acc * jnp.exp(top - new_top) + rows_dot(va[:, at], weights)
                return new_top, acc

            start = (
                jnp.full((1, QB), -3e38, jnp.float32),
                jnp.zeros((HEAD_DIM + 16, QB), jnp.float32),
            )
            finish(i, *lax.fori_loop(*span(i), step, start))


def backward_kernel(count, shift, first_block, chunk, last, ends_ref, base_ref, own_ref, *refs):
    q_ref, k_ref, v_ref = parts_of(own_ref)
    if shift:
        k_ref, v_ref = parts_of(refs[0])
        refs = refs[1:]
    o_ref, do_ref, log_ref, *refs = refs
    if first_block > 0:
        sums_in, _, *refs = refs
    grad_ref, *refs = refs
    sums_out = None
    if shift:
        window_ref, *refs = refs
    if not last:
        sums_out, *refs = refs
    qa, da, kn, vn, qn, dn, ks, sums, dq_part, sums_sem, dq_sem, *refs = refs
    k_blocks = k_ref.shape[0]
    key_count = k_blocks * BLOCK
    base = base_ref[0]
    scale = HEAD_DIM ** -0.5
    start = base + first_block * BLOCK
    low, high = image_span(ends_ref, count, start, start + chunk * BLOCK - 1)
    low = jnp.maximum(low - base + shift, 0) // BLOCK
    high = jnp.minimum(high - base + shift + BLOCK - 1, key_count) // BLOCK
    held_low, held_high = (0, k_blocks) if last or first_block == 0 else (low, high)

    def block_at(i):
        return pl.ds(pl.multiple_of(i * BLOCK, BLOCK), BLOCK)

    if first_block > 0:

        @pl.loop(held_low, held_high)
        def _(i):
            pltpu.make_async_copy(sums_in.at[block_at(i)], sums.at[block_at(i)], sums_sem.at[i]).start()

    else:
        sums[...] = jnp.zeros_like(sums)

    @pl.loop(low, high)
    def _(i):
        at = block_at(i)
        away = (membership(ends_ref, count, base - shift + i * BLOCK, BLOCK) - 1.0) * FAR
        ones = jnp.ones((16, BLOCK), jnp.float32)
        keys = k_ref[i].astype(jnp.float32)
        kn[at, :] = jnp.concatenate([keys, away, ones], axis=0).T.astype(jnp.bfloat16)
        vn[at, :] = jnp.concatenate([v_ref[i].astype(jnp.float32), ones], axis=0).T.astype(jnp.bfloat16)
        ks[:, at] = (keys * scale).astype(jnp.bfloat16)

    @pl.loop(0, chunk)
    def _(i):
        at = block_at(i)
        block = first_block + i
        inside = membership(ends_ref, count, base + block * BLOCK, BLOCK)
        pad = jnp.zeros((13, BLOCK), jnp.float32)
        scaled = q_ref[block].astype(jnp.float32) * scale
        qn[at, :] = scaled.T.astype(jnp.bfloat16)
        qa[:, at] = jnp.concatenate(
            [scaled, inside] + split3(-log_ref[:, block_at(block)]) + [pad], axis=0
        ).astype(jnp.bfloat16)
        grads = do_ref[block].astype(jnp.float32)
        row_dot = jnp.sum(grads * o_ref[block].astype(jnp.float32), axis=0, keepdims=True)
        dn[at, :] = grads.T.astype(jnp.bfloat16)
        da[:, at] = jnp.concatenate([grads] + split3(-row_dot) + [pad], axis=0).astype(jnp.bfloat16)

    if first_block > 0:

        @pl.loop(held_low, held_high)
        def _(i):
            pltpu.make_async_copy(sums_in.at[block_at(i)], sums.at[block_at(i)], sums_sem.at[i]).wait()

    @pl.loop(0, chunk)
    def _(i):
        q_at = block_at(i)
        q_part = qa[:, q_at]
        d_part = da[:, q_at]
        q_rows = qn[q_at, :]
        d_rows = dn[q_at, :]
        first = start + i * BLOCK
        key_low, key_high = image_span(ends_ref, count, first, first + BLOCK - 1)
        key_low = jnp.maximum(key_low - base + shift, 0) // BLOCK
        key_high = jnp.minimum(key_high - base + shift + BLOCK - 1, key_count) // BLOCK

        def step(j, dq):
            at = block_at(j)
            probs = jnp.exp(rows_dot(kn[at, :], q_part))
            score_grad = (probs * rows_dot(vn[at, :], d_part)).astype(jnp.bfloat16)
            sums[at, 0:HEAD_DIM] += rows_dot(score_grad, q_rows)
            sums[at, HEAD_DIM : 2 * HEAD_DIM] += rows_dot(probs.astype(jnp.bfloat16), d_rows)
            return dq + rows_dot(ks[:, at], score_grad)

        dq = lax.fori_loop(key_low, key_high, step, jnp.zeros((HEAD_DIM, BLOCK), jnp.float32))
        dq_part[i] = dq.astype(jnp.bfloat16)

    def query_copy(i):
        return pltpu.make_async_copy(
            dq_part.at[i], grad_ref.at[first_block + i, 0:HEAD_DIM], dq_sem.at[i]
        )

    for i in range(chunk):
        query_copy(i).start()
    if not last:

        @pl.loop(held_low, held_high)
        def _(i):
            pltpu.make_async_copy(sums.at[block_at(i)], sums_out.at[block_at(i)], sums_sem.at[i]).start()

        @pl.loop(held_low, held_high)
        def _(i):
            pltpu.make_async_copy(sums.at[block_at(i)], sums_out.at[block_at(i)], sums_sem.at[i]).wait()

    elif shift:

        @pl.loop(0, k_blocks)
        def _(i):
            window_ref[i] = sums[block_at(i), :].T

    else:
        kv_part, kv_sem = refs

        def key_copy(i):
            return pltpu.make_async_copy(
                kv_part.at[i], grad_ref.at[i, HEAD_DIM : 3 * HEAD_DIM], kv_sem.at[i]
            )

        @pl.loop(0, k_blocks)
        def _(i):
            kv_part[i] = sums[block_at(i), :].T.astype(jnp.bfloat16)
            key_copy(i).start()

        @pl.loop(0, k_blocks)
        def _(i):
            key_copy(i).wait()

    for i in range(chunk):
        query_copy(i).wait()


def vmem_spec():
    return pl.BlockSpec(memory_space=pltpu.VMEM)


def smem_spec():
    return pl.BlockSpec(memory_space=pltpu.SMEM)


def attention_forward(ends, base, own, window, shift):
    blocks = own.shape[0]
    tokens, keys = blocks * BLOCK, blocks * BLOCK + 2 * shift
    arrays = [own] + ([window] if shift else [])
    return pl.pallas_call(
        partial(forward_kernel, ends.shape[0], shift),
        out_shape=(
            jax.ShapeDtypeStruct((blocks, HEAD_DIM, BLOCK), jnp.bfloat16),
            jax.ShapeDtypeStruct((1, tokens), jnp.float32),
        ),
        in_specs=[smem_spec(), smem_spec()] + [vmem_spec()] * len(arrays),
        out_specs=(vmem_spec(), vmem_spec()),
        scratch_shapes=[
            pltpu.VMEM((HEAD_DIM + 16, tokens), jnp.bfloat16),
            pltpu.VMEM((keys, HEAD_DIM + 16), jnp.bfloat16),
            pltpu.VMEM((HEAD_DIM + 16, keys), jnp.bfloat16),
            pltpu.VMEM((8, BLOCK), jnp.float32),
        ],
        compiler_params=pltpu.CompilerParams(vmem_limit_bytes=48 * 1024 * 1024),
        cost_estimate=pl.CostEstimate(flops=FORWARD_COST, bytes_accessed=tokens * 512, transcendentals=0),
    )(ends, base, *arrays)


def attention_backward(ends, base, own, window, o, do, log, shift, first_block, chunk, carried):
    blocks = own.shape[0]
    tokens, keys = chunk * BLOCK, blocks * BLOCK + 2 * shift
    last = first_block + chunk == blocks
    low, f32 = jnp.bfloat16, jnp.float32
    arrays = [own] + ([window] if shift else []) + [o, do, log]
    in_specs = [smem_spec(), smem_spec()] + [vmem_spec()] * len(arrays)
    out_shape = [jax.ShapeDtypeStruct((blocks, HEAD_DIM if shift else 3 * HEAD_DIM, BLOCK), low)]
    out_specs = [any_spec()]
    aliases = {}
    if carried is not None:
        place_at = 2 + len(arrays)
        arrays += list(carried)
        in_specs += [any_spec(), any_spec()]
        aliases = {place_at + 1: 0}
        if not last:
            aliases[place_at] = 1
    if shift:
        out_shape.append(jax.ShapeDtypeStruct((keys // BLOCK, 2 * HEAD_DIM, BLOCK), f32))
        out_specs.append(vmem_spec())
    if not last:
        out_shape.append(jax.ShapeDtypeStruct((keys, 2 * HEAD_DIM), f32))
        out_specs.append(any_spec())
    scratch = [
        pltpu.VMEM((HEAD_DIM + 32, tokens), low),
        pltpu.VMEM((HEAD_DIM + 16, tokens), low),
        pltpu.VMEM((keys, HEAD_DIM + 32), low),
        pltpu.VMEM((keys, HEAD_DIM + 16), low),
        pltpu.VMEM((tokens, HEAD_DIM), low),
        pltpu.VMEM((tokens, HEAD_DIM), low),
        pltpu.VMEM((HEAD_DIM, keys), low),
        pltpu.VMEM((keys, 2 * HEAD_DIM), f32),
        pltpu.VMEM((chunk, HEAD_DIM, BLOCK), low),
        pltpu.SemaphoreType.DMA((keys // BLOCK,)),
        pltpu.SemaphoreType.DMA((chunk,)),
    ]
    if last and not shift:
        scratch += [
            pltpu.VMEM((blocks, 2 * HEAD_DIM, BLOCK), low),
            pltpu.SemaphoreType.DMA((blocks,)),
        ]
    return pl.pallas_call(
        partial(backward_kernel, ends.shape[0], shift, first_block, chunk, last),
        out_shape=out_shape,
        in_specs=in_specs,
        out_specs=out_specs,
        scratch_shapes=scratch,
        input_output_aliases=aliases,
        compiler_params=pltpu.CompilerParams(vmem_limit_bytes=50 * 1024 * 1024),
        cost_estimate=pl.CostEstimate(flops=BACKWARD_COST * chunk // blocks, bytes_accessed=tokens * 1024, transcendentals=0),
    )(ends, base, *arrays)


def any_spec():
    return pl.BlockSpec(memory_space=pl.ANY)


def block_rows(rows, cols):
    while rows * cols > 512 * 1024 and rows % 16 == 0:
        rows //= 2
    return rows


def take_kernel(at_ref, in_ref, out_ref):
    out_ref[...] = in_ref[...]


def take(x, index, count):
    rows, cols = x.shape[0] // count, x.shape[1]
    size = block_rows(rows, cols)
    steps = rows // size
    return pl.pallas_call(
        take_kernel,
        out_shape=jax.ShapeDtypeStruct((rows, cols), x.dtype),
        grid_spec=pltpu.PrefetchScalarGridSpec(
            num_scalar_prefetch=1,
            grid=(steps,),
            in_specs=[pl.BlockSpec((size, cols), lambda j, at_ref: (at_ref[0] * steps + j, 0))],
            out_specs=pl.BlockSpec((size, cols), lambda j, at_ref: (j, 0)),
        ),
        cost_estimate=pl.CostEstimate(flops=0, bytes_accessed=2 * rows * cols * x.dtype.itemsize, transcendentals=0),
    )(index.astype(jnp.int32).reshape(1), x)


def place_kernel(owner, row_ref, col_ref, *refs):
    out_ref = refs[-1]
    for i, piece in enumerate(owner):

        @pl.when(pl.program_id(0) == i)
        def _(piece=piece):
            out_ref[...] = refs[piece][...].astype(out_ref.dtype)


def place(pieces, row_at, col_at, dtype, rows, shape, cols=None, block=0):
    cols = cols or pieces[0].shape[1]
    owner = [n for n, piece in enumerate(pieces) for _ in range(piece.shape[0] // rows)]
    count = len(owner)
    size = block_rows(rows, cols)
    steps = rows // size

    def piece_map(piece):
        turns = [i for i in range(count) if owner[i] == piece]
        first, last = turns[0], turns[-1]

        def index(s, j, row_ref, col_ref):
            inside = j + (s - first) * steps
            end = (last - first + 1) * steps - 1
            return (jnp.where(s < first, 0, jnp.where(s > last, end, inside)), block)

        return index

    return pl.pallas_call(
        partial(place_kernel, owner),
        out_shape=jax.ShapeDtypeStruct(shape, dtype),
        grid_spec=pltpu.PrefetchScalarGridSpec(
            num_scalar_prefetch=2,
            grid=(count, steps),
            in_specs=[pl.BlockSpec((size, cols), piece_map(i)) for i in range(len(pieces))],
            out_specs=pl.BlockSpec(
                (size, cols), lambda s, j, row_ref, col_ref: (row_ref[s] * steps + j, col_ref[s])
            ),
        ),
        cost_estimate=pl.CostEstimate(
            flops=0,
            bytes_accessed=count * rows * cols * (2 + jnp.dtype(dtype).itemsize),
            transcendentals=0,
        ),
    )(row_at, col_at, *pieces)


def head_columns_kernel(head_ref, q_ref, k_ref, v_ref, out_ref):
    odd = lax.rem(head_ref[0], 2) == 1
    for part, ref in enumerate((q_ref, k_ref, v_ref)):
        both = ref[...].astype(jnp.float32).T
        mine = jnp.where(odd, both[HEAD_DIM:], both[:HEAD_DIM])
        out_ref[part * HEAD_DIM : (part + 1) * HEAD_DIM] = mine.astype(out_ref.dtype)


def head_columns(w, head):
    rows, pairs = w.shape[0], HEADS // 2

    def spec(part):
        return pl.BlockSpec(
            (rows, 2 * HEAD_DIM), lambda i, head_ref: (0, part * pairs + head_ref[0] // 2)
        )

    return pl.pallas_call(
        head_columns_kernel,
        out_shape=jax.ShapeDtypeStruct((3 * HEAD_DIM, rows), w.dtype),
        grid_spec=pltpu.PrefetchScalarGridSpec(
            num_scalar_prefetch=1,
            grid=(1,),
            in_specs=[spec(part) for part in range(3)],
            out_specs=pl.BlockSpec((3 * HEAD_DIM, rows), lambda i, head_ref: (0, 0)),
        ),
    )(head.astype(jnp.int32).reshape(1), w, w, w)


def project_kernel(count, place_ref, w_ref, bias_ref, *refs):
    blocks, out_ref, made, sem = refs[:count], refs[-3], refs[-2], refs[-1]

    def copy(i):
        return pltpu.make_async_copy(made.at[i], out_ref.at[place_ref[i]], sem.at[i])

    size = w_ref.shape[2]
    for i in range(count):
        total = bias_ref[...]
        for f in range(w_ref.shape[0]):
            total += lax.dot_general(
                w_ref[f], blocks[i][:, f * size : (f + 1) * size], (((1,), (1,)), ((), ())),
                preferred_element_type=jnp.float32,
            )
        made[i] = total.astype(jnp.bfloat16)
        copy(i).start()
    for i in range(count):
        copy(i).wait()


def project(so_far, places, w, bias, blocks):
    count = len(blocks)
    rows, width = blocks[0].shape
    cols = w.shape[1]
    arrays = [w, bias, *blocks] + ([] if so_far is None else [so_far])
    specs = [vmem_spec()] * (2 + count) + ([] if so_far is None else [any_spec()])
    return pl.pallas_call(
        partial(project_kernel, count),
        out_shape=jax.ShapeDtypeStruct((HEADS, cols, rows), jnp.bfloat16),
        in_specs=[smem_spec()] + specs,
        out_specs=any_spec(),
        scratch_shapes=[
            pltpu.VMEM((count, cols, rows), jnp.bfloat16),
            pltpu.SemaphoreType.DMA((count,)),
        ],
        input_output_aliases={} if so_far is None else {3 + count: 0},
        compiler_params=pltpu.CompilerParams(vmem_limit_bytes=24 * 1024 * 1024),
        cost_estimate=pl.CostEstimate(flops=4 * count * rows * width * cols, bytes_accessed=count * rows * width * 2, transcendentals=0),
    )(jnp.stack(places).astype(jnp.int32), *arrays)


SLOTS = 4


def head_weight_kernel(count, place_ref, grad_ref, *refs):
    blocks, (out_ref, held, sem) = refs[:count], refs[count:]

    def copy(b):
        return pltpu.make_async_copy(blocks[b], held.at[b % SLOTS], sem.at[b % SLOTS])

    for b in range(SLOTS - 1):
        copy(b).start()
    out_ref[...] = jnp.zeros_like(out_ref)

    @pl.loop(0, count)
    def _(i):
        slot = lax.rem(i, SLOTS)
        pltpu.make_async_copy(blocks[0], held.at[slot], sem.at[slot]).wait()
        for b in range(SLOTS - 1, count):

            @pl.when(i + SLOTS - 1 == b)
            def _(b=b):
                copy(b).start()

        out_ref[...] += rows_dot(grad_ref[place_ref[i]], held[slot])


def head_weight(places, grad, blocks):
    count = len(blocks)
    rows, width = blocks[0].shape
    cols = grad.shape[1]
    return pl.pallas_call(
        partial(head_weight_kernel, count),
        out_shape=jax.ShapeDtypeStruct((cols, width), jnp.float32),
        in_specs=[smem_spec(), vmem_spec()] + [any_spec()] * count,
        out_specs=vmem_spec(),
        scratch_shapes=[
            pltpu.VMEM((SLOTS, rows, width), jnp.bfloat16),
            pltpu.SemaphoreType.DMA((SLOTS,)),
        ],
        compiler_params=pltpu.CompilerParams(vmem_limit_bytes=24 * 1024 * 1024),
        cost_estimate=pl.CostEstimate(flops=4 * count * rows * width * cols, bytes_accessed=count * rows * width * 2, transcendentals=0),
    )(jnp.stack(places).astype(jnp.int32), grad, *blocks)


def weave_kernel(count, at_ref, *refs):
    pieces, (out_ref, held) = refs[:count], refs[count:]
    for i in range(count):
        held[at_ref[i]] = pieces[i][...]
    for part in range(3):
        for pair in range(count // 2):
            rows = slice(part * HEAD_DIM, (part + 1) * HEAD_DIM)
            both = jnp.concatenate([held[2 * pair, rows], held[2 * pair + 1, rows]], axis=0)
            at = (part * count + 2 * pair) * HEAD_DIM
            out_ref[:, at : at + 2 * HEAD_DIM] = both.astype(jnp.float32).T


def weave(pieces, places):
    count = len(pieces)
    cols, rows = pieces[0].shape
    size = 128
    return pl.pallas_call(
        partial(weave_kernel, count),
        out_shape=jax.ShapeDtypeStruct((rows, count * cols), jnp.float32),
        grid_spec=pltpu.PrefetchScalarGridSpec(
            num_scalar_prefetch=1,
            grid=(rows // size,),
            in_specs=[pl.BlockSpec((cols, size), lambda i, at_ref: (0, i))] * count,
            out_specs=pl.BlockSpec((size, count * cols), lambda i, at_ref: (i, 0)),
            scratch_shapes=[pltpu.VMEM((count, cols, size), pieces[0].dtype)],
        ),
        cost_estimate=pl.CostEstimate(
            flops=0, bytes_accessed=6 * count * cols * rows, transcendentals=0
        ),
    )(places, *pieces)


SEQ = ("z", "y", "c")
SWAP = ((0, 1), (1, 0))


def norm_forward(hidden, gain_vec, offset_vec):
    centre = hidden - jnp.mean(hidden, axis=-1, keepdims=True)
    spread = jnp.mean(centre * centre, axis=-1, keepdims=True)
    inv_std = lax.rsqrt(spread + NORM_EPS)
    scaled = centre * inv_std
    return (scaled * gain_vec + offset_vec, scaled, inv_std)


def norm_backward(grad_out, scaled, inv_std, gain_vec):
    gain_grad = jnp.sum(grad_out * scaled, axis=0)
    offset_grad = jnp.sum(grad_out, axis=0)
    grad_scaled = grad_out * gain_vec
    grad_in = inv_std * (
        grad_scaled
        - jnp.mean(grad_scaled, axis=-1, keepdims=True)
        - scaled * jnp.mean(grad_scaled * scaled, axis=-1, keepdims=True)
    )
    return (gain_grad, offset_grad, grad_in)


def dot(a, b, a_dim, b_dim):
    return lax.dot_general(
        a, b, (((a_dim,), (b_dim,)), ((), ())), preferred_element_type=jnp.float32
    )


def tie(x, *others):
    others = [other for other in others if other is not None]
    return lax.optimization_barrier((x, *others))[0] if others else x


def linear(start, first, a, second, b):
    start, first, second = (jnp.array(x, jnp.int32) for x in (start, first, second))
    return start + first * a + second * b


def pick(x, i, axis=0):
    return lax.dynamic_index_in_dim(x, i, axis, keepdims=False)


def swap(x, axis):
    return lax.ppermute(x, axis, SWAP)


def in_order(own, other, position):
    return jnp.where(position == 0, jnp.stack([own, other]), jnp.stack([other, own]))


def fetch_fsdp(shard, pieces, *others):
    if lax.axis_size("f") != 2:
        return [], [lax.all_gather(shard, "f", axis=0, tiled=True)]
    first = lax.axis_index("c") * pieces
    shard = tie(shard, *others)
    taken = [take(shard, first + i, 2 * pieces) for i in range(pieces)]
    return taken, [swap(part, "f") for part in taken]


def share_cores(fetched, *others):
    if lax.axis_size("f") != 2:
        return fetched
    return fetched + [swap(tie(piece, *others), "c") for piece in fetched]


def join_fsdp(shard, pieces, *others):
    if lax.axis_size("f") != 2:
        return pieces[0]
    core, here = lax.axis_index("c"), lax.axis_index("f")
    count = len(pieces) // 2
    step = range(count)
    at = linear(
        (*range(2 * count), *(2 * count + i for i in step), *(3 * count + i for i in step)),
        (2 * count,) * (2 * count) + (-2 * count,) * (2 * count),
        here,
        (0,) * (2 * count) + (count,) * count + (-count,) * count,
        core,
    )
    rows, cols = shard.shape
    return place(
        [tie(shard, *others), *pieces], at, jnp.zeros_like(at), shard.dtype, rows // (2 * count), (2 * rows, cols)
    )


def join_small(shard):
    if lax.axis_size("f") != 2:
        return lax.all_gather(shard, "f", axis=0, tiled=False)
    return in_order(shard, swap(shard, "f"), lax.axis_index("f"))


def halve(x, axis, pairs=SWAP, here=None):
    here = lax.axis_index(axis) if here is None else here
    got = lax.ppermute(pick(x, 1 - here), axis, pairs)
    return pick(x, here).astype(jnp.float32) + got.astype(jnp.float32)


def plane_pairs(bit):
    return [(i, i ^ bit) for i in range(4)]


class WeightSum:
    def __init__(self, terms, scale):
        self.terms, self.scale = terms, scale
        self.widths = [right.shape[1] // 2 for _, right, _ in terms]
        self.cols = sum(self.widths)
        self.rows = terms[0][0].shape[1 - terms[0][2]] // lax.axis_size("f")

    def after(self, others):
        self.terms = [(left, tie(right, *others), dim) for left, right, dim in self.terms]

    def term(self, n, c, f, half=None):
        left, right, dim = self.terms[n]
        rows, start = self.rows, f * self.rows
        if half is not None:
            rows //= 2
            start = start + half * rows
        left = lax.dynamic_slice_in_dim(left, start, rows, 1 - dim)
        right = lax.dynamic_slice_in_dim(right, c * self.widths[n], self.widths[n], 1)
        return dot(left, right, dim, 0)

    def joined(self, parts):
        parts = [part.astype(jnp.bfloat16) for part in parts]
        return parts[0] if len(parts) == 1 else jnp.concatenate(parts, axis=1)

    def half_of(self, x, half):
        rows = x.shape[0] // 2
        return lax.dynamic_slice_in_dim(x, half * rows, rows, 0).astype(jnp.float32)

    def other_core(self, *others):
        self.after(others)
        core, parts, here = lax.axis_index("c"), lax.axis_size("f"), lax.axis_index("f")
        order = [1 - here, here] if parts == 2 else range(parts)
        self.got = []
        for f in order:
            sent = [self.term(n, 1 - core, f).astype(jnp.bfloat16) for n in range(len(self.terms))]
            self.got.append([swap(part, "c") for part in sent])
        return sent[-1]

    def other_f(self, *others):
        self.after(others)
        core, parts, here = lax.axis_index("c"), lax.axis_size("f"), lax.axis_index("f")
        y, count = lax.axis_index("y"), range(len(self.terms))
        if parts == 2:
            self.far = []
            for half in (1 - y, y):
                sent = self.joined(
                    [self.term(n, core, 1 - here, half) + self.half_of(self.got[0][n], half) for n in count]
                )
                self.far.append(swap(sent, "f"))
                self.after([sent])
            return sent
        total = [
            self.joined([self.term(n, core, f) + self.got[f][n].astype(jnp.float32) for n in count])
            for f in range(parts)
        ]
        self.total = lax.psum_scatter(jnp.stack(total), "f", scatter_dimension=0, tiled=False)
        return self.total

    def here_half(self, k, half):
        core, parts, here = lax.axis_index("c"), lax.axis_size("f"), lax.axis_index("f")
        if parts != 2:
            return [self.half_of(self.total, half)]
        x, at = [], 0
        for n, width in enumerate(self.widths):
            total = self.term(n, core, here, half) + self.half_of(self.got[1][n], half)
            x.append(total + self.far[k][:, at : at + width].astype(jnp.float32))
            at += width
        return x

    def near_y(self, *others):
        self.after(others)
        sent = self.joined(self.here_half(0, 1 - lax.axis_index("y")))
        self.coming = lax.ppermute(sent, "y", SWAP)
        return sent

    def near_z(self, *others):
        self.coming = tie(self.coming, *others)
        self.after(others)
        x, at = [], 0
        for part in self.here_half(1, lax.axis_index("y")):
            width = part.shape[1]
            x.append(part + self.coming[:, at : at + width].astype(jnp.float32))
            at += width
        x = self.joined(x).reshape(2, -1, self.cols)
        low_z = lax.rem(lax.axis_index("z"), 2)
        sent = pick(x, 1 - low_z)
        self.kept, self.coming = pick(x, low_z), lax.ppermute(sent, "z", plane_pairs(1))
        return sent

    def added(self, x, others):
        return x.astype(jnp.float32) + tie(self.coming, *others).astype(jnp.float32)

    def far_z(self, *others):
        self.x = self.added(self.kept, others).astype(jnp.bfloat16)
        self.coming = lax.ppermute(self.x, "z", plane_pairs(2))
        return self.x

    def back_near_z(self, *others):
        x = self.added(self.x, others)
        if lax.axis_size("g") > 1:
            x = lax.psum(x, "g")
        self.x = (x * self.scale).astype(jnp.bfloat16)
        self.coming = lax.ppermute(self.x, "z", plane_pairs(1))
        return self.x

    def back_y(self, *others):
        coming = tie(self.coming, *others)
        x = in_order(self.x, coming, lax.rem(lax.axis_index("z"), 2)).reshape(-1, self.cols)
        self.near = lax.ppermute(x, "y", SWAP)
        self.x, self.across = x, swap(x, "c")
        return x

    def results(self, *others):
        y, c = lax.axis_index("y"), lax.axis_index("c")
        near = tie(self.near, *others)
        pieces = [self.x, near, self.across, swap(near, "c")]
        row_at = linear((0, 1, 0, 1), (1, -1, 1, -1), y, (0, 0, 0, 0), c)
        col_at = linear((0, 0, 1, 1), (0, 0, 0, 0), y, (1, 1, -1, -1), c)
        rows, at, results = pieces[0].shape[0], 0, []
        for width in self.widths:
            results.append(
                place(
                    pieces, row_at, col_at, jnp.float32, rows, (2 * rows, 2 * width), width, at // width
                )
            )
            at += width
        return results


class VectorSum:
    def __init__(self, vectors, scale):
        self.sizes = [vec.shape[0] // lax.axis_size("f") for vec in vectors]
        self.x = jnp.concatenate([vec.reshape(lax.axis_size("f"), -1) for vec in vectors], axis=1) * scale

    def core(self, *others):
        self.x = tie(self.x, *others)
        self.coming = swap(self.x, "c")
        return self.x

    def other_f(self, *others):
        x = self.x + tie(self.coming, *others)
        if lax.axis_size("f") == 2:
            here = lax.axis_index("f")
            self.x, sent = pick(x, here), pick(x, 1 - here)
            self.coming = swap(sent, "f")
            return sent
        self.x = lax.psum_scatter(x, "f", scatter_dimension=0, tiled=False)
        self.coming = jnp.zeros_like(self.x)
        return self.x

    def hop(self, axis, pairs, others):
        self.x = self.x + tie(self.coming, *others)
        self.coming = lax.ppermute(self.x, axis, pairs)
        return self.x

    def near_y(self, *others):
        return self.hop("y", SWAP, others)

    def near_z(self, *others):
        return self.hop("z", plane_pairs(1), others)

    def far_z(self, *others):
        return self.hop("z", plane_pairs(2), others)

    def result(self, *others):
        self.total = self.x + tie(self.coming, *others)
        if lax.axis_size("g") > 1:
            self.total = lax.psum(self.total, "g")
        return self.total

    def vectors(self):
        at = 0
        for size in self.sizes:
            yield self.total[at : at + size]
            at += size


def arrivals(count):
    table = []
    for z in range(count):
        hops = []
        for t in range(1, count):
            if z - t >= 0:
                hops.append(("up", t))
            if z + t < count:
                hops.append(("down", t))
        table.append(hops)
    return table


def gather_group(x, use, beside):
    z, y, c = (lax.axis_index(axis) for axis in SEQ)
    count = lax.axis_size("z")
    table = arrivals(count)
    up, down = x, x
    hops = {}
    block, plane = x, z
    state, items = None, []
    for t in range(1, count + 1):
        first = plane * 4
        if t < count:
            up = lax.ppermute(up, "z", [(i, i + 1) for i in range(t - 1, count - 1)])
            down = lax.ppermute(down, "z", [(i, i - 1) for i in range(1, count - t + 1)])
        near = swap(block, "y")
        items += [(block, first + 2 * y + c), (swap(block, "c"), first + 2 * y + 1 - c)]
        across, places = zip(*items)
        across = lax.optimization_barrier(across)
        state = use(state, across, places)
        up, down, near, state, _ = lax.optimization_barrier(
            (up, down, near, state, beside[t - 1] if t <= len(beside) else [])
        )
        items = [(near, first + 2 * (1 - y) + c), (swap(near, "c"), first + 2 * (1 - y) + 1 - c)]
        if t < count:
            hops["up", t], hops["down", t] = up, down
            names = sorted({table[i][t - 1] for i in range(count)})
            block, plane = None, z
            for name in names:
                here = [i for i in range(count) if table[i][t - 1] == name]
                chosen = (z >= here[0]) & (z <= here[-1])
                block = hops[name] if block is None else jnp.where(chosen, hops[name], block)
                plane = jnp.where(chosen, z + (-name[1] if name[0] == "up" else name[1]), plane)
    return use(state, *zip(*items))


def body(
    patches, pos_embed, lengths, out_grad,
    ln1_gain, ln1_bias, w_qkv, b_qv, w_out, b_out,
    ln2_gain, ln2_bias, w_fc1, b_fc1, w_fc2, b_fc2,
):
    f32, low = jnp.float32, jnp.bfloat16
    rows, width = patches.shape[1:]
    groups, parts = lax.axis_size("g"), lax.axis_size("f")
    head = lax.axis_index(SEQ)
    group = lax.axis_index("g")
    shard_index = lax.axis_index("f")
    scale = 1.0 / (parts * math.sqrt(rows * HEADS * groups))

    gain_one, bias_one, qv_bias = (
        join_small(vec).reshape(-1).astype(f32) for vec in (ln1_gain, ln1_bias, b_qv)
    )
    hidden = patches[0].astype(f32) + pos_embed[0].astype(f32)
    normed_pre, scaled_one, inv_one = norm_forward(hidden, gain_one, bias_one)
    normed = normed_pre.astype(low)

    shard_rows = w_qkv.shape[0]
    head_full = join_small(head_columns(w_qkv, head)).reshape(parts, 3 * HEAD_DIM, shard_rows)
    head_bias = jnp.concatenate(
        [
            lax.dynamic_slice_in_dim(qv_bias, head * HEAD_DIM, HEAD_DIM),
            jnp.zeros((HEAD_DIM,), f32),
            lax.dynamic_slice_in_dim(qv_bias, width + head * HEAD_DIM, HEAD_DIM),
        ]
    )[:, None]

    normed = tie(normed, head_bias, head_full)
    kept_blocks, kept_places = [], []

    def add_blocks(qkv, blocks, places):
        kept_blocks.extend(blocks)
        kept_places.extend(places)
        return project(qkv, places, head_full, head_bias, blocks)

    out_taken, out_part = fetch_fsdp(w_out, 1, normed)
    fc1_taken, fc1_part = fetch_fsdp(w_fc1, 2, normed)
    fc2_taken, fc2_part = fetch_fsdp(w_fc2, 2, normed)
    qkv_taken, qkv_part = fetch_fsdp(w_qkv, 2, normed)
    out_full = join_fsdp(w_out, share_cores(out_part))
    beside = [out_part + out_taken + fc1_taken + fc2_taken + qkv_taken, [], fc1_part[:1], fc1_part[1:] + [out_full]]
    qkv = gather_group(normed, add_blocks, beside)
    ends = jnp.cumsum(lengths[0]).astype(jnp.int32)
    base = (group * (rows * HEADS)).astype(jnp.int32).reshape(1)
    shift, window = 0, None
    up = [(i, i + 1) for i in range(groups - 1)]
    down = [(i + 1, i) for i in range(groups - 1)]
    if groups > 1:
        margin = -(-LONG // rows)
        shift = margin * rows
        both = qkv[:, HEAD_DIM:]
        before = lax.ppermute(both[HEADS - margin :], "g", up)
        after = lax.ppermute(both[:margin], "g", down)
        window = jnp.concatenate([before, both, after], axis=0)
    attended, log_total = attention_forward(
        ends, base, qkv, window, shift
    )
    fc2_part = share_cores(fc2_part, attended)
    fc1_full = join_fsdp(w_fc1, share_cores(fc1_part), attended)
    fc2_full = join_fsdp(w_fc2, fc2_part, attended)
    small = (b_out, ln2_gain, ln2_bias, b_fc1, b_fc2)
    packed = join_small(tie(jnp.concatenate(small), normed))
    vectors, at = [], 0
    for vec in small:
        size = vec.shape[0]
        vectors.append(packed[:, at : at + size].reshape(-1).astype(f32))
        at += size
    out_bias, gain_two, bias_two, fc1_bias, fc2_bias = vectors
    mixed = lax.all_to_all(attended, SEQ, 0, 0, tiled=True).reshape(width, rows)

    branch = dot(mixed, out_full, 0, 0) + out_bias
    middle = hidden + tie(branch, fc2_full, qkv_part[0])
    normed_two_pre, scaled_two, inv_two = norm_forward(middle, gain_two, bias_two)
    normed_two = normed_two_pre.astype(low)
    inner_sum = dot(normed_two, fc1_full, 1, 0) + fc1_bias
    active, gelu_pull = jax.vjp(partial(jax.nn.gelu, approximate=True), inner_sum)
    active_low = active.astype(low)

    out_cot = out_grad[0]
    cot_full = out_cot.astype(f32)
    active_low, *qkv_part = lax.optimization_barrier((active_low, *qkv_part))
    qkv_part = share_cores(qkv_part)
    fc2_sum = WeightSum([(active_low, out_cot, 0)], scale)
    token = fc2_sum.other_core()
    active_grad = dot(tie(out_cot, token), fc2_full, 1, 1)
    inner_grad = gelu_pull(active_grad)[0].astype(low)
    token = fc2_sum.other_f(inner_grad)
    norm_two_grad = dot(tie(inner_grad, token), fc1_full, 1, 1)
    gain_two_grad, bias_two_grad, middle_from_norm = norm_backward(
        norm_two_grad, scaled_two, inv_two, gain_two
    )
    middle_grad = cot_full + middle_from_norm
    branch_grad = middle_grad.astype(low)
    mixed_grad = dot(out_full, branch_grad, 1, 1).astype(low)
    attended_grad = lax.all_to_all(
        mixed_grad.reshape(HEADS, HEAD_DIM, rows), SEQ, 0, 0, tiled=True
    )
    rest_sum = WeightSum([(normed_two, inner_grad, 0), (mixed, branch_grad, 1)], scale)
    token = rest_sum.other_core(mixed_grad)
    token = fc2_sum.near_y(token)
    token = rest_sum.other_f(token)
    block_out = middle + (dot(tie(active_low, token), fc2_full, 1, 0) + fc2_bias)
    tokens = [block_out]

    plan = [
        [fc2_sum.near_z, rest_sum.near_y],
        [fc2_sum.far_z, rest_sum.near_z],
        [fc2_sum.back_near_z, rest_sum.far_z],
        [fc2_sum.back_y],
        [rest_sum.back_near_z, lambda *after: fc2_sum.near],
        [rest_sum.back_y],
    ]
    carried, first = None, 0
    for chunk in [HEADS] if groups > 1 else CHUNKS:
        results = attention_backward(
            ends, tie(base, *tokens), qkv, window, attended, attended_grad, log_total, shift,
            first, chunk, carried,
        )
        carried, first = results[::-1], first + chunk
        tokens = []
        for move in plan.pop(0):
            tokens.append(move(results[0], *tokens))
    for moves in plan:
        for move in moves:
            tokens.append(move(results[0]))
    head_grad, *window_grad = results
    if groups > 1:
        both = window_grad[0]
        inner = both[margin : margin + HEADS]
        before = lax.ppermute(both[:margin], "g", down)
        after = lax.ppermute(both[margin + HEADS :], "g", up)
        inner = inner.at[HEADS - margin :].add(before).at[:margin].add(after)
        head_grad = jnp.concatenate([head_grad, inner.astype(low)], axis=1)
    token_grad = lax.all_to_all(tie(head_grad, *tokens), SEQ, 0, 0, tiled=True)

    weight_part = head_weight(kept_places, head_grad, kept_blocks)
    weight_part = weight_part.reshape(3 * HEAD_DIM, parts, shard_rows).transpose(1, 0, 2)
    if parts == 2:
        weight_part = halve(weight_part, "f")
    else:
        weight_part = lax.psum_scatter(weight_part, "f", scatter_dimension=0, tiled=False)
    if groups > 1:
        weight_part = lax.psum(weight_part, "g")

    weight_part = (weight_part * scale).astype(low)
    qkv_full = join_fsdp(w_qkv, qkv_part, weight_part)
    (fc2_grad,) = fc2_sum.results(qkv_full)
    fc1_grad, out_weight_grad = rest_sum.results(fc2_grad)
    token_grad = tie(token_grad, fc1_grad, out_weight_grad)
    z, y, c = (lax.axis_index(axis) for axis in SEQ)
    hops = [weight_part] + [
        lax.ppermute(weight_part, "z", [(i, (i + k) % 4) for i in range(4)]) for k in range(1, 4)
    ]

    token_grad = (
        tie(token_grad, fc2_grad).reshape(HEADS, 3, HEAD_DIM, rows).transpose(1, 0, 2, 3).reshape(3 * width, rows)
    )
    norm_one_grad = dot(token_grad, qkv_full, 0, 1)
    gain_one_grad, bias_one_grad, hidden_from_norm = norm_backward(
        norm_one_grad, scaled_one, inv_one, gain_one
    )
    patch_grad = middle_grad + hidden_from_norm

    head_sums = jnp.sum(head_grad.astype(f32), axis=(0, 2))
    qv_grad = jnp.zeros((2 * width,), f32)
    qv_grad = lax.dynamic_update_slice(qv_grad, head_sums[:HEAD_DIM], (head * HEAD_DIM,))
    qv_grad = lax.dynamic_update_slice(
        qv_grad, head_sums[2 * HEAD_DIM :], (width + head * HEAD_DIM,)
    )
    late = VectorSum(
        (
            gain_one_grad,
            bias_one_grad,
            qv_grad,
            jnp.sum(branch_grad.astype(f32), axis=0),
            gain_two_grad,
            bias_two_grad,
            jnp.sum(inner_grad.astype(f32), axis=0),
            jnp.sum(cot_full, axis=0),
        ),
        scale,
    )
    hops = [tie(piece, gain_one_grad) for piece in hops]
    token = late.core()
    token = late.other_f(token)
    pieces = hops + [swap(piece, "y") for piece in hops]
    pieces += [swap(tie(piece, token), "c") for piece in pieces]
    token = late.near_y(token)
    token = late.near_z(token)
    late.far_z(token)
    planes = lax.rem(z + 4 - jnp.arange(4, dtype=jnp.int32), 4) * 4
    near_places = [planes + 2 * y + c, planes + 2 * (1 - y) + c]
    places = jnp.concatenate(near_places + [place_at + 1 - 2 * c for place_at in near_places])
    qkv_weight_grad = weave(pieces, places)
    late.result()
    (
        ln1_gain_sum, ln1_bias_sum, qv_sum, out_bias_sum,
        ln2_gain_sum, ln2_bias_sum, fc1_bias_sum, fc2_bias_sum,
    ) = late.vectors()
    return (
        block_out.astype(low)[None],
        patch_grad[None],
        ln1_gain_sum,
        ln1_bias_sum,
        qkv_weight_grad,
        qv_sum,
        out_weight_grad,
        out_bias_sum,
        ln2_gain_sum,
        ln2_bias_sum,
        fc1_grad,
        fc1_bias_sum,
        fc2_grad,
        fc2_bias_sum,
    )


def solution(mesh):
    seq, parts = mesh.shape["seq"], mesh.shape["fsdp"]
    fine = Mesh(mesh.devices.reshape(seq // HEADS, HEADS // 4, 2, 2, parts), ("g", "z", "y", "c", "f"))
    rows = P("f", ("g",) + SEQ, None)
    vec, mat = P("f"), P("f", None)
    in_specs = (rows, rows, mat, rows, vec, vec, mat, vec, mat, vec, vec, vec, mat, vec, mat, vec)
    out_specs = (rows, rows, vec, vec, mat, vec, mat, vec, vec, vec, mat, vec, mat, vec)
    return jax.shard_map(body, mesh=fine, in_specs=in_specs, out_specs=out_specs, check_vma=False)
```

```python
import math
from functools import partial

import jax
import jax.numpy as jnp
from jax import lax
from jax.experimental import pallas as pl
from jax.experimental.pallas import tpu as pltpu
from jax.sharding import Mesh, PartitionSpec as P

HEADS = 16
LONG = 2304
NORM_EPS = 1e-06
CHUNKS = (2, 3, 3, 3, 3, 2)
HEAD_DIM = 64
BLOCK = 512
FAR = 1e30
QB = 512
KB = 512
HALF = 256
CALM_SCORE = 60.0
FORWARD_COST = 50_000_000_000
BACKWARD_COST = 75_000_000_000


def rows_dot(a, b):
    return lax.dot_general(a, b, (((1,), (0,)), ((), ())), preferred_element_type=jnp.float32)


def membership(ends_ref, count, first, width):
    place = first + lax.broadcasted_iota(jnp.int32, (16, width), 1)
    row = lax.broadcasted_iota(jnp.int32, (16, width), 0)
    low = jnp.zeros((16, width), jnp.int32)
    high = jnp.zeros((16, width), jnp.int32)
    for i in range(count):
        begin = ends_ref[i - 1] if i > 0 else 0
        low = jnp.where(row == i, begin, low)
        high = jnp.where(row == i, ends_ref[i], high)
    return jnp.where((place >= low) & (place < high), 1.0, 0.0)


def image_span(ends_ref, count, first, last):
    low = jnp.int32(0)
    high = ends_ref[count - 1]
    for i in range(count - 1):
        end = ends_ref[i]
        low = jnp.where(end <= first, end, low)
    for i in range(count - 2, -1, -1):
        end = ends_ref[i]
        high = jnp.where(end > last, end, high)
    return low, high


def over_keys(low, high, step, carry):
    def whole(j, carry):
        return step(pl.ds(pl.multiple_of((low + 2 * j) * HALF, HALF), KB), carry)

    def half(j, carry):
        return step(pl.ds(pl.multiple_of(j * HALF, HALF), HALF), carry)

    pairs = (high - low) // 2
    carry = lax.fori_loop(0, pairs, whole, carry)
    return lax.fori_loop(low + 2 * pairs, high, half, carry)


def split3(x):
    top = x.astype(jnp.bfloat16)
    rest = x - top.astype(jnp.float32)
    mid = rest.astype(jnp.bfloat16)
    low = (rest - mid.astype(jnp.float32)).astype(jnp.bfloat16)
    return [top.astype(jnp.float32), mid.astype(jnp.float32), low.astype(jnp.float32)]


def parts_of(ref):
    return [ref.at[:, i * HEAD_DIM : (i + 1) * HEAD_DIM, :] for i in range(ref.shape[1] // HEAD_DIM)]


def forward_kernel(count, shift, pieces, ends_ref, base_ref, *refs):
    if shift:
        own_ref, window_ref, o_ref, log_ref, qa, kn, va, peak = refs
        q_ref = parts_of(own_ref)[0]
        k_ref, v_ref = parts_of(window_ref)
    else:
        place_ref, *refs = refs
        made, (o_ref, log_ref, own_ref, qa, kn, va, peak) = refs[:pieces], refs[pieces:]
        for i in range(pieces):
            own_ref[place_ref[i]] = made[i][...]
        q_ref, k_ref, v_ref = parts_of(own_ref)
    peak[...] = jnp.zeros_like(peak)
    q_blocks = q_ref.shape[0]
    k_blocks = k_ref.shape[0]
    key_count = k_blocks * BLOCK
    base = base_ref[0]

    @pl.loop(0, k_blocks)
    def _(i):
        at = pl.ds(pl.multiple_of(i * BLOCK, BLOCK), BLOCK)
        away = (membership(ends_ref, count, base - shift + i * BLOCK, BLOCK) - 1.0) * FAR
        keys = k_ref[i].astype(jnp.float32)
        peak[1:2] = jnp.maximum(peak[1:2], jnp.sum(keys * keys, axis=0, keepdims=True))
        both = jnp.concatenate([keys, away], axis=0)
        kn[at, :] = both.T.astype(jnp.bfloat16)
        va[:, at] = jnp.concatenate(
            [v_ref[i].astype(jnp.float32), jnp.ones((16, BLOCK), jnp.float32)], axis=0
        ).astype(jnp.bfloat16)

    @pl.loop(0, q_blocks)
    def _(i):
        at = pl.ds(pl.multiple_of(i * BLOCK, BLOCK), BLOCK)
        inside = membership(ends_ref, count, base + i * BLOCK, BLOCK)
        asked = q_ref[i].astype(jnp.float32)
        peak[0:1] = jnp.maximum(peak[0:1], jnp.sum(asked * asked, axis=0, keepdims=True))
        qa[:, at] = jnp.concatenate(
            [asked * (HEAD_DIM ** -0.5), inside], axis=0
        ).astype(jnp.bfloat16)

    per = BLOCK // QB
    calm = CALM_SCORE * HEAD_DIM ** 0.5
    peaks = [jnp.max(peak[i : i + 1]) for i in range(2)]

    def span(i):
        first = base + i * QB
        low, high = image_span(ends_ref, count, first, first + QB - 1)
        low = jnp.maximum(low - base + shift, 0) // HALF
        return low, jnp.minimum(high - base + shift + HALF - 1, key_count) // HALF

    def finish(i, top, acc):
        total = acc[HEAD_DIM : HEAD_DIM + 1]
        o_ref[i // per, :, pl.ds(pl.multiple_of((i % per) * QB, QB), QB)] = (
            acc[:HEAD_DIM] / total
        ).astype(jnp.bfloat16)
        log_ref[:, pl.ds(pl.multiple_of(i * QB, QB), QB)] = top + jnp.log(total)

    small = peaks[0] * peaks[1] <= calm * calm

    @pl.when(small)
    def _():
        @pl.loop(0, q_blocks * per)
        def _(i):
            q_part = qa[:, pl.ds(pl.multiple_of(i * QB, QB), QB)]

            def step(at, acc):
                weights = jnp.exp(rows_dot(kn[at, :], q_part)).astype(jnp.bfloat16)
                return acc + rows_dot(va[:, at], weights)

            finish(i, 0.0, over_keys(*span(i), step, jnp.zeros((HEAD_DIM + 16, QB), jnp.float32)))

    @pl.when(jnp.logical_not(small))
    def _():
        @pl.loop(0, q_blocks * per)
        def _(i):
            q_part = qa[:, pl.ds(pl.multiple_of(i * QB, QB), QB)]

            def step(at, carry):
                top, acc = carry
                scores = rows_dot(kn[at, :], q_part)
                new_top = jnp.maximum(top, jnp.max(scores, axis=0, keepdims=True))
                weights = jnp.exp(scores - new_top).astype(jnp.bfloat16)
                acc = acc * jnp.exp(top - new_top) + rows_dot(va[:, at], weights)
                return new_top, acc

            start = (
                jnp.full((1, QB), -3e38, jnp.float32),
                jnp.zeros((HEAD_DIM + 16, QB), jnp.float32),
            )
            finish(i, *over_keys(*span(i), step, start))


def backward_kernel(count, shift, first_block, chunk, last, ends_ref, base_ref, own_ref, *refs):
    q_ref, k_ref, v_ref = parts_of(own_ref)
    if shift:
        k_ref, v_ref = parts_of(refs[0])
        refs = refs[1:]
    o_ref, do_ref, log_ref, *refs = refs
    if first_block > 0:
        sums_in, _, *refs = refs
    grad_ref, *refs = refs
    sums_out = None
    if shift:
        window_ref, *refs = refs
    if not last:
        sums_out, *refs = refs
    qa, da, kn, vn, qn, dn, ks, sums, dq_part, sums_sem, dq_sem, *refs = refs
    k_blocks = k_ref.shape[0]
    key_count = k_blocks * BLOCK
    base = base_ref[0]
    scale = HEAD_DIM ** -0.5
    start = base + first_block * BLOCK
    low, high = image_span(ends_ref, count, start, start + chunk * BLOCK - 1)
    low = jnp.maximum(low - base + shift, 0) // BLOCK
    high = jnp.minimum(high - base + shift + BLOCK - 1, key_count) // BLOCK
    held_low, held_high = (0, k_blocks) if last or first_block == 0 else (low, high)

    def block_at(i):
        return pl.ds(pl.multiple_of(i * BLOCK, BLOCK), BLOCK)

    if first_block > 0:

        @pl.loop(held_low, held_high)
        def _(i):
            pltpu.make_async_copy(sums_in.at[block_at(i)], sums.at[block_at(i)], sums_sem.at[i]).start()

    else:
        sums[...] = jnp.zeros_like(sums)

    @pl.loop(low, high)
    def _(i):
        at = block_at(i)
        away = (membership(ends_ref, count, base - shift + i * BLOCK, BLOCK) - 1.0) * FAR
        ones = jnp.ones((16, BLOCK), jnp.float32)
        keys = k_ref[i].astype(jnp.float32)
        kn[at, :] = jnp.concatenate([keys, away, ones], axis=0).T.astype(jnp.bfloat16)
        vn[at, :] = jnp.concatenate([v_ref[i].astype(jnp.float32), ones], axis=0).T.astype(jnp.bfloat16)
        ks[:, at] = (keys * scale).astype(jnp.bfloat16)

    @pl.loop(0, chunk)
    def _(i):
        at = block_at(i)
        block = first_block + i
        inside = membership(ends_ref, count, base + block * BLOCK, BLOCK)
        pad = jnp.zeros((13, BLOCK), jnp.float32)
        scaled = q_ref[block].astype(jnp.float32) * scale
        qn[at, :] = scaled.T.astype(jnp.bfloat16)
        qa[:, at] = jnp.concatenate(
            [scaled, inside] + split3(-log_ref[:, block_at(block)]) + [pad], axis=0
        ).astype(jnp.bfloat16)
        grads = do_ref[block].astype(jnp.float32)
        row_dot = jnp.sum(grads * o_ref[block].astype(jnp.float32), axis=0, keepdims=True)
        dn[at, :] = grads.T.astype(jnp.bfloat16)
        da[:, at] = jnp.concatenate([grads] + split3(-row_dot) + [pad], axis=0).astype(jnp.bfloat16)

    if first_block > 0:

        @pl.loop(held_low, held_high)
        def _(i):
            pltpu.make_async_copy(sums_in.at[block_at(i)], sums.at[block_at(i)], sums_sem.at[i]).wait()

    @pl.loop(0, chunk)
    def _(i):
        q_at = block_at(i)
        q_part = qa[:, q_at]
        d_part = da[:, q_at]
        q_rows = qn[q_at, :]
        d_rows = dn[q_at, :]
        first = start + i * BLOCK
        key_low, key_high = image_span(ends_ref, count, first, first + BLOCK - 1)
        key_low = jnp.maximum(key_low - base + shift, 0) // HALF
        key_high = jnp.minimum(key_high - base + shift + HALF - 1, key_count) // HALF

        def step(at, dq):
            probs = jnp.exp(rows_dot(kn[at, :], q_part))
            score_grad = (probs * rows_dot(vn[at, :], d_part)).astype(jnp.bfloat16)
            sums[at, 0:HEAD_DIM] += rows_dot(score_grad, q_rows)
            sums[at, HEAD_DIM : 2 * HEAD_DIM] += rows_dot(probs.astype(jnp.bfloat16), d_rows)
            return dq + rows_dot(ks[:, at], score_grad)

        dq = over_keys(key_low, key_high, step, jnp.zeros((HEAD_DIM, BLOCK), jnp.float32))
        dq_part[i] = dq.astype(jnp.bfloat16)

    def query_copy(i):
        return pltpu.make_async_copy(
            dq_part.at[i], grad_ref.at[first_block + i, 0:HEAD_DIM], dq_sem.at[i]
        )

    for i in range(chunk):
        query_copy(i).start()
    if not last:

        @pl.loop(held_low, held_high)
        def _(i):
            pltpu.make_async_copy(sums.at[block_at(i)], sums_out.at[block_at(i)], sums_sem.at[i]).start()

        @pl.loop(held_low, held_high)
        def _(i):
            pltpu.make_async_copy(sums.at[block_at(i)], sums_out.at[block_at(i)], sums_sem.at[i]).wait()

    elif shift:

        @pl.loop(0, k_blocks)
        def _(i):
            window_ref[i] = sums[block_at(i), :].T

    else:
        kv_part, kv_sem = refs

        def key_copy(i):
            return pltpu.make_async_copy(
                kv_part.at[i], grad_ref.at[i, HEAD_DIM : 3 * HEAD_DIM], kv_sem.at[i]
            )

        @pl.loop(0, k_blocks)
        def _(i):
            kv_part[i] = sums[block_at(i), :].T.astype(jnp.bfloat16)
            key_copy(i).start()

        @pl.loop(0, k_blocks)
        def _(i):
            key_copy(i).wait()

    for i in range(chunk):
        query_copy(i).wait()


def vmem_spec():
    return pl.BlockSpec(memory_space=pltpu.VMEM)


def smem_spec():
    return pl.BlockSpec(memory_space=pltpu.SMEM)


def attention_forward(ends, base, made, places, window, shift):
    blocks = made[0].shape[0] if shift else len(made)
    tokens, keys = blocks * BLOCK, blocks * BLOCK + 2 * shift
    low = jnp.bfloat16
    out_shape = [
        jax.ShapeDtypeStruct((blocks, HEAD_DIM, BLOCK), low),
        jax.ShapeDtypeStruct((1, tokens), jnp.float32),
    ]
    if shift:
        arrays, in_specs = [*made, window], [smem_spec()] * 2 + [vmem_spec()] * 2
    else:
        arrays, in_specs = [places, *made], [smem_spec()] * 3 + [vmem_spec()] * blocks
        out_shape.append(jax.ShapeDtypeStruct((blocks, 3 * HEAD_DIM, BLOCK), low))
    return pl.pallas_call(
        partial(forward_kernel, ends.shape[0], shift, blocks),
        out_shape=out_shape,
        in_specs=in_specs,
        out_specs=[vmem_spec()] * len(out_shape),
        scratch_shapes=[
            pltpu.VMEM((HEAD_DIM + 16, tokens), low),
            pltpu.VMEM((keys, HEAD_DIM + 16), low),
            pltpu.VMEM((HEAD_DIM + 16, keys), low),
            pltpu.VMEM((8, BLOCK), jnp.float32),
        ],
        compiler_params=pltpu.CompilerParams(vmem_limit_bytes=48 * 1024 * 1024),
        cost_estimate=pl.CostEstimate(
            flops=FORWARD_COST, bytes_accessed=tokens * 512, transcendentals=0
        ),
    )(ends, base, *arrays)


def attention_backward(ends, base, own, window, o, do, log, shift, first_block, chunk, carried):
    blocks = own.shape[0]
    tokens, keys = chunk * BLOCK, blocks * BLOCK + 2 * shift
    last = first_block + chunk == blocks
    low, f32 = jnp.bfloat16, jnp.float32
    arrays = [own] + ([window] if shift else []) + [o, do, log]
    in_specs = [smem_spec(), smem_spec()] + [vmem_spec()] * len(arrays)
    out_shape = [jax.ShapeDtypeStruct((blocks, HEAD_DIM if shift else 3 * HEAD_DIM, BLOCK), low)]
    out_specs = [any_spec()]
    aliases = {}
    if carried is not None:
        place_at = 2 + len(arrays)
        arrays += list(carried)
        in_specs += [any_spec(), any_spec()]
        aliases = {place_at + 1: 0}
        if not last:
            aliases[place_at] = 1
    if shift:
        out_shape.append(jax.ShapeDtypeStruct((keys // BLOCK, 2 * HEAD_DIM, BLOCK), f32))
        out_specs.append(vmem_spec())
    if not last:
        out_shape.append(jax.ShapeDtypeStruct((keys, 2 * HEAD_DIM), f32))
        out_specs.append(any_spec())
    scratch = [
        pltpu.VMEM((HEAD_DIM + 32, tokens), low),
        pltpu.VMEM((HEAD_DIM + 16, tokens), low),
        pltpu.VMEM((keys, HEAD_DIM + 32), low),
        pltpu.VMEM((keys, HEAD_DIM + 16), low),
        pltpu.VMEM((tokens, HEAD_DIM), low),
        pltpu.VMEM((tokens, HEAD_DIM), low),
        pltpu.VMEM((HEAD_DIM, keys), low),
        pltpu.VMEM((keys, 2 * HEAD_DIM), f32),
        pltpu.VMEM((chunk, HEAD_DIM, BLOCK), low),
        pltpu.SemaphoreType.DMA((keys // BLOCK,)),
        pltpu.SemaphoreType.DMA((chunk,)),
    ]
    if last and not shift:
        scratch += [
            pltpu.VMEM((blocks, 2 * HEAD_DIM, BLOCK), low),
            pltpu.SemaphoreType.DMA((blocks,)),
        ]
    return pl.pallas_call(
        partial(backward_kernel, ends.shape[0], shift, first_block, chunk, last),
        out_shape=out_shape,
        in_specs=in_specs,
        out_specs=out_specs,
        scratch_shapes=scratch,
        input_output_aliases=aliases,
        compiler_params=pltpu.CompilerParams(vmem_limit_bytes=50 * 1024 * 1024),
        cost_estimate=pl.CostEstimate(flops=BACKWARD_COST * chunk // blocks, bytes_accessed=tokens * 1024, transcendentals=0),
    )(ends, base, *arrays)


def any_spec():
    return pl.BlockSpec(memory_space=pl.ANY)


def block_rows(rows, cols):
    while rows * cols > 512 * 1024 and rows % 16 == 0:
        rows //= 2
    return rows


def take_kernel(at_ref, in_ref, out_ref):
    out_ref[...] = in_ref[...]


def take(x, index, count):
    rows, cols = x.shape[0] // count, x.shape[1]
    size = block_rows(rows, cols)
    steps = rows // size
    return pl.pallas_call(
        take_kernel,
        out_shape=jax.ShapeDtypeStruct((rows, cols), x.dtype),
        grid_spec=pltpu.PrefetchScalarGridSpec(
            num_scalar_prefetch=1,
            grid=(steps,),
            in_specs=[pl.BlockSpec((size, cols), lambda j, at_ref: (at_ref[0] * steps + j, 0))],
            out_specs=pl.BlockSpec((size, cols), lambda j, at_ref: (j, 0)),
        ),
        cost_estimate=pl.CostEstimate(flops=0, bytes_accessed=2 * rows * cols * x.dtype.itemsize, transcendentals=0),
    )(index.astype(jnp.int32).reshape(1), x)


def place_kernel(owner, row_ref, col_ref, *refs):
    out_ref = refs[-1]
    for i, piece in enumerate(owner):

        @pl.when(pl.program_id(0) == i)
        def _(piece=piece):
            out_ref[...] = refs[piece][...].astype(out_ref.dtype)


def place(pieces, row_at, col_at, dtype, rows, shape, cols=None, block=0):
    cols = cols or pieces[0].shape[1]
    owner = [n for n, piece in enumerate(pieces) for _ in range(piece.shape[0] // rows)]
    count = len(owner)
    size = block_rows(rows, cols)
    steps = rows // size

    def piece_map(piece):
        turns = [i for i in range(count) if owner[i] == piece]
        first, last = turns[0], turns[-1]

        def index(s, j, row_ref, col_ref):
            inside = j + (s - first) * steps
            end = (last - first + 1) * steps - 1
            return (jnp.where(s < first, 0, jnp.where(s > last, end, inside)), block)

        return index

    return pl.pallas_call(
        partial(place_kernel, owner),
        out_shape=jax.ShapeDtypeStruct(shape, dtype),
        grid_spec=pltpu.PrefetchScalarGridSpec(
            num_scalar_prefetch=2,
            grid=(count, steps),
            in_specs=[pl.BlockSpec((size, cols), piece_map(i)) for i in range(len(pieces))],
            out_specs=pl.BlockSpec(
                (size, cols), lambda s, j, row_ref, col_ref: (row_ref[s] * steps + j, col_ref[s])
            ),
        ),
        cost_estimate=pl.CostEstimate(
            flops=0,
            bytes_accessed=count * rows * cols * (2 + jnp.dtype(dtype).itemsize),
            transcendentals=0,
        ),
    )(row_at, col_at, *pieces)


def plane_columns_kernel(plane_ref, q_ref, k_ref, v_ref, out_ref):
    for part, ref in enumerate((q_ref, k_ref, v_ref)):
        cols = ref[...].astype(jnp.float32).T
        for j in range(4):
            at = (3 * j + part) * HEAD_DIM
            out_ref[at : at + HEAD_DIM] = cols[j * HEAD_DIM : (j + 1) * HEAD_DIM].astype(out_ref.dtype)


def plane_columns(w, plane):
    rows = w.shape[0]

    def spec(part):
        return pl.BlockSpec((rows, 4 * HEAD_DIM), lambda i, plane_ref: (0, part * (HEADS // 4) + plane_ref[0]))

    return pl.pallas_call(
        plane_columns_kernel,
        out_shape=jax.ShapeDtypeStruct((12 * HEAD_DIM, rows), w.dtype),
        grid_spec=pltpu.PrefetchScalarGridSpec(
            num_scalar_prefetch=1,
            grid=(1,),
            in_specs=[spec(part) for part in range(3)],
            out_specs=pl.BlockSpec((12 * HEAD_DIM, rows), lambda i, plane_ref: (0, 0)),
        ),
    )(plane.astype(jnp.int32).reshape(1), w, w, w)


def project_kernel(head_ref, w_ref, bias_ref, block_ref, *out_refs):
    size = w_ref.shape[2]
    rows = 3 * HEAD_DIM
    for i, out_ref in enumerate(out_refs):
        at = pl.ds(pl.multiple_of(head_ref[i] * rows, HEAD_DIM), rows)
        total = bias_ref[at, :]
        for f in range(w_ref.shape[0]):
            total += lax.dot_general(
                w_ref[f, at, :], block_ref[:, f * size : (f + 1) * size], (((1,), (1,)), ((), ())),
                preferred_element_type=jnp.float32,
            )
        out_ref[...] = total.astype(jnp.bfloat16)


def project(heads, w, bias, block):
    rows, width = block.shape
    count = heads.shape[0]
    shape = jax.ShapeDtypeStruct((3 * HEAD_DIM, rows), jnp.bfloat16)
    return pl.pallas_call(
        project_kernel,
        out_shape=[shape] * count,
        in_specs=[smem_spec()] + [vmem_spec()] * 3,
        out_specs=[vmem_spec()] * count,
        compiler_params=pltpu.CompilerParams(vmem_limit_bytes=24 * 1024 * 1024),
        cost_estimate=pl.CostEstimate(
            flops=6 * count * rows * width * 3 * HEAD_DIM, bytes_accessed=rows * width * 2, transcendentals=0
        ),
    )(heads, w, bias, block)


def assemble_kernel(count, place_ref, *refs):
    pieces, out_ref, sem = refs[:count], refs[count], refs[count + 1]

    def copy(i):
        return pltpu.make_async_copy(pieces[i], out_ref.at[place_ref[i]], sem.at[i])

    for i in range(count):
        copy(i).start()
    for i in range(count):
        copy(i).wait()


def assemble(pieces, places):
    count = len(pieces)
    return pl.pallas_call(
        partial(assemble_kernel, count),
        out_shape=jax.ShapeDtypeStruct((count,) + pieces[0].shape, pieces[0].dtype),
        in_specs=[smem_spec()] + [vmem_spec()] * count,
        out_specs=any_spec(),
        scratch_shapes=[pltpu.SemaphoreType.DMA((count,))],
        compiler_params=pltpu.CompilerParams(vmem_limit_bytes=16 * 1024 * 1024),
        cost_estimate=pl.CostEstimate(
            flops=0, bytes_accessed=4 * count * pieces[0].size, transcendentals=0
        ),
    )(places, *pieces)


SLOTS = 4


def head_weight_kernel(count, place_ref, grad_ref, *refs):
    blocks, (out_ref, held, sem) = refs[:count], refs[count:]

    def copy(b):
        return pltpu.make_async_copy(blocks[b], held.at[b % SLOTS], sem.at[b % SLOTS])

    for b in range(SLOTS - 1):
        copy(b).start()
    out_ref[...] = jnp.zeros_like(out_ref)

    @pl.loop(0, count)
    def _(i):
        slot = lax.rem(i, SLOTS)
        pltpu.make_async_copy(blocks[0], held.at[slot], sem.at[slot]).wait()
        for b in range(SLOTS - 1, count):

            @pl.when(i + SLOTS - 1 == b)
            def _(b=b):
                copy(b).start()

        out_ref[...] += rows_dot(grad_ref[place_ref[i]], held[slot])


def head_weight(places, grad, blocks):
    count = len(blocks)
    rows, width = blocks[0].shape
    cols = grad.shape[1]
    return pl.pallas_call(
        partial(head_weight_kernel, count),
        out_shape=jax.ShapeDtypeStruct((cols, width), jnp.float32),
        in_specs=[smem_spec(), vmem_spec()] + [any_spec()] * count,
        out_specs=vmem_spec(),
        scratch_shapes=[
            pltpu.VMEM((SLOTS, rows, width), jnp.bfloat16),
            pltpu.SemaphoreType.DMA((SLOTS,)),
        ],
        compiler_params=pltpu.CompilerParams(vmem_limit_bytes=24 * 1024 * 1024),
        cost_estimate=pl.CostEstimate(flops=4 * count * rows * width * cols, bytes_accessed=count * rows * width * 2, transcendentals=0),
    )(places, grad, *blocks)


def weave_kernel(count, at_ref, *refs):
    pieces, (out_ref, held) = refs[:count], refs[count:]
    for i in range(count):
        held[at_ref[i]] = pieces[i][...]
    for part in range(3):
        for pair in range(count // 2):
            rows = slice(part * HEAD_DIM, (part + 1) * HEAD_DIM)
            both = jnp.concatenate([held[2 * pair, rows], held[2 * pair + 1, rows]], axis=0)
            at = (part * count + 2 * pair) * HEAD_DIM
            out_ref[:, at : at + 2 * HEAD_DIM] = both.astype(jnp.float32).T


def weave(pieces, places):
    count = len(pieces)
    cols, rows = pieces[0].shape
    size = 128
    return pl.pallas_call(
        partial(weave_kernel, count),
        out_shape=jax.ShapeDtypeStruct((rows, count * cols), jnp.float32),
        grid_spec=pltpu.PrefetchScalarGridSpec(
            num_scalar_prefetch=1,
            grid=(rows // size,),
            in_specs=[pl.BlockSpec((cols, size), lambda i, at_ref: (0, i))] * count,
            out_specs=pl.BlockSpec((size, count * cols), lambda i, at_ref: (i, 0)),
            scratch_shapes=[pltpu.VMEM((count, cols, size), pieces[0].dtype)],
        ),
        cost_estimate=pl.CostEstimate(
            flops=0, bytes_accessed=6 * count * cols * rows, transcendentals=0
        ),
    )(places, *pieces)


SEQ = ("z", "y", "c")
SWAP = ((0, 1), (1, 0))


def norm_forward(hidden, gain_vec, offset_vec):
    centre = hidden - jnp.mean(hidden, axis=-1, keepdims=True)
    spread = jnp.mean(centre * centre, axis=-1, keepdims=True)
    inv_std = lax.rsqrt(spread + NORM_EPS)
    scaled = centre * inv_std
    return (scaled * gain_vec + offset_vec, scaled, inv_std)


def norm_backward(grad_out, scaled, inv_std, gain_vec):
    gain_grad = jnp.sum(grad_out * scaled, axis=0)
    offset_grad = jnp.sum(grad_out, axis=0)
    grad_scaled = grad_out * gain_vec
    grad_in = inv_std * (
        grad_scaled
        - jnp.mean(grad_scaled, axis=-1, keepdims=True)
        - scaled * jnp.mean(grad_scaled * scaled, axis=-1, keepdims=True)
    )
    return (gain_grad, offset_grad, grad_in)


def dot(a, b, a_dim, b_dim):
    return lax.dot_general(
        a, b, (((a_dim,), (b_dim,)), ((), ())), preferred_element_type=jnp.float32
    )


def tie(x, *others):
    others = [other for other in others if other is not None]
    return lax.optimization_barrier((x, *others))[0] if others else x


def linear(start, first, a, second, b):
    start, first, second = (jnp.array(x, jnp.int32) for x in (start, first, second))
    return start + first * a + second * b


def pick(x, i, axis=0):
    return lax.dynamic_index_in_dim(x, i, axis, keepdims=False)


def swap(x, axis):
    return lax.ppermute(x, axis, SWAP)


def in_order(own, other, position):
    return jnp.where(position == 0, jnp.stack([own, other]), jnp.stack([other, own]))


def fetch_fsdp(shard, pieces, *others):
    if lax.axis_size("f") != 2:
        return [], [lax.all_gather(shard, "f", axis=0, tiled=True)]
    first = lax.axis_index("c") * pieces
    shard = tie(shard, *others)
    taken = [take(shard, first + i, 2 * pieces) for i in range(pieces)]
    return taken, [swap(part, "f") for part in taken]


def share_cores(fetched, *others):
    if lax.axis_size("f") != 2:
        return fetched
    return fetched + [swap(tie(piece, *others), "c") for piece in fetched]


def join_fsdp(shard, pieces, *others):
    if lax.axis_size("f") != 2:
        return pieces[0]
    core, here = lax.axis_index("c"), lax.axis_index("f")
    count = len(pieces) // 2
    step = range(count)
    at = linear(
        (*range(2 * count), *(2 * count + i for i in step), *(3 * count + i for i in step)),
        (2 * count,) * (2 * count) + (-2 * count,) * (2 * count),
        here,
        (0,) * (2 * count) + (count,) * count + (-count,) * count,
        core,
    )
    rows, cols = shard.shape
    return place(
        [tie(shard, *others), *pieces], at, jnp.zeros_like(at), shard.dtype, rows // (2 * count), (2 * rows, cols)
    )


def join_small(shard):
    if lax.axis_size("f") != 2:
        return lax.all_gather(shard, "f", axis=0, tiled=False)
    return in_order(shard, swap(shard, "f"), lax.axis_index("f"))


def halve(x, axis, pairs=SWAP, here=None):
    here = lax.axis_index(axis) if here is None else here
    got = lax.ppermute(pick(x, 1 - here), axis, pairs)
    return pick(x, here).astype(jnp.float32) + got.astype(jnp.float32)


def plane_pairs(bit):
    return [(i, i ^ bit) for i in range(4)]


class WeightSum:
    def __init__(self, terms, scale):
        self.terms, self.scale = terms, scale
        self.widths = [right.shape[1] // 2 for _, right, _ in terms]
        self.cols = sum(self.widths)
        self.rows = terms[0][0].shape[1 - terms[0][2]] // lax.axis_size("f")

    def after(self, others):
        self.terms = [(left, tie(right, *others), dim) for left, right, dim in self.terms]

    def term(self, n, c, f, half=None):
        left, right, dim = self.terms[n]
        rows, start = self.rows, f * self.rows
        if half is not None:
            rows //= 2
            start = start + half * rows
        left = lax.dynamic_slice_in_dim(left, start, rows, 1 - dim)
        right = lax.dynamic_slice_in_dim(right, c * self.widths[n], self.widths[n], 1)
        return dot(left, right, dim, 0)

    def joined(self, parts):
        parts = [part.astype(jnp.bfloat16) for part in parts]
        return parts[0] if len(parts) == 1 else jnp.concatenate(parts, axis=1)

    def half_of(self, x, half):
        rows = x.shape[0] // 2
        return lax.dynamic_slice_in_dim(x, half * rows, rows, 0).astype(jnp.float32)

    def other_core(self, *others):
        self.after(others)
        core, parts, here = lax.axis_index("c"), lax.axis_size("f"), lax.axis_index("f")
        order = [1 - here, here] if parts == 2 else range(parts)
        self.got = []
        for f in order:
            sent = [self.term(n, 1 - core, f).astype(jnp.bfloat16) for n in range(len(self.terms))]
            self.got.append([swap(part, "c") for part in sent])
        return sent[-1]

    def other_f(self, *others):
        self.after(others)
        core, parts, here = lax.axis_index("c"), lax.axis_size("f"), lax.axis_index("f")
        y, count = lax.axis_index("y"), range(len(self.terms))
        if parts == 2:
            self.far = []
            for half in (1 - y, y):
                sent = self.joined(
                    [self.term(n, core, 1 - here, half) + self.half_of(self.got[0][n], half) for n in count]
                )
                self.far.append(swap(sent, "f"))
                self.after([sent])
            return sent
        total = [
            self.joined([self.term(n, core, f) + self.got[f][n].astype(jnp.float32) for n in count])
            for f in range(parts)
        ]
        self.far = []
        self.total = lax.psum_scatter(jnp.stack(total), "f", scatter_dimension=0, tiled=False)
        return self.total

    def here_half(self, k, half):
        core, parts, here = lax.axis_index("c"), lax.axis_size("f"), lax.axis_index("f")
        if parts != 2:
            return [self.half_of(self.total, half)]
        x, at = [], 0
        for n, width in enumerate(self.widths):
            total = self.term(n, core, here, half) + self.half_of(self.got[1][n], half)
            x.append(total + self.far[k][:, at : at + width].astype(jnp.float32))
            at += width
        return x

    def near_y(self, *others):
        self.after(others)
        sent = self.joined(self.here_half(0, 1 - lax.axis_index("y")))
        self.coming = lax.ppermute(sent, "y", SWAP)
        return sent

    def near_z(self, *others):
        self.coming = tie(self.coming, *others)
        self.after(others)
        x, at = [], 0
        for part in self.here_half(1, lax.axis_index("y")):
            width = part.shape[1]
            x.append(part + self.coming[:, at : at + width].astype(jnp.float32))
            at += width
        x = self.joined(x).reshape(2, -1, self.cols)
        low_z = lax.rem(lax.axis_index("z"), 2)
        sent = pick(x, 1 - low_z)
        self.kept, self.coming = pick(x, low_z), lax.ppermute(sent, "z", plane_pairs(1))
        return sent

    def added(self, x, others):
        return x.astype(jnp.float32) + tie(self.coming, *others).astype(jnp.float32)

    def far_z(self, *others):
        self.x = self.added(self.kept, others).astype(jnp.bfloat16)
        self.coming = lax.ppermute(self.x, "z", plane_pairs(2))
        return self.x

    def back_near_z(self, *others):
        x = self.added(self.x, others)
        if lax.axis_size("g") > 1:
            x = lax.psum(x, "g")
        self.x = (x * self.scale).astype(jnp.bfloat16)
        self.coming = lax.ppermute(self.x, "z", plane_pairs(1))
        return self.x

    def back_y(self, *others):
        coming = tie(self.coming, *others)
        x = in_order(self.x, coming, lax.rem(lax.axis_index("z"), 2)).reshape(-1, self.cols)
        self.near = lax.ppermute(x, "y", SWAP)
        self.x, self.across = x, swap(x, "c")
        return x

    def results(self, *others):
        y, c = lax.axis_index("y"), lax.axis_index("c")
        near = tie(self.near, *others)
        pieces = [self.x, near, self.across, swap(near, "c")]
        row_at = linear((0, 1, 0, 1), (1, -1, 1, -1), y, (0, 0, 0, 0), c)
        col_at = linear((0, 0, 1, 1), (0, 0, 0, 0), y, (1, 1, -1, -1), c)
        rows, at, results = pieces[0].shape[0], 0, []
        for width in self.widths:
            results.append(
                place(
                    pieces, row_at, col_at, jnp.float32, rows, (2 * rows, 2 * width), width, at // width
                )
            )
            at += width
        return results


class VectorSum:
    def __init__(self, vectors, scale):
        self.sizes = [vec.shape[0] // lax.axis_size("f") for vec in vectors]
        self.x = jnp.concatenate([vec.reshape(lax.axis_size("f"), -1) for vec in vectors], axis=1) * scale

    def core(self, *others):
        self.x = tie(self.x, *others)
        self.coming = swap(self.x, "c")
        return self.x

    def other_f(self, *others):
        x = self.x + tie(self.coming, *others)
        if lax.axis_size("f") == 2:
            here = lax.axis_index("f")
            self.x, sent = pick(x, here), pick(x, 1 - here)
            self.coming = swap(sent, "f")
            return sent
        self.x = lax.psum_scatter(x, "f", scatter_dimension=0, tiled=False)
        self.coming = jnp.zeros_like(self.x)
        return self.x

    def hop(self, axis, pairs, others):
        self.x = self.x + tie(self.coming, *others)
        self.coming = lax.ppermute(self.x, axis, pairs)
        return self.x

    def near_y(self, *others):
        return self.hop("y", SWAP, others)

    def near_z(self, *others):
        return self.hop("z", plane_pairs(1), others)

    def far_z(self, *others):
        return self.hop("z", plane_pairs(2), others)

    def result(self, *others):
        self.total = self.x + tie(self.coming, *others)
        if lax.axis_size("g") > 1:
            self.total = lax.psum(self.total, "g")
        return self.total

    def vectors(self):
        at = 0
        for size in self.sizes:
            yield self.total[at : at + size]
            at += size


def arrivals(count):
    table = []
    for z in range(count):
        hops = []
        for t in range(1, count):
            if z - t >= 0:
                hops.append(("up", t))
            if z + t < count:
                hops.append(("down", t))
        table.append(hops)
    return table


def gather_planes(x, use, beside, later):
    z = lax.axis_index("z")
    count = lax.axis_size("z")
    table = arrivals(count)
    up, down = x, x
    hops = {}
    blocks, planes, used = [x], [z], []
    for t in range(1, count):
        up = lax.ppermute(up, "z", [(i, i + 1) for i in range(t - 1, count - 1)])
        down = lax.ppermute(down, "z", [(i, i - 1) for i in range(1, count - t + 1)])
        made = use(blocks[-1])
        before = used.pop() if used else []
        up, down, before, made[0], extra, _ = lax.optimization_barrier(
            (up, down, before, made[0], later[t - 1](blocks), beside[t - 1])
        )
        later[t - 1](blocks, extra)
        used += [before] * (t > 1) + [made]
        hops["up", t], hops["down", t] = up, down
        names = sorted({table[i][t - 1] for i in range(count)})
        block, plane = None, z
        for name in names:
            here = [i for i in range(count) if table[i][t - 1] == name]
            chosen = (z >= here[0]) & (z <= here[-1])
            block = hops[name] if block is None else jnp.where(chosen, hops[name], block)
            plane = jnp.where(chosen, z + (-name[1] if name[0] == "up" else name[1]), plane)
        blocks.append(block)
        planes.append(plane)
    used.append(use(blocks[-1]))
    return blocks, planes, used


def body(
    patches, pos_embed, lengths, out_grad,
    ln1_gain, ln1_bias, w_qkv, b_qv, w_out, b_out,
    ln2_gain, ln2_bias, w_fc1, b_fc1, w_fc2, b_fc2,
):
    f32, low = jnp.float32, jnp.bfloat16
    rows, width = patches.shape[1:]
    groups, parts = lax.axis_size("g"), lax.axis_size("f")
    head = lax.axis_index(SEQ)
    group = lax.axis_index("g")
    shard_index = lax.axis_index("f")
    scale = 1.0 / (parts * math.sqrt(rows * HEADS * groups))

    gain_one, bias_one, qv_bias = (
        join_small(vec).reshape(-1).astype(f32) for vec in (ln1_gain, ln1_bias, b_qv)
    )
    hidden = patches[0].astype(f32) + pos_embed[0].astype(f32)
    normed_pre, scaled_one, inv_one = norm_forward(hidden, gain_one, bias_one)
    normed = normed_pre.astype(low)

    shard_rows = w_qkv.shape[0]
    z, y, c = (lax.axis_index(axis) for axis in SEQ)
    place_in_plane = 2 * y + c
    plane_weights = join_small(plane_columns(tie(w_qkv, gain_one, bias_one, qv_bias), z)).reshape(parts, 12 * HEAD_DIM, shard_rows)
    q_bias, v_bias = (
        lax.dynamic_slice_in_dim(qv_bias, at + z * 4 * HEAD_DIM, 4 * HEAD_DIM).reshape(4, HEAD_DIM)
        for at in (0, width)
    )
    plane_bias = jnp.concatenate([q_bias, jnp.zeros((4, HEAD_DIM), f32), v_bias], axis=1).reshape(-1, 1)
    others = jnp.array([0, 1, 2, 3], jnp.int32)
    heads_made = others ^ place_in_plane

    def heads_of(block):
        own, core, near, far = project(heads_made, plane_weights, plane_bias, block)
        return [
            own, swap(core, "c"), swap(near, "y"),
            lax.ppermute(far, ("y", "c"), [(i, 3 - i) for i in range(4)]),
        ]

    out_taken, out_part = fetch_fsdp(w_out, 1, normed)
    fc1_taken, fc1_part = fetch_fsdp(w_fc1, 2, normed)
    fc2_taken, fc2_part = fetch_fsdp(w_fc2, 2, normed)
    qkv_taken, qkv_part = fetch_fsdp(w_qkv, 2, normed)
    out_full = join_fsdp(w_out, share_cores(out_part))
    beside = [
        out_taken + fc1_taken + fc2_taken + qkv_taken, out_part, fc1_part[:1] + [out_full],
    ]
    near_blocks = []

    def swap_later(first):
        def step(blocks, done=None):
            if done is None:
                return [swap(blocks[first], "y")] if first is not None else []
            near_blocks.extend(done)

        return step

    later = [swap_later(None), swap_later(0), swap_later(1)]
    blocks, planes, made = gather_planes(normed, heads_of, beside, later)
    blocks_at = jnp.concatenate([plane * 4 + heads_made for plane in planes])
    made = [piece for round_made in made for piece in round_made]
    if groups > 1:
        qkv = assemble(made, blocks_at)
    ends = jnp.cumsum(lengths[0]).astype(jnp.int32)
    base = (group * (rows * HEADS)).astype(jnp.int32).reshape(1)
    shift, window = 0, None
    up = [(i, i + 1) for i in range(groups - 1)]
    down = [(i + 1, i) for i in range(groups - 1)]
    if groups > 1:
        margin = -(-LONG // rows)
        shift = margin * rows
        both = qkv[:, HEAD_DIM:]
        before = lax.ppermute(both[HEADS - margin :], "g", up)
        after = lax.ppermute(both[:margin], "g", down)
        window = jnp.concatenate([before, both, after], axis=0)
    if groups > 1:
        attended, log_total = attention_forward(ends, base, [qkv], None, window, shift)
    else:
        attended, log_total, qkv = attention_forward(ends, base, made, blocks_at, None, 0)
    attended, near_last = lax.optimization_barrier((attended, swap(blocks[2], "y")))
    near_blocks.append(near_last)
    fc2_part = share_cores(fc2_part, attended)
    fc1_full = join_fsdp(w_fc1, share_cores(fc1_part), attended)
    fc2_full = join_fsdp(w_fc2, fc2_part, attended)
    small = (b_out, ln2_gain, ln2_bias, b_fc1, b_fc2)
    packed = join_small(tie(jnp.concatenate(small), normed))
    vectors, at = [], 0
    for vec in small:
        size = vec.shape[0]
        vectors.append(packed[:, at : at + size].reshape(-1).astype(f32))
        at += size
    out_bias, gain_two, bias_two, fc1_bias, fc2_bias = vectors
    mixed = lax.all_to_all(attended, SEQ, 0, 0, tiled=True).reshape(width, rows)

    branch = dot(mixed, out_full, 0, 0) + out_bias
    middle = hidden + tie(branch, fc2_full, qkv_part[0])
    normed_two_pre, scaled_two, inv_two = norm_forward(middle, gain_two, bias_two)
    normed_two = normed_two_pre.astype(low)
    inner_sum = dot(normed_two, fc1_full, 1, 0) + fc1_bias
    active, gelu_pull = jax.vjp(partial(jax.nn.gelu, approximate=True), inner_sum)
    active_low = active.astype(low)

    out_cot = out_grad[0]
    cot_full = out_cot.astype(f32)
    active_low, *qkv_part = lax.optimization_barrier((active_low, *qkv_part))
    qkv_part = share_cores(qkv_part)
    fc2_sum = WeightSum([(active_low, out_cot, 0)], scale)
    token = fc2_sum.other_core()
    active_grad = dot(tie(out_cot, token), fc2_full, 1, 1)
    inner_grad = gelu_pull(active_grad)[0].astype(low)
    near_blocks.append(swap(tie(blocks[3], fc2_full), "y"))
    token = fc2_sum.other_f(inner_grad, near_blocks[3])
    norm_two_grad = dot(tie(inner_grad, token), fc1_full, 1, 1)
    gain_two_grad, bias_two_grad, middle_from_norm = norm_backward(
        norm_two_grad, scaled_two, inv_two, gain_two
    )
    middle_grad = cot_full + middle_from_norm
    branch_grad = middle_grad.astype(low)
    mixed_grad = dot(out_full, branch_grad, 1, 1).astype(low)
    attended_grad = lax.all_to_all(
        mixed_grad.reshape(HEADS, HEAD_DIM, rows), SEQ, 0, 0, tiled=True
    )
    rest_sum = WeightSum([(normed_two, inner_grad, 0), (mixed, branch_grad, 1)], scale)
    token = rest_sum.other_core(mixed_grad)
    token = fc2_sum.near_y(token)
    token = rest_sum.other_f(token, *fc2_sum.far[1:])
    column = list(blocks)
    across = [swap(tie(block, mixed_grad), "c") for block in column + near_blocks]
    tokens = [token] + across

    plan = [
        [fc2_sum.near_z, rest_sum.near_y],
        [fc2_sum.far_z, rest_sum.near_z],
        [fc2_sum.back_near_z, rest_sum.far_z],
        [fc2_sum.back_y],
        [rest_sum.back_near_z, lambda *after: fc2_sum.near],
        [rest_sum.back_y],
    ]
    carried, first = None, 0
    for chunk in [HEADS] if groups > 1 else CHUNKS:
        results = attention_backward(
            ends, tie(base, *tokens), qkv, window, attended, attended_grad, log_total, shift,
            first, chunk, carried,
        )
        carried, first = results[::-1], first + chunk
        tokens = []
        for move in plan.pop(0):
            tokens.append(move(results[0], *tokens))
    for moves in plan:
        for move in moves:
            tokens.append(move(results[0]))
    head_grad, *window_grad = results
    if groups > 1:
        both = window_grad[0]
        inner = both[margin : margin + HEADS]
        before = lax.ppermute(both[:margin], "g", down)
        after = lax.ppermute(both[margin + HEADS :], "g", up)
        inner = inner.at[HEADS - margin :].add(before).at[:margin].add(after)
        head_grad = jnp.concatenate([head_grad, inner.astype(low)], axis=1)
    token_grad = lax.all_to_all(tie(head_grad, *tokens), SEQ, 0, 0, tiled=True)

    weight_part = head_weight(
        jnp.concatenate([jnp.stack(planes) * 4 + (place_in_plane ^ k) for k in (0, 2, 1, 3)]).astype(jnp.int32),
        head_grad,
        column + near_blocks + across,
    )
    weight_part = weight_part.reshape(3 * HEAD_DIM, parts, shard_rows).transpose(1, 0, 2)
    if parts == 2:
        weight_part = halve(weight_part, "f")
    else:
        weight_part = lax.psum_scatter(weight_part, "f", scatter_dimension=0, tiled=False)
    if groups > 1:
        weight_part = lax.psum(weight_part, "g")

    weight_part = (weight_part * scale).astype(low)
    qkv_full = join_fsdp(w_qkv, qkv_part, weight_part)
    (fc2_grad,) = fc2_sum.results(qkv_full)
    fc1_grad, out_weight_grad = rest_sum.results(fc2_grad)
    token_grad = tie(token_grad, fc1_grad, out_weight_grad)
    block_out = middle + (dot(tie(active_low, weight_part), fc2_full, 1, 0) + fc2_bias)
    hops = [weight_part] + [
        lax.ppermute(weight_part, "z", [(i, (i + k) % 4) for i in range(4)]) for k in range(1, 4)
    ]

    token_grad = (
        tie(token_grad, fc2_grad).reshape(HEADS, 3, HEAD_DIM, rows).transpose(1, 0, 2, 3).reshape(3 * width, rows)
    )
    norm_one_grad = dot(token_grad, qkv_full, 0, 1)
    gain_one_grad, bias_one_grad, hidden_from_norm = norm_backward(
        norm_one_grad, scaled_one, inv_one, gain_one
    )
    patch_grad = middle_grad + hidden_from_norm

    head_sums = jnp.sum(head_grad.astype(f32), axis=(0, 2))
    qv_grad = jnp.zeros((2 * width,), f32)
    qv_grad = lax.dynamic_update_slice(qv_grad, head_sums[:HEAD_DIM], (head * HEAD_DIM,))
    qv_grad = lax.dynamic_update_slice(
        qv_grad, head_sums[2 * HEAD_DIM :], (width + head * HEAD_DIM,)
    )
    late = VectorSum(
        (
            gain_one_grad,
            bias_one_grad,
            qv_grad,
            jnp.sum(branch_grad.astype(f32), axis=0),
            gain_two_grad,
            bias_two_grad,
            jnp.sum(inner_grad.astype(f32), axis=0),
            jnp.sum(cot_full, axis=0),
        ),
        scale,
    )
    hops = [tie(piece, gain_one_grad) for piece in hops]
    token = late.core()
    token = late.other_f(token)
    pieces = hops + [swap(piece, "y") for piece in hops]
    pieces += [swap(tie(piece, token), "c") for piece in pieces]
    token = late.near_y(token)
    token = late.near_z(token)
    late.far_z(token)
    firsts = lax.rem(z + 4 - jnp.arange(4, dtype=jnp.int32), 4) * 4
    near_places = [firsts + 2 * y + c, firsts + 2 * (1 - y) + c]
    places = jnp.concatenate(near_places + [place_at + 1 - 2 * c for place_at in near_places])
    qkv_weight_grad = weave(pieces, places)
    late.result()
    (
        ln1_gain_sum, ln1_bias_sum, qv_sum, out_bias_sum,
        ln2_gain_sum, ln2_bias_sum, fc1_bias_sum, fc2_bias_sum,
    ) = late.vectors()
    return (
        block_out.astype(low)[None],
        patch_grad[None],
        ln1_gain_sum,
        ln1_bias_sum,
        qkv_weight_grad,
        qv_sum,
        out_weight_grad,
        out_bias_sum,
        ln2_gain_sum,
        ln2_bias_sum,
        fc1_grad,
        fc1_bias_sum,
        fc2_grad,
        fc2_bias_sum,
    )


def solution(mesh):
    seq, parts = mesh.shape["seq"], mesh.shape["fsdp"]
    fine = Mesh(mesh.devices.reshape(seq // HEADS, HEADS // 4, 2, 2, parts), ("g", "z", "y", "c", "f"))
    rows = P("f", ("g",) + SEQ, None)
    vec, mat = P("f"), P("f", None)
    in_specs = (rows, rows, mat, rows, vec, vec, mat, vec, mat, vec, vec, vec, mat, vec, mat, vec)
    out_specs = (rows, rows, vec, vec, mat, vec, mat, vec, vec, vec, mat, vec, mat, vec)
    return jax.shard_map(body, mesh=fine, in_specs=in_specs, out_specs=out_specs, check_vma=False)
```

```python
import math
from functools import partial

import jax
import jax.numpy as jnp
from jax import lax
from jax.experimental import pallas as pl
from jax.experimental.pallas import tpu as pltpu
from jax.sharding import Mesh, PartitionSpec as P

HEADS = 16
LONG = 2304
NORM_EPS = 1e-06
CHUNKS = (2, 4, 3, 2, 3, 2)
HEAD_DIM = 64
BLOCK = 512
FAR = 1e30
QB = 512
KB = 512
HALF = 256
CALM_SCORE = 60.0
FORWARD_COST = 50_000_000_000
BACKWARD_COST = 75_000_000_000


def rows_dot(a, b):
    return lax.dot_general(a, b, (((1,), (0,)), ((), ())), preferred_element_type=jnp.float32)


def membership(ends_ref, count, first, width):
    place = first + lax.broadcasted_iota(jnp.int32, (16, width), 1)
    row = lax.broadcasted_iota(jnp.int32, (16, width), 0)
    low = jnp.zeros((16, width), jnp.int32)
    high = jnp.zeros((16, width), jnp.int32)
    for i in range(count):
        begin = ends_ref[i - 1] if i > 0 else 0
        low = jnp.where(row == i, begin, low)
        high = jnp.where(row == i, ends_ref[i], high)
    return jnp.where((place >= low) & (place < high), 1.0, 0.0)


def image_span(ends_ref, count, first, last):
    low = jnp.int32(0)
    high = ends_ref[count - 1]
    for i in range(count - 1):
        end = ends_ref[i]
        low = jnp.where(end <= first, end, low)
    for i in range(count - 2, -1, -1):
        end = ends_ref[i]
        high = jnp.where(end > last, end, high)
    return low, high


def over_keys(low, high, step, carry):
    def whole(j, carry):
        return step(pl.ds(pl.multiple_of((low + 2 * j) * HALF, HALF), KB), carry)

    def half(j, carry):
        return step(pl.ds(pl.multiple_of(j * HALF, HALF), HALF), carry)

    pairs = (high - low) // 2
    carry = lax.fori_loop(0, pairs, whole, carry)
    return lax.fori_loop(low + 2 * pairs, high, half, carry)


def split3(x):
    top = x.astype(jnp.bfloat16)
    rest = x - top.astype(jnp.float32)
    mid = rest.astype(jnp.bfloat16)
    low = (rest - mid.astype(jnp.float32)).astype(jnp.bfloat16)
    return [top.astype(jnp.float32), mid.astype(jnp.float32), low.astype(jnp.float32)]


def parts_of(ref):
    return [ref.at[:, i * HEAD_DIM : (i + 1) * HEAD_DIM, :] for i in range(ref.shape[1] // HEAD_DIM)]


def forward_kernel(count, shift, pieces, ends_ref, base_ref, *refs):
    if shift:
        own_ref, window_ref, o_ref, log_ref, qa, kn, va, peak = refs
        q_ref = parts_of(own_ref)[0]
        k_ref, v_ref = parts_of(window_ref)
    else:
        place_ref, *refs = refs
        made, (o_ref, log_ref, own_ref, qa, kn, va, peak) = refs[:pieces], refs[pieces:]
        for i in range(pieces):
            own_ref[place_ref[i]] = made[i][...]
        q_ref, k_ref, v_ref = parts_of(own_ref)
    peak[...] = jnp.zeros_like(peak)
    q_blocks = q_ref.shape[0]
    k_blocks = k_ref.shape[0]
    key_count = k_blocks * BLOCK
    base = base_ref[0]

    @pl.loop(0, k_blocks)
    def _(i):
        at = pl.ds(pl.multiple_of(i * BLOCK, BLOCK), BLOCK)
        away = (membership(ends_ref, count, base - shift + i * BLOCK, BLOCK) - 1.0) * FAR
        keys = k_ref[i].astype(jnp.float32)
        peak[1:2] = jnp.maximum(peak[1:2], jnp.sum(keys * keys, axis=0, keepdims=True))
        both = jnp.concatenate([keys, away], axis=0)
        kn[at, :] = both.T.astype(jnp.bfloat16)
        va[:, at] = jnp.concatenate(
            [v_ref[i].astype(jnp.float32), jnp.ones((16, BLOCK), jnp.float32)], axis=0
        ).astype(jnp.bfloat16)

    @pl.loop(0, q_blocks)
    def _(i):
        at = pl.ds(pl.multiple_of(i * BLOCK, BLOCK), BLOCK)
        inside = membership(ends_ref, count, base + i * BLOCK, BLOCK)
        asked = q_ref[i].astype(jnp.float32)
        peak[0:1] = jnp.maximum(peak[0:1], jnp.sum(asked * asked, axis=0, keepdims=True))
        qa[:, at] = jnp.concatenate(
            [asked * (HEAD_DIM ** -0.5), inside], axis=0
        ).astype(jnp.bfloat16)

    per = BLOCK // QB
    calm = CALM_SCORE * HEAD_DIM ** 0.5
    peaks = [jnp.max(peak[i : i + 1]) for i in range(2)]

    def span(i):
        first = base + i * QB
        low, high = image_span(ends_ref, count, first, first + QB - 1)
        low = jnp.maximum(low - base + shift, 0) // HALF
        return low, jnp.minimum(high - base + shift + HALF - 1, key_count) // HALF

    def finish(i, top, acc):
        total = acc[HEAD_DIM : HEAD_DIM + 1]
        o_ref[i // per, :, pl.ds(pl.multiple_of((i % per) * QB, QB), QB)] = (
            acc[:HEAD_DIM] / total
        ).astype(jnp.bfloat16)
        log_ref[:, pl.ds(pl.multiple_of(i * QB, QB), QB)] = top + jnp.log(total)

    small = peaks[0] * peaks[1] <= calm * calm

    @pl.when(small)
    def _():
        @pl.loop(0, q_blocks * per)
        def _(i):
            q_part = qa[:, pl.ds(pl.multiple_of(i * QB, QB), QB)]

            def step(at, acc):
                weights = jnp.exp(rows_dot(kn[at, :], q_part)).astype(jnp.bfloat16)
                return acc + rows_dot(va[:, at], weights)

            finish(i, 0.0, over_keys(*span(i), step, jnp.zeros((HEAD_DIM + 16, QB), jnp.float32)))

    @pl.when(jnp.logical_not(small))
    def _():
        @pl.loop(0, q_blocks * per)
        def _(i):
            q_part = qa[:, pl.ds(pl.multiple_of(i * QB, QB), QB)]

            def step(at, carry):
                top, acc = carry
                scores = rows_dot(kn[at, :], q_part)
                new_top = jnp.maximum(top, jnp.max(scores, axis=0, keepdims=True))
                weights = jnp.exp(scores - new_top).astype(jnp.bfloat16)
                acc = acc * jnp.exp(top - new_top) + rows_dot(va[:, at], weights)
                return new_top, acc

            start = (
                jnp.full((1, QB), -3e38, jnp.float32),
                jnp.zeros((HEAD_DIM + 16, QB), jnp.float32),
            )
            finish(i, *over_keys(*span(i), step, start))


def backward_kernel(count, shift, first_block, chunk, last, ends_ref, base_ref, own_ref, *refs):
    q_ref, k_ref, v_ref = parts_of(own_ref)
    if shift:
        k_ref, v_ref = parts_of(refs[0])
        refs = refs[1:]
    o_ref, do_ref, log_ref, *refs = refs
    if first_block > 0:
        sums_in, _, *refs = refs
    grad_ref, *refs = refs
    sums_out = None
    if shift:
        window_ref, *refs = refs
    if not last:
        sums_out, *refs = refs
    qa, da, kn, vn, qn, dn, ks, sums, dq_part, sums_sem, dq_sem, *refs = refs
    k_blocks = k_ref.shape[0]
    key_count = k_blocks * BLOCK
    base = base_ref[0]
    scale = HEAD_DIM ** -0.5
    start = base + first_block * BLOCK
    low, high = image_span(ends_ref, count, start, start + chunk * BLOCK - 1)
    low = jnp.maximum(low - base + shift, 0) // BLOCK
    high = jnp.minimum(high - base + shift + BLOCK - 1, key_count) // BLOCK
    held_low, held_high = (0, k_blocks) if last or first_block == 0 else (low, high)

    def block_at(i):
        return pl.ds(pl.multiple_of(i * BLOCK, BLOCK), BLOCK)

    if first_block > 0:

        @pl.loop(held_low, held_high)
        def _(i):
            pltpu.make_async_copy(sums_in.at[block_at(i)], sums.at[block_at(i)], sums_sem.at[i]).start()

    else:
        sums[...] = jnp.zeros_like(sums)

    @pl.loop(low, high)
    def _(i):
        at = block_at(i)
        away = (membership(ends_ref, count, base - shift + i * BLOCK, BLOCK) - 1.0) * FAR
        ones = jnp.ones((16, BLOCK), jnp.float32)
        keys = k_ref[i].astype(jnp.float32)
        kn[at, :] = jnp.concatenate([keys, away, ones], axis=0).T.astype(jnp.bfloat16)
        vn[at, :] = jnp.concatenate([v_ref[i].astype(jnp.float32), ones], axis=0).T.astype(jnp.bfloat16)
        ks[:, at] = (keys * scale).astype(jnp.bfloat16)

    @pl.loop(0, chunk)
    def _(i):
        at = block_at(i)
        block = first_block + i
        inside = membership(ends_ref, count, base + block * BLOCK, BLOCK)
        pad = jnp.zeros((13, BLOCK), jnp.float32)
        scaled = q_ref[block].astype(jnp.float32) * scale
        qn[at, :] = scaled.T.astype(jnp.bfloat16)
        qa[:, at] = jnp.concatenate(
            [scaled, inside] + split3(-log_ref[:, block_at(block)]) + [pad], axis=0
        ).astype(jnp.bfloat16)
        grads = do_ref[block].astype(jnp.float32)
        row_dot = jnp.sum(grads * o_ref[block].astype(jnp.float32), axis=0, keepdims=True)
        dn[at, :] = grads.T.astype(jnp.bfloat16)
        da[:, at] = jnp.concatenate([grads] + split3(-row_dot) + [pad], axis=0).astype(jnp.bfloat16)

    if first_block > 0:

        @pl.loop(held_low, held_high)
        def _(i):
            pltpu.make_async_copy(sums_in.at[block_at(i)], sums.at[block_at(i)], sums_sem.at[i]).wait()

    @pl.loop(0, chunk)
    def _(i):
        q_at = block_at(i)
        q_part = qa[:, q_at]
        d_part = da[:, q_at]
        q_rows = qn[q_at, :]
        d_rows = dn[q_at, :]
        first = start + i * BLOCK
        key_low, key_high = image_span(ends_ref, count, first, first + BLOCK - 1)
        key_low = jnp.maximum(key_low - base + shift, 0) // HALF
        key_high = jnp.minimum(key_high - base + shift + HALF - 1, key_count) // HALF

        def step(at, dq):
            probs = jnp.exp(rows_dot(kn[at, :], q_part))
            score_grad = (probs * rows_dot(vn[at, :], d_part)).astype(jnp.bfloat16)
            sums[at, 0:HEAD_DIM] += rows_dot(score_grad, q_rows)
            sums[at, HEAD_DIM : 2 * HEAD_DIM] += rows_dot(probs.astype(jnp.bfloat16), d_rows)
            return dq + rows_dot(ks[:, at], score_grad)

        dq = over_keys(key_low, key_high, step, jnp.zeros((HEAD_DIM, BLOCK), jnp.float32))
        dq_part[i] = dq.astype(jnp.bfloat16)

    def query_copy(i):
        return pltpu.make_async_copy(
            dq_part.at[i], grad_ref.at[first_block + i, 0:HEAD_DIM], dq_sem.at[i]
        )

    for i in range(chunk):
        query_copy(i).start()
    if not last:

        @pl.loop(held_low, held_high)
        def _(i):
            pltpu.make_async_copy(sums.at[block_at(i)], sums_out.at[block_at(i)], sums_sem.at[i]).start()

        @pl.loop(held_low, held_high)
        def _(i):
            pltpu.make_async_copy(sums.at[block_at(i)], sums_out.at[block_at(i)], sums_sem.at[i]).wait()

    elif shift:

        @pl.loop(0, k_blocks)
        def _(i):
            window_ref[i] = sums[block_at(i), :].T

    else:
        kv_part, kv_sem = refs

        def key_copy(i):
            return pltpu.make_async_copy(
                kv_part.at[i], grad_ref.at[i, HEAD_DIM : 3 * HEAD_DIM], kv_sem.at[i]
            )

        @pl.loop(0, k_blocks)
        def _(i):
            kv_part[i] = sums[block_at(i), :].T.astype(jnp.bfloat16)
            key_copy(i).start()

        @pl.loop(0, k_blocks)
        def _(i):
            key_copy(i).wait()

    for i in range(chunk):
        query_copy(i).wait()


def vmem_spec():
    return pl.BlockSpec(memory_space=pltpu.VMEM)


def smem_spec():
    return pl.BlockSpec(memory_space=pltpu.SMEM)


def attention_forward(ends, base, made, places, window, shift):
    blocks = made[0].shape[0] if shift else len(made)
    tokens, keys = blocks * BLOCK, blocks * BLOCK + 2 * shift
    low = jnp.bfloat16
    out_shape = [
        jax.ShapeDtypeStruct((blocks, HEAD_DIM, BLOCK), low),
        jax.ShapeDtypeStruct((1, tokens), jnp.float32),
    ]
    if shift:
        arrays, in_specs = [*made, window], [smem_spec()] * 2 + [vmem_spec()] * 2
    else:
        arrays, in_specs = [places, *made], [smem_spec()] * 3 + [vmem_spec()] * blocks
        out_shape.append(jax.ShapeDtypeStruct((blocks, 3 * HEAD_DIM, BLOCK), low))
    return pl.pallas_call(
        partial(forward_kernel, ends.shape[0], shift, blocks),
        out_shape=out_shape,
        in_specs=in_specs,
        out_specs=[vmem_spec()] * len(out_shape),
        scratch_shapes=[
            pltpu.VMEM((HEAD_DIM + 16, tokens), low),
            pltpu.VMEM((keys, HEAD_DIM + 16), low),
            pltpu.VMEM((HEAD_DIM + 16, keys), low),
            pltpu.VMEM((8, BLOCK), jnp.float32),
        ],
        compiler_params=pltpu.CompilerParams(vmem_limit_bytes=48 * 1024 * 1024),
        cost_estimate=pl.CostEstimate(
            flops=FORWARD_COST, bytes_accessed=tokens * 512, transcendentals=0
        ),
    )(ends, base, *arrays)


def attention_backward(ends, base, own, window, o, do, log, shift, first_block, chunk, carried):
    blocks = own.shape[0]
    tokens, keys = chunk * BLOCK, blocks * BLOCK + 2 * shift
    last = first_block + chunk == blocks
    low, f32 = jnp.bfloat16, jnp.float32
    arrays = [own] + ([window] if shift else []) + [o, do, log]
    in_specs = [smem_spec(), smem_spec()] + [vmem_spec()] * len(arrays)
    out_shape = [jax.ShapeDtypeStruct((blocks, HEAD_DIM if shift else 3 * HEAD_DIM, BLOCK), low)]
    out_specs = [any_spec()]
    aliases = {}
    if carried is not None:
        place_at = 2 + len(arrays)
        arrays += list(carried)
        in_specs += [any_spec(), any_spec()]
        aliases = {place_at + 1: 0}
        if not last:
            aliases[place_at] = 1
    if shift:
        out_shape.append(jax.ShapeDtypeStruct((keys // BLOCK, 2 * HEAD_DIM, BLOCK), f32))
        out_specs.append(vmem_spec())
    if not last:
        out_shape.append(jax.ShapeDtypeStruct((keys, 2 * HEAD_DIM), f32))
        out_specs.append(any_spec())
    scratch = [
        pltpu.VMEM((HEAD_DIM + 32, tokens), low),
        pltpu.VMEM((HEAD_DIM + 16, tokens), low),
        pltpu.VMEM((keys, HEAD_DIM + 32), low),
        pltpu.VMEM((keys, HEAD_DIM + 16), low),
        pltpu.VMEM((tokens, HEAD_DIM), low),
        pltpu.VMEM((tokens, HEAD_DIM), low),
        pltpu.VMEM((HEAD_DIM, keys), low),
        pltpu.VMEM((keys, 2 * HEAD_DIM), f32),
        pltpu.VMEM((chunk, HEAD_DIM, BLOCK), low),
        pltpu.SemaphoreType.DMA((keys // BLOCK,)),
        pltpu.SemaphoreType.DMA((chunk,)),
    ]
    if last and not shift:
        scratch += [
            pltpu.VMEM((blocks, 2 * HEAD_DIM, BLOCK), low),
            pltpu.SemaphoreType.DMA((blocks,)),
        ]
    return pl.pallas_call(
        partial(backward_kernel, ends.shape[0], shift, first_block, chunk, last),
        out_shape=out_shape,
        in_specs=in_specs,
        out_specs=out_specs,
        scratch_shapes=scratch,
        input_output_aliases=aliases,
        compiler_params=pltpu.CompilerParams(vmem_limit_bytes=50 * 1024 * 1024),
        cost_estimate=pl.CostEstimate(flops=BACKWARD_COST * chunk // blocks, bytes_accessed=tokens * 1024, transcendentals=0),
    )(ends, base, *arrays)


def any_spec():
    return pl.BlockSpec(memory_space=pl.ANY)


def block_rows(rows, cols):
    while rows * cols > 512 * 1024 and rows % 16 == 0:
        rows //= 2
    return rows


def take_kernel(at_ref, in_ref, out_ref):
    out_ref[...] = in_ref[...]


def take(x, index, count):
    rows, cols = x.shape[0] // count, x.shape[1]
    size = block_rows(rows, cols)
    steps = rows // size
    return pl.pallas_call(
        take_kernel,
        out_shape=jax.ShapeDtypeStruct((rows, cols), x.dtype),
        grid_spec=pltpu.PrefetchScalarGridSpec(
            num_scalar_prefetch=1,
            grid=(steps,),
            in_specs=[pl.BlockSpec((size, cols), lambda j, at_ref: (at_ref[0] * steps + j, 0))],
            out_specs=pl.BlockSpec((size, cols), lambda j, at_ref: (j, 0)),
        ),
        cost_estimate=pl.CostEstimate(flops=0, bytes_accessed=2 * rows * cols * x.dtype.itemsize, transcendentals=0),
    )(index.astype(jnp.int32).reshape(1), x)


def place_kernel(owner, row_ref, col_ref, *refs):
    out_ref = refs[-1]
    for i, piece in enumerate(owner):

        @pl.when(pl.program_id(0) == i)
        def _(piece=piece):
            out_ref[...] = refs[piece][...].astype(out_ref.dtype)


def place(pieces, row_at, col_at, dtype, rows, shape, cols=None, block=0):
    cols = cols or pieces[0].shape[1]
    owner = [n for n, piece in enumerate(pieces) for _ in range(piece.shape[0] // rows)]
    count = len(owner)
    size = block_rows(rows, cols)
    steps = rows // size

    def piece_map(piece):
        turns = [i for i in range(count) if owner[i] == piece]
        first, last = turns[0], turns[-1]

        def index(s, j, row_ref, col_ref):
            inside = j + (s - first) * steps
            end = (last - first + 1) * steps - 1
            return (jnp.where(s < first, 0, jnp.where(s > last, end, inside)), block)

        return index

    return pl.pallas_call(
        partial(place_kernel, owner),
        out_shape=jax.ShapeDtypeStruct(shape, dtype),
        grid_spec=pltpu.PrefetchScalarGridSpec(
            num_scalar_prefetch=2,
            grid=(count, steps),
            in_specs=[pl.BlockSpec((size, cols), piece_map(i)) for i in range(len(pieces))],
            out_specs=pl.BlockSpec(
                (size, cols), lambda s, j, row_ref, col_ref: (row_ref[s] * steps + j, col_ref[s])
            ),
        ),
        cost_estimate=pl.CostEstimate(
            flops=0,
            bytes_accessed=count * rows * cols * (2 + jnp.dtype(dtype).itemsize),
            transcendentals=0,
        ),
    )(row_at, col_at, *pieces)


def plane_columns_kernel(plane_ref, q_ref, k_ref, v_ref, out_ref):
    for part, ref in enumerate((q_ref, k_ref, v_ref)):
        cols = ref[...].astype(jnp.float32).T
        for j in range(4):
            at = (3 * j + part) * HEAD_DIM
            out_ref[at : at + HEAD_DIM] = cols[j * HEAD_DIM : (j + 1) * HEAD_DIM].astype(out_ref.dtype)


def plane_columns(w, plane):
    rows = w.shape[0]

    def spec(part):
        return pl.BlockSpec((rows, 4 * HEAD_DIM), lambda i, plane_ref: (0, part * (HEADS // 4) + plane_ref[0]))

    return pl.pallas_call(
        plane_columns_kernel,
        out_shape=jax.ShapeDtypeStruct((12 * HEAD_DIM, rows), w.dtype),
        grid_spec=pltpu.PrefetchScalarGridSpec(
            num_scalar_prefetch=1,
            grid=(1,),
            in_specs=[spec(part) for part in range(3)],
            out_specs=pl.BlockSpec((12 * HEAD_DIM, rows), lambda i, plane_ref: (0, 0)),
        ),
    )(plane.astype(jnp.int32).reshape(1), w, w, w)


def project_kernel(head_ref, w_ref, bias_ref, block_ref, *out_refs):
    size = w_ref.shape[2]
    rows = 3 * HEAD_DIM
    for i, out_ref in enumerate(out_refs):
        at = pl.ds(pl.multiple_of(head_ref[i] * rows, HEAD_DIM), rows)
        total = bias_ref[at, :]
        for f in range(w_ref.shape[0]):
            total += lax.dot_general(
                w_ref[f, at, :], block_ref[:, f * size : (f + 1) * size], (((1,), (1,)), ((), ())),
                preferred_element_type=jnp.float32,
            )
        out_ref[...] = total.astype(jnp.bfloat16)


def project(heads, w, bias, block):
    rows, width = block.shape
    count = heads.shape[0]
    shape = jax.ShapeDtypeStruct((3 * HEAD_DIM, rows), jnp.bfloat16)
    return pl.pallas_call(
        project_kernel,
        out_shape=[shape] * count,
        in_specs=[smem_spec()] + [vmem_spec()] * 3,
        out_specs=[vmem_spec()] * count,
        compiler_params=pltpu.CompilerParams(vmem_limit_bytes=24 * 1024 * 1024),
        cost_estimate=pl.CostEstimate(
            flops=6 * count * rows * width * 3 * HEAD_DIM, bytes_accessed=rows * width * 2, transcendentals=0
        ),
    )(heads, w, bias, block)


def assemble_kernel(count, place_ref, *refs):
    pieces, out_ref, sem = refs[:count], refs[count], refs[count + 1]

    def copy(i):
        return pltpu.make_async_copy(pieces[i], out_ref.at[place_ref[i]], sem.at[i])

    for i in range(count):
        copy(i).start()
    for i in range(count):
        copy(i).wait()


def assemble(pieces, places):
    count = len(pieces)
    return pl.pallas_call(
        partial(assemble_kernel, count),
        out_shape=jax.ShapeDtypeStruct((count,) + pieces[0].shape, pieces[0].dtype),
        in_specs=[smem_spec()] + [vmem_spec()] * count,
        out_specs=any_spec(),
        scratch_shapes=[pltpu.SemaphoreType.DMA((count,))],
        compiler_params=pltpu.CompilerParams(vmem_limit_bytes=16 * 1024 * 1024),
        cost_estimate=pl.CostEstimate(
            flops=0, bytes_accessed=4 * count * pieces[0].size, transcendentals=0
        ),
    )(places, *pieces)


SLOTS = 4


def head_weight_kernel(count, place_ref, grad_ref, *refs):
    blocks, (out_ref, held, sem) = refs[:count], refs[count:]

    def copy(b):
        return pltpu.make_async_copy(blocks[b], held.at[b % SLOTS], sem.at[b % SLOTS])

    for b in range(SLOTS - 1):
        copy(b).start()
    out_ref[...] = jnp.zeros_like(out_ref)

    @pl.loop(0, count)
    def _(i):
        slot = lax.rem(i, SLOTS)
        pltpu.make_async_copy(blocks[0], held.at[slot], sem.at[slot]).wait()
        for b in range(SLOTS - 1, count):

            @pl.when(i + SLOTS - 1 == b)
            def _(b=b):
                copy(b).start()

        out_ref[...] += rows_dot(grad_ref[place_ref[i]], held[slot])


def head_weight(places, grad, blocks):
    count = len(blocks)
    rows, width = blocks[0].shape
    cols = grad.shape[1]
    return pl.pallas_call(
        partial(head_weight_kernel, count),
        out_shape=jax.ShapeDtypeStruct((cols, width), jnp.float32),
        in_specs=[smem_spec(), vmem_spec()] + [any_spec()] * count,
        out_specs=vmem_spec(),
        scratch_shapes=[
            pltpu.VMEM((SLOTS, rows, width), jnp.bfloat16),
            pltpu.SemaphoreType.DMA((SLOTS,)),
        ],
        compiler_params=pltpu.CompilerParams(vmem_limit_bytes=24 * 1024 * 1024),
        cost_estimate=pl.CostEstimate(flops=4 * count * rows * width * cols, bytes_accessed=count * rows * width * 2, transcendentals=0),
    )(places, grad, *blocks)


def weave_kernel(count, at_ref, *refs):
    pieces, (out_ref, held) = refs[:count], refs[count:]
    for i in range(count):
        held[at_ref[i]] = pieces[i][...]
    for part in range(3):
        for pair in range(count // 2):
            rows = slice(part * HEAD_DIM, (part + 1) * HEAD_DIM)
            both = jnp.concatenate([held[2 * pair, rows], held[2 * pair + 1, rows]], axis=0)
            at = (part * count + 2 * pair) * HEAD_DIM
            out_ref[:, at : at + 2 * HEAD_DIM] = both.astype(jnp.float32).T


def weave(pieces, places):
    count = len(pieces)
    cols, rows = pieces[0].shape
    size = 128
    return pl.pallas_call(
        partial(weave_kernel, count),
        out_shape=jax.ShapeDtypeStruct((rows, count * cols), jnp.float32),
        grid_spec=pltpu.PrefetchScalarGridSpec(
            num_scalar_prefetch=1,
            grid=(rows // size,),
            in_specs=[pl.BlockSpec((cols, size), lambda i, at_ref: (0, i))] * count,
            out_specs=pl.BlockSpec((size, count * cols), lambda i, at_ref: (i, 0)),
            scratch_shapes=[pltpu.VMEM((count, cols, size), pieces[0].dtype)],
        ),
        cost_estimate=pl.CostEstimate(
            flops=0, bytes_accessed=6 * count * cols * rows, transcendentals=0
        ),
    )(places, *pieces)


SEQ = ("z", "y", "c")
SWAP = ((0, 1), (1, 0))


def norm_forward(hidden, gain_vec, offset_vec):
    centre = hidden - jnp.mean(hidden, axis=-1, keepdims=True)
    spread = jnp.mean(centre * centre, axis=-1, keepdims=True)
    inv_std = lax.rsqrt(spread + NORM_EPS)
    scaled = centre * inv_std
    return (scaled * gain_vec + offset_vec, scaled, inv_std)


def norm_backward(grad_out, scaled, inv_std, gain_vec):
    gain_grad = jnp.sum(grad_out * scaled, axis=0)
    offset_grad = jnp.sum(grad_out, axis=0)
    grad_scaled = grad_out * gain_vec
    grad_in = inv_std * (
        grad_scaled
        - jnp.mean(grad_scaled, axis=-1, keepdims=True)
        - scaled * jnp.mean(grad_scaled * scaled, axis=-1, keepdims=True)
    )
    return (gain_grad, offset_grad, grad_in)


def dot(a, b, a_dim, b_dim):
    return lax.dot_general(
        a, b, (((a_dim,), (b_dim,)), ((), ())), preferred_element_type=jnp.float32
    )


def tie(x, *others):
    others = [other for other in others if other is not None]
    return lax.optimization_barrier((x, *others))[0] if others else x


def linear(start, first, a, second, b):
    start, first, second = (jnp.array(x, jnp.int32) for x in (start, first, second))
    return start + first * a + second * b


def pick(x, i, axis=0):
    return lax.dynamic_index_in_dim(x, i, axis, keepdims=False)


def swap(x, axis):
    return lax.ppermute(x, axis, SWAP)


def in_order(own, other, position):
    return jnp.where(position == 0, jnp.stack([own, other]), jnp.stack([other, own]))


def fetch_fsdp(shard, pieces, *others):
    if lax.axis_size("f") != 2:
        return [], [lax.all_gather(shard, "f", axis=0, tiled=True)]
    first = lax.axis_index("c") * pieces
    shard = tie(shard, *others)
    taken = [take(shard, first + i, 2 * pieces) for i in range(pieces)]
    return taken, [swap(part, "f") for part in taken]


def share_cores(fetched, *others):
    if lax.axis_size("f") != 2:
        return fetched
    return fetched + [swap(tie(piece, *others), "c") for piece in fetched]


def join_fsdp(shard, pieces, *others):
    if lax.axis_size("f") != 2:
        return pieces[0]
    core, here = lax.axis_index("c"), lax.axis_index("f")
    count = len(pieces) // 2
    step = range(count)
    at = linear(
        (*range(2 * count), *(2 * count + i for i in step), *(3 * count + i for i in step)),
        (2 * count,) * (2 * count) + (-2 * count,) * (2 * count),
        here,
        (0,) * (2 * count) + (count,) * count + (-count,) * count,
        core,
    )
    rows, cols = shard.shape
    return place(
        [tie(shard, *others), *pieces], at, jnp.zeros_like(at), shard.dtype, rows // (2 * count), (2 * rows, cols)
    )


def join_small(shard):
    if lax.axis_size("f") != 2:
        return lax.all_gather(shard, "f", axis=0, tiled=False)
    return in_order(shard, swap(shard, "f"), lax.axis_index("f"))


def halve(x, axis, pairs=SWAP, here=None):
    here = lax.axis_index(axis) if here is None else here
    got = lax.ppermute(pick(x, 1 - here), axis, pairs)
    return pick(x, here).astype(jnp.float32) + got.astype(jnp.float32)


def plane_pairs(bit):
    return [(i, i ^ bit) for i in range(4)]


class WeightSum:
    def __init__(self, terms, scale):
        self.terms, self.scale = terms, scale
        self.widths = [right.shape[1] // 2 for _, right, _ in terms]
        self.cols = sum(self.widths)
        self.rows = terms[0][0].shape[1 - terms[0][2]] // lax.axis_size("f")

    def after(self, others):
        self.terms = [(left, tie(right, *others), dim) for left, right, dim in self.terms]

    def term(self, n, c, f, half=None):
        left, right, dim = self.terms[n]
        rows, start = self.rows, f * self.rows
        if half is not None:
            rows //= 2
            start = start + half * rows
        left = lax.dynamic_slice_in_dim(left, start, rows, 1 - dim)
        right = lax.dynamic_slice_in_dim(right, c * self.widths[n], self.widths[n], 1)
        return dot(left, right, dim, 0)

    def joined(self, parts):
        parts = [part.astype(jnp.bfloat16) for part in parts]
        return parts[0] if len(parts) == 1 else jnp.concatenate(parts, axis=1)

    def half_of(self, x, half):
        rows = x.shape[0] // 2
        return lax.dynamic_slice_in_dim(x, half * rows, rows, 0).astype(jnp.float32)

    def other_core(self, *others):
        self.after(others)
        core, parts, here = lax.axis_index("c"), lax.axis_size("f"), lax.axis_index("f")
        order = [1 - here, here] if parts == 2 else range(parts)
        self.got = []
        for f in order:
            sent = [self.term(n, 1 - core, f).astype(jnp.bfloat16) for n in range(len(self.terms))]
            self.got.append([swap(part, "c") for part in sent])
        return sent[-1]

    def other_f(self, *others):
        self.after(others)
        core, parts, here = lax.axis_index("c"), lax.axis_size("f"), lax.axis_index("f")
        y, count = lax.axis_index("y"), range(len(self.terms))
        if parts == 2:
            self.far = []
            for half in (1 - y, y):
                sent = self.joined(
                    [self.term(n, core, 1 - here, half) + self.half_of(self.got[0][n], half) for n in count]
                )
                self.far.append(swap(sent, "f"))
                self.after([sent])
            return sent
        total = [
            self.joined([self.term(n, core, f) + self.got[f][n].astype(jnp.float32) for n in count])
            for f in range(parts)
        ]
        self.far = []
        self.total = lax.psum_scatter(jnp.stack(total), "f", scatter_dimension=0, tiled=False)
        return self.total

    def here_half(self, k, half):
        core, parts, here = lax.axis_index("c"), lax.axis_size("f"), lax.axis_index("f")
        if parts != 2:
            return [self.half_of(self.total, half)]
        x, at = [], 0
        for n, width in enumerate(self.widths):
            total = self.term(n, core, here, half) + self.half_of(self.got[1][n], half)
            x.append(total + self.far[k][:, at : at + width].astype(jnp.float32))
            at += width
        return x

    def near_y(self, *others):
        self.after(others)
        sent = self.joined(self.here_half(0, 1 - lax.axis_index("y")))
        self.coming = lax.ppermute(sent, "y", SWAP)
        return sent

    def near_z(self, *others):
        self.coming = tie(self.coming, *others)
        self.after(others)
        x, at = [], 0
        for part in self.here_half(1, lax.axis_index("y")):
            width = part.shape[1]
            x.append(part + self.coming[:, at : at + width].astype(jnp.float32))
            at += width
        x = self.joined(x).reshape(2, -1, self.cols)
        low_z = lax.rem(lax.axis_index("z"), 2)
        sent = pick(x, 1 - low_z)
        self.kept, self.coming = pick(x, low_z), lax.ppermute(sent, "z", plane_pairs(1))
        return sent

    def added(self, x, others):
        return x.astype(jnp.float32) + tie(self.coming, *others).astype(jnp.float32)

    def far_z(self, *others):
        self.x = self.added(self.kept, others).astype(jnp.bfloat16)
        self.coming = lax.ppermute(self.x, "z", plane_pairs(2))
        return self.x

    def back_near_z(self, *others):
        x = self.added(self.x, others)
        if lax.axis_size("g") > 1:
            x = lax.psum(x, "g")
        self.x = (x * self.scale).astype(jnp.bfloat16)
        self.coming = lax.ppermute(self.x, "z", plane_pairs(1))
        return self.x

    def back_y(self, *others):
        coming = tie(self.coming, *others)
        x = in_order(self.x, coming, lax.rem(lax.axis_index("z"), 2)).reshape(-1, self.cols)
        self.near = lax.ppermute(x, "y", SWAP)
        self.x, self.across = x, swap(x, "c")
        return x

    def results(self, *others):
        y, c = lax.axis_index("y"), lax.axis_index("c")
        near = tie(self.near, *others)
        pieces = [self.x, near, self.across, swap(near, "c")]
        row_at = linear((0, 1, 0, 1), (1, -1, 1, -1), y, (0, 0, 0, 0), c)
        col_at = linear((0, 0, 1, 1), (0, 0, 0, 0), y, (1, 1, -1, -1), c)
        rows, at, results = pieces[0].shape[0], 0, []
        for width in self.widths:
            results.append(
                place(
                    pieces, row_at, col_at, jnp.float32, rows, (2 * rows, 2 * width), width, at // width
                )
            )
            at += width
        return results


class VectorSum:
    def __init__(self, vectors, scale):
        self.sizes = [vec.shape[0] // lax.axis_size("f") for vec in vectors]
        self.x = jnp.concatenate([vec.reshape(lax.axis_size("f"), -1) for vec in vectors], axis=1) * scale

    def core(self, *others):
        self.x = tie(self.x, *others)
        self.coming = swap(self.x, "c")
        return self.x

    def other_f(self, *others):
        x = self.x + tie(self.coming, *others)
        if lax.axis_size("f") == 2:
            here = lax.axis_index("f")
            self.x, sent = pick(x, here), pick(x, 1 - here)
            self.coming = swap(sent, "f")
            return sent
        self.x = lax.psum_scatter(x, "f", scatter_dimension=0, tiled=False)
        self.coming = jnp.zeros_like(self.x)
        return self.x

    def hop(self, axis, pairs, others):
        self.x = self.x + tie(self.coming, *others)
        self.coming = lax.ppermute(self.x, axis, pairs)
        return self.x

    def near_y(self, *others):
        return self.hop("y", SWAP, others)

    def near_z(self, *others):
        return self.hop("z", plane_pairs(1), others)

    def far_z(self, *others):
        return self.hop("z", plane_pairs(2), others)

    def result(self, *others):
        self.total = self.x + tie(self.coming, *others)
        if lax.axis_size("g") > 1:
            self.total = lax.psum(self.total, "g")
        return self.total

    def vectors(self):
        at = 0
        for size in self.sizes:
            yield self.total[at : at + size]
            at += size


def arrivals(count):
    table = []
    for z in range(count):
        hops = []
        for t in range(1, count):
            if z - t >= 0:
                hops.append(("up", t))
            if z + t < count:
                hops.append(("down", t))
        table.append(hops)
    return table


def gather_planes(x, use, beside, later):
    z = lax.axis_index("z")
    count = lax.axis_size("z")
    table = arrivals(count)
    up, down = x, x
    hops = {}
    blocks, planes, used = [x], [z], []
    for t in range(1, count):
        up = lax.ppermute(up, "z", [(i, i + 1) for i in range(t - 1, count - 1)])
        down = lax.ppermute(down, "z", [(i, i - 1) for i in range(1, count - t + 1)])
        made = use(blocks[-1])
        before = used.pop() if used else []
        up, down, before, made[0], extra, _ = lax.optimization_barrier(
            (up, down, before, made[0], later[t - 1](blocks), beside[t - 1])
        )
        later[t - 1](blocks, extra)
        used += [before] * (t > 1) + [made]
        hops["up", t], hops["down", t] = up, down
        names = sorted({table[i][t - 1] for i in range(count)})
        block, plane = None, z
        for name in names:
            here = [i for i in range(count) if table[i][t - 1] == name]
            chosen = (z >= here[0]) & (z <= here[-1])
            block = hops[name] if block is None else jnp.where(chosen, hops[name], block)
            plane = jnp.where(chosen, z + (-name[1] if name[0] == "up" else name[1]), plane)
        blocks.append(block)
        planes.append(plane)
    used.append(use(blocks[-1]))
    return blocks, planes, used


def body(
    patches, pos_embed, lengths, out_grad,
    ln1_gain, ln1_bias, w_qkv, b_qv, w_out, b_out,
    ln2_gain, ln2_bias, w_fc1, b_fc1, w_fc2, b_fc2,
):
    f32, low = jnp.float32, jnp.bfloat16
    rows, width = patches.shape[1:]
    groups, parts = lax.axis_size("g"), lax.axis_size("f")
    head = lax.axis_index(SEQ)
    group = lax.axis_index("g")
    shard_index = lax.axis_index("f")
    scale = 1.0 / (parts * math.sqrt(rows * HEADS * groups))

    gain_one, bias_one, qv_bias = (
        join_small(vec).reshape(-1).astype(f32) for vec in (ln1_gain, ln1_bias, b_qv)
    )
    hidden = patches[0].astype(f32) + pos_embed[0].astype(f32)
    normed_pre, scaled_one, inv_one = norm_forward(hidden, gain_one, bias_one)
    normed = normed_pre.astype(low)

    shard_rows = w_qkv.shape[0]
    z, y, c = (lax.axis_index(axis) for axis in SEQ)
    place_in_plane = 2 * y + c
    plane_weights = join_small(plane_columns(tie(w_qkv, gain_one, bias_one, qv_bias), z)).reshape(parts, 12 * HEAD_DIM, shard_rows)
    q_bias, v_bias = (
        lax.dynamic_slice_in_dim(qv_bias, at + z * 4 * HEAD_DIM, 4 * HEAD_DIM).reshape(4, HEAD_DIM)
        for at in (0, width)
    )
    plane_bias = jnp.concatenate([q_bias, jnp.zeros((4, HEAD_DIM), f32), v_bias], axis=1).reshape(-1, 1)
    others = jnp.array([0, 1, 2, 3], jnp.int32)
    heads_made = others ^ place_in_plane

    def heads_of(block):
        own, core, near, far = project(heads_made, plane_weights, plane_bias, block)
        return [
            own, swap(core, "c"), swap(near, "y"),
            lax.ppermute(far, ("y", "c"), [(i, 3 - i) for i in range(4)]),
        ]

    out_taken, out_part = fetch_fsdp(w_out, 1, normed)
    fc1_taken, fc1_part = fetch_fsdp(w_fc1, 2, normed)
    fc2_taken, fc2_part = fetch_fsdp(w_fc2, 2, normed)
    if parts == 2:
        fc2_part = [swap(tie(part, fc1_part[1]), "f") for part in fc2_taken]
    qkv_taken, qkv_part = fetch_fsdp(w_qkv, 2, normed)
    out_full = join_fsdp(w_out, share_cores(out_part))
    beside = [
        out_taken + fc1_taken + fc2_taken + qkv_taken, out_part, fc1_part[:1] + [out_full],
    ]
    near_blocks = []

    def swap_later(first):
        def step(blocks, done=None):
            if done is None:
                return [swap(blocks[first], "y")] if first is not None else []
            near_blocks.extend(done)

        return step

    later = [swap_later(None), swap_later(0), swap_later(1)]
    blocks, planes, made = gather_planes(normed, heads_of, beside, later)
    blocks_at = jnp.concatenate([plane * 4 + heads_made for plane in planes])
    made = [piece for round_made in made for piece in round_made]
    if groups > 1:
        qkv = assemble(made, blocks_at)
    ends = jnp.cumsum(lengths[0]).astype(jnp.int32)
    base = (group * (rows * HEADS)).astype(jnp.int32).reshape(1)
    shift, window = 0, None
    up = [(i, i + 1) for i in range(groups - 1)]
    down = [(i + 1, i) for i in range(groups - 1)]
    if groups > 1:
        margin = -(-LONG // rows)
        shift = margin * rows
        both = qkv[:, HEAD_DIM:]
        before = lax.ppermute(both[HEADS - margin :], "g", up)
        after = lax.ppermute(both[:margin], "g", down)
        window = jnp.concatenate([before, both, after], axis=0)
    if groups > 1:
        attended, log_total = attention_forward(ends, base, [qkv], None, window, shift)
    else:
        attended, log_total, qkv = attention_forward(ends, base, made, blocks_at, None, 0)
    attended, near_last = lax.optimization_barrier((attended, swap(blocks[2], "y")))
    near_blocks.append(near_last)
    fc2_part = share_cores(fc2_part, attended)
    fc1_full = join_fsdp(w_fc1, share_cores(fc1_part), attended)
    fc2_full = join_fsdp(w_fc2, fc2_part, attended)
    small = (b_out, ln2_gain, ln2_bias, b_fc1, b_fc2)
    packed, at, total = 0.0, 0, sum(vec.shape[0] for vec in small)
    for vec in small:
        packed += jnp.pad(vec, (at, total - at - vec.shape[0]))
        at += vec.shape[0]
    packed = join_small(tie(packed, normed))
    vectors, at = [], 0
    for vec in small:
        size = vec.shape[0]
        vectors.append(packed[:, at : at + size].reshape(-1).astype(f32))
        at += size
    out_bias, gain_two, bias_two, fc1_bias, fc2_bias = vectors
    mixed = lax.all_to_all(attended, SEQ, 0, 0, tiled=True).reshape(width, rows)

    branch = dot(mixed, out_full, 0, 0) + out_bias
    middle = hidden + tie(branch, fc2_full, qkv_part[0])
    normed_two_pre, scaled_two, inv_two = norm_forward(middle, gain_two, bias_two)
    normed_two = normed_two_pre.astype(low)
    inner_sum = dot(normed_two, fc1_full, 1, 0) + fc1_bias
    active, gelu_pull = jax.vjp(partial(jax.nn.gelu, approximate=True), inner_sum)
    active_low = active.astype(low)

    out_cot = out_grad[0]
    cot_full = out_cot.astype(f32)
    active_low, *qkv_part = lax.optimization_barrier((active_low, *qkv_part))
    qkv_part = share_cores(qkv_part)
    fc2_sum = WeightSum([(active_low, out_cot, 0)], scale)
    token = fc2_sum.other_core()
    active_grad = dot(tie(out_cot, token), fc2_full, 1, 1)
    inner_grad = gelu_pull(active_grad)[0].astype(low)
    near_blocks.append(swap(tie(blocks[3], fc2_full), "y"))
    token = fc2_sum.other_f(inner_grad, near_blocks[3])
    norm_two_grad = dot(tie(inner_grad, token), fc1_full, 1, 1)
    gain_two_grad, bias_two_grad, middle_from_norm = norm_backward(
        norm_two_grad, scaled_two, inv_two, gain_two
    )
    middle_grad = cot_full + middle_from_norm
    branch_grad = middle_grad.astype(low)
    mixed_grad = dot(out_full, branch_grad, 1, 1).astype(low)
    attended_grad = lax.all_to_all(
        mixed_grad.reshape(HEADS, HEAD_DIM, rows), SEQ, 0, 0, tiled=True
    )
    rest_sum = WeightSum([(normed_two, inner_grad, 0), (mixed, branch_grad, 1)], scale)
    token = rest_sum.other_core(mixed_grad)
    token = fc2_sum.near_y(token)
    token = rest_sum.other_f(token, *fc2_sum.far[1:])
    column = list(blocks)
    across = [swap(tie(block, mixed_grad), "c") for block in column + near_blocks]
    tokens = [token] + across

    plan = [
        [fc2_sum.near_z, rest_sum.near_y],
        [fc2_sum.far_z, rest_sum.near_z],
        [fc2_sum.back_near_z, rest_sum.far_z],
        [fc2_sum.back_y],
        [rest_sum.back_near_z, lambda *after: fc2_sum.near],
        [rest_sum.back_y],
    ]
    carried, first = None, 0
    for chunk in [HEADS] if groups > 1 else CHUNKS:
        results = attention_backward(
            ends, tie(base, *tokens), qkv, window, attended, attended_grad, log_total, shift,
            first, chunk, carried,
        )
        carried, first = results[::-1], first + chunk
        tokens = []
        for move in plan.pop(0):
            tokens.append(move(results[0], *tokens))
    for moves in plan:
        for move in moves:
            tokens.append(move(results[0]))
    head_grad, *window_grad = results
    if groups > 1:
        both = window_grad[0]
        inner = both[margin : margin + HEADS]
        before = lax.ppermute(both[:margin], "g", down)
        after = lax.ppermute(both[margin + HEADS :], "g", up)
        inner = inner.at[HEADS - margin :].add(before).at[:margin].add(after)
        head_grad = jnp.concatenate([head_grad, inner.astype(low)], axis=1)
    token_grad = lax.all_to_all(tie(head_grad, *tokens), SEQ, 0, 0, tiled=True)

    weight_part = head_weight(
        jnp.concatenate([jnp.stack(planes) * 4 + (place_in_plane ^ k) for k in (0, 2, 1, 3)]).astype(jnp.int32),
        head_grad,
        column + near_blocks + across,
    )
    weight_part = weight_part.reshape(3 * HEAD_DIM, parts, shard_rows).transpose(1, 0, 2)
    if parts == 2:
        weight_part = halve(weight_part, "f")
    else:
        weight_part = lax.psum_scatter(weight_part, "f", scatter_dimension=0, tiled=False)
    if groups > 1:
        weight_part = lax.psum(weight_part, "g")

    weight_part = (weight_part * scale).astype(low)
    qkv_full = join_fsdp(w_qkv, qkv_part, weight_part)
    (fc2_grad,) = fc2_sum.results(qkv_full)
    fc1_grad, out_weight_grad = rest_sum.results(fc2_grad)
    token_grad = tie(token_grad, fc1_grad, out_weight_grad)
    block_out = middle + (dot(tie(active_low, weight_part), fc2_full, 1, 0) + fc2_bias)
    hops = [weight_part] + [
        lax.ppermute(weight_part, "z", [(i, (i + k) % 4) for i in range(4)]) for k in range(1, 4)
    ]

    token_grad = (
        tie(token_grad, fc2_grad).reshape(HEADS, 3, HEAD_DIM, rows).transpose(1, 0, 2, 3).reshape(3 * width, rows)
    )
    norm_one_grad = dot(token_grad, qkv_full, 0, 1)
    gain_one_grad, bias_one_grad, hidden_from_norm = norm_backward(
        norm_one_grad, scaled_one, inv_one, gain_one
    )
    patch_grad = middle_grad + hidden_from_norm

    head_sums = jnp.sum(head_grad.astype(f32), axis=(0, 2))
    qv_grad = jnp.zeros((2 * width,), f32)
    qv_grad = lax.dynamic_update_slice(qv_grad, head_sums[:HEAD_DIM], (head * HEAD_DIM,))
    qv_grad = lax.dynamic_update_slice(
        qv_grad, head_sums[2 * HEAD_DIM :], (width + head * HEAD_DIM,)
    )
    late = VectorSum(
        (
            gain_one_grad,
            bias_one_grad,
            qv_grad,
            jnp.sum(branch_grad.astype(f32), axis=0),
            gain_two_grad,
            bias_two_grad,
            jnp.sum(inner_grad.astype(f32), axis=0),
            jnp.sum(cot_full, axis=0),
        ),
        scale,
    )
    hops = [tie(piece, gain_one_grad) for piece in hops]
    token = late.core()
    token = late.other_f(token)
    pieces = hops + [swap(piece, "y") for piece in hops]
    pieces += [swap(tie(piece, token), "c") for piece in pieces]
    token = late.near_y(token)
    token = late.near_z(token)
    late.far_z(token)
    firsts = lax.rem(z + 4 - jnp.arange(4, dtype=jnp.int32), 4) * 4
    near_places = [firsts + 2 * y + c, firsts + 2 * (1 - y) + c]
    places = jnp.concatenate(near_places + [place_at + 1 - 2 * c for place_at in near_places])
    qkv_weight_grad = weave(pieces, places)
    late.result()
    (
        ln1_gain_sum, ln1_bias_sum, qv_sum, out_bias_sum,
        ln2_gain_sum, ln2_bias_sum, fc1_bias_sum, fc2_bias_sum,
    ) = late.vectors()
    return (
        block_out.astype(low)[None],
        patch_grad[None],
        ln1_gain_sum,
        ln1_bias_sum,
        qkv_weight_grad,
        qv_sum,
        out_weight_grad,
        out_bias_sum,
        ln2_gain_sum,
        ln2_bias_sum,
        fc1_grad,
        fc1_bias_sum,
        fc2_grad,
        fc2_bias_sum,
    )


def solution(mesh):
    seq, parts = mesh.shape["seq"], mesh.shape["fsdp"]
    fine = Mesh(mesh.devices.reshape(seq // HEADS, HEADS // 4, 2, 2, parts), ("g", "z", "y", "c", "f"))
    rows = P("f", ("g",) + SEQ, None)
    vec, mat = P("f"), P("f", None)
    in_specs = (rows, rows, mat, rows, vec, vec, mat, vec, mat, vec, vec, vec, mat, vec, mat, vec)
    out_specs = (rows, rows, vec, vec, mat, vec, mat, vec, vec, vec, mat, vec, mat, vec)
    return jax.shard_map(body, mesh=fine, in_specs=in_specs, out_specs=out_specs, check_vma=False)
```

```python
import math
from functools import partial

import jax
import jax.numpy as jnp
from jax import lax
from jax.experimental import pallas as pl
from jax.experimental.pallas import tpu as pltpu
from jax.sharding import Mesh, PartitionSpec as P

HEADS = 16
LONG = 2304
NORM_EPS = 1e-06
CHUNKS = (2, 4, 3, 2, 3, 2)
HEAD_DIM = 64
BLOCK = 512
FAR = 1e30
QB = 512
KB = 512
HALF = 256
CALM_SCORE = 60.0
FORWARD_COST = 50_000_000_000
BACKWARD_COST = 75_000_000_000


def rows_dot(a, b):
    return lax.dot_general(a, b, (((1,), (0,)), ((), ())), preferred_element_type=jnp.float32)


def membership(ends_ref, count, first, width):
    place = first + lax.broadcasted_iota(jnp.int32, (16, width), 1)
    row = lax.broadcasted_iota(jnp.int32, (16, width), 0)
    low = jnp.zeros((16, width), jnp.int32)
    high = jnp.zeros((16, width), jnp.int32)
    for i in range(count):
        begin = ends_ref[i - 1] if i > 0 else 0
        low = jnp.where(row == i, begin, low)
        high = jnp.where(row == i, ends_ref[i], high)
    return jnp.where((place >= low) & (place < high), 1.0, 0.0)


def image_span(ends_ref, count, first, last):
    low = jnp.int32(0)
    high = ends_ref[count - 1]
    for i in range(count - 1):
        end = ends_ref[i]
        low = jnp.where(end <= first, end, low)
    for i in range(count - 2, -1, -1):
        end = ends_ref[i]
        high = jnp.where(end > last, end, high)
    return low, high


def over_keys(low, high, step, carry):
    def whole(j, carry):
        return step(pl.ds(pl.multiple_of((low + 2 * j) * HALF, HALF), KB), carry)

    def half(j, carry):
        return step(pl.ds(pl.multiple_of(j * HALF, HALF), HALF), carry)

    pairs = (high - low) // 2
    carry = lax.fori_loop(0, pairs, whole, carry)
    return lax.fori_loop(low + 2 * pairs, high, half, carry)


def split3(x):
    top = x.astype(jnp.bfloat16)
    rest = x - top.astype(jnp.float32)
    mid = rest.astype(jnp.bfloat16)
    low = (rest - mid.astype(jnp.float32)).astype(jnp.bfloat16)
    return [top.astype(jnp.float32), mid.astype(jnp.float32), low.astype(jnp.float32)]


def parts_of(ref):
    return [ref.at[:, i * HEAD_DIM : (i + 1) * HEAD_DIM, :] for i in range(ref.shape[1] // HEAD_DIM)]


def forward_kernel(count, shift, pieces, ends_ref, base_ref, *refs):
    if shift:
        own_ref, window_ref, o_ref, log_ref, qa, kn, va, peak = refs
        q_ref = parts_of(own_ref)[0]
        k_ref, v_ref = parts_of(window_ref)
    else:
        place_ref, *refs = refs
        made, (o_ref, log_ref, own_ref, qa, kn, va, peak) = refs[:pieces], refs[pieces:]
        for i in range(pieces):
            own_ref[place_ref[i]] = made[i][...]
        q_ref, k_ref, v_ref = parts_of(own_ref)
    peak[...] = jnp.zeros_like(peak)
    q_blocks = q_ref.shape[0]
    k_blocks = k_ref.shape[0]
    key_count = k_blocks * BLOCK
    base = base_ref[0]

    @pl.loop(0, k_blocks)
    def _(i):
        at = pl.ds(pl.multiple_of(i * BLOCK, BLOCK), BLOCK)
        away = (membership(ends_ref, count, base - shift + i * BLOCK, BLOCK) - 1.0) * FAR
        keys = k_ref[i].astype(jnp.float32)
        peak[1:2] = jnp.maximum(peak[1:2], jnp.sum(keys * keys, axis=0, keepdims=True))
        both = jnp.concatenate([keys, away], axis=0)
        kn[at, :] = both.T.astype(jnp.bfloat16)
        va[:, at] = jnp.concatenate(
            [v_ref[i].astype(jnp.float32), jnp.ones((16, BLOCK), jnp.float32)], axis=0
        ).astype(jnp.bfloat16)

    @pl.loop(0, q_blocks)
    def _(i):
        at = pl.ds(pl.multiple_of(i * BLOCK, BLOCK), BLOCK)
        inside = membership(ends_ref, count, base + i * BLOCK, BLOCK)
        asked = q_ref[i].astype(jnp.float32)
        peak[0:1] = jnp.maximum(peak[0:1], jnp.sum(asked * asked, axis=0, keepdims=True))
        qa[:, at] = jnp.concatenate(
            [asked * (HEAD_DIM ** -0.5), inside], axis=0
        ).astype(jnp.bfloat16)

    per = BLOCK // QB
    calm = CALM_SCORE * HEAD_DIM ** 0.5
    peaks = [jnp.max(peak[i : i + 1]) for i in range(2)]

    def span(i):
        first = base + i * QB
        low, high = image_span(ends_ref, count, first, first + QB - 1)
        low = jnp.maximum(low - base + shift, 0) // HALF
        return low, jnp.minimum(high - base + shift + HALF - 1, key_count) // HALF

    def finish(i, top, acc):
        total = acc[HEAD_DIM : HEAD_DIM + 1]
        o_ref[i // per, :, pl.ds(pl.multiple_of((i % per) * QB, QB), QB)] = (
            acc[:HEAD_DIM] / total
        ).astype(jnp.bfloat16)
        log_ref[:, pl.ds(pl.multiple_of(i * QB, QB), QB)] = top + jnp.log(total)

    small = peaks[0] * peaks[1] <= calm * calm

    @pl.when(small)
    def _():
        @pl.loop(0, q_blocks * per)
        def _(i):
            q_part = qa[:, pl.ds(pl.multiple_of(i * QB, QB), QB)]

            def step(at, acc):
                weights = jnp.exp(rows_dot(kn[at, :], q_part)).astype(jnp.bfloat16)
                return acc + rows_dot(va[:, at], weights)

            finish(i, 0.0, over_keys(*span(i), step, jnp.zeros((HEAD_DIM + 16, QB), jnp.float32)))

    @pl.when(jnp.logical_not(small))
    def _():
        @pl.loop(0, q_blocks * per)
        def _(i):
            q_part = qa[:, pl.ds(pl.multiple_of(i * QB, QB), QB)]

            def step(at, carry):
                top, acc = carry
                scores = rows_dot(kn[at, :], q_part)
                new_top = jnp.maximum(top, jnp.max(scores, axis=0, keepdims=True))
                weights = jnp.exp(scores - new_top).astype(jnp.bfloat16)
                acc = acc * jnp.exp(top - new_top) + rows_dot(va[:, at], weights)
                return new_top, acc

            start = (
                jnp.full((1, QB), -3e38, jnp.float32),
                jnp.zeros((HEAD_DIM + 16, QB), jnp.float32),
            )
            finish(i, *over_keys(*span(i), step, start))


def backward_kernel(count, shift, first_block, chunk, last, ends_ref, base_ref, own_ref, *refs):
    q_ref, k_ref, v_ref = parts_of(own_ref)
    if shift:
        k_ref, v_ref = parts_of(refs[0])
        refs = refs[1:]
    o_ref, do_ref, log_ref, *refs = refs
    if first_block > 0:
        sums_in, _, *refs = refs
    grad_ref, *refs = refs
    sums_out = None
    if shift:
        window_ref, *refs = refs
    if not last:
        sums_out, *refs = refs
    qa, da, kn, vn, qn, dn, ks, sums, dq_part, sums_sem, dq_sem, *refs = refs
    k_blocks = k_ref.shape[0]
    key_count = k_blocks * BLOCK
    base = base_ref[0]
    scale = HEAD_DIM ** -0.5
    start = base + first_block * BLOCK
    low, high = image_span(ends_ref, count, start, start + chunk * BLOCK - 1)
    low = jnp.maximum(low - base + shift, 0) // BLOCK
    high = jnp.minimum(high - base + shift + BLOCK - 1, key_count) // BLOCK
    held_low, held_high = (0, k_blocks) if last or first_block == 0 else (low, high)

    def block_at(i):
        return pl.ds(pl.multiple_of(i * BLOCK, BLOCK), BLOCK)

    if first_block > 0:

        @pl.loop(held_low, held_high)
        def _(i):
            pltpu.make_async_copy(sums_in.at[block_at(i)], sums.at[block_at(i)], sums_sem.at[i]).start()

    else:
        sums[...] = jnp.zeros_like(sums)

    @pl.loop(low, high)
    def _(i):
        at = block_at(i)
        away = (membership(ends_ref, count, base - shift + i * BLOCK, BLOCK) - 1.0) * FAR
        ones = jnp.ones((16, BLOCK), jnp.float32)
        keys = k_ref[i].astype(jnp.float32)
        kn[at, :] = jnp.concatenate([keys, away, ones], axis=0).T.astype(jnp.bfloat16)
        vn[at, :] = jnp.concatenate([v_ref[i].astype(jnp.float32), ones], axis=0).T.astype(jnp.bfloat16)
        ks[:, at] = (keys * scale).astype(jnp.bfloat16)

    @pl.loop(0, chunk)
    def _(i):
        at = block_at(i)
        block = first_block + i
        inside = membership(ends_ref, count, base + block * BLOCK, BLOCK)
        pad = jnp.zeros((13, BLOCK), jnp.float32)
        scaled = q_ref[block].astype(jnp.float32) * scale
        qn[at, :] = scaled.T.astype(jnp.bfloat16)
        qa[:, at] = jnp.concatenate(
            [scaled, inside] + split3(-log_ref[:, block_at(block)]) + [pad], axis=0
        ).astype(jnp.bfloat16)
        grads = do_ref[block].astype(jnp.float32)
        row_dot = jnp.sum(grads * o_ref[block].astype(jnp.float32), axis=0, keepdims=True)
        dn[at, :] = grads.T.astype(jnp.bfloat16)
        da[:, at] = jnp.concatenate([grads] + split3(-row_dot) + [pad], axis=0).astype(jnp.bfloat16)

    if first_block > 0:

        @pl.loop(held_low, held_high)
        def _(i):
            pltpu.make_async_copy(sums_in.at[block_at(i)], sums.at[block_at(i)], sums_sem.at[i]).wait()

    @pl.loop(0, chunk)
    def _(i):
        q_at = block_at(i)
        q_part = qa[:, q_at]
        d_part = da[:, q_at]
        q_rows = qn[q_at, :]
        d_rows = dn[q_at, :]
        first = start + i * BLOCK
        key_low, key_high = image_span(ends_ref, count, first, first + BLOCK - 1)
        key_low = jnp.maximum(key_low - base + shift, 0) // HALF
        key_high = jnp.minimum(key_high - base + shift + HALF - 1, key_count) // HALF

        def step(at, dq):
            probs = jnp.exp(rows_dot(kn[at, :], q_part))
            score_grad = (probs * rows_dot(vn[at, :], d_part)).astype(jnp.bfloat16)
            sums[at, 0:HEAD_DIM] += rows_dot(score_grad, q_rows)
            sums[at, HEAD_DIM : 2 * HEAD_DIM] += rows_dot(probs.astype(jnp.bfloat16), d_rows)
            return dq + rows_dot(ks[:, at], score_grad)

        dq = over_keys(key_low, key_high, step, jnp.zeros((HEAD_DIM, BLOCK), jnp.float32))
        dq_part[i] = dq.astype(jnp.bfloat16)

    def query_copy(i):
        return pltpu.make_async_copy(
            dq_part.at[i], grad_ref.at[first_block + i, 0:HEAD_DIM], dq_sem.at[i]
        )

    for i in range(chunk):
        query_copy(i).start()
    if not last:

        @pl.loop(held_low, held_high)
        def _(i):
            pltpu.make_async_copy(sums.at[block_at(i)], sums_out.at[block_at(i)], sums_sem.at[i]).start()

        @pl.loop(held_low, held_high)
        def _(i):
            pltpu.make_async_copy(sums.at[block_at(i)], sums_out.at[block_at(i)], sums_sem.at[i]).wait()

    elif shift:

        @pl.loop(0, k_blocks)
        def _(i):
            window_ref[i] = sums[block_at(i), :].T

    else:
        kv_part, kv_sem = refs

        def key_copy(i):
            return pltpu.make_async_copy(
                kv_part.at[i], grad_ref.at[i, HEAD_DIM : 3 * HEAD_DIM], kv_sem.at[i]
            )

        @pl.loop(0, k_blocks)
        def _(i):
            kv_part[i] = sums[block_at(i), :].T.astype(jnp.bfloat16)
            key_copy(i).start()

        @pl.loop(0, k_blocks)
        def _(i):
            key_copy(i).wait()

    for i in range(chunk):
        query_copy(i).wait()


def vmem_spec():
    return pl.BlockSpec(memory_space=pltpu.VMEM)


def smem_spec():
    return pl.BlockSpec(memory_space=pltpu.SMEM)


def attention_forward(ends, base, made, places, window, shift):
    blocks = made[0].shape[0] if shift else len(made)
    tokens, keys = blocks * BLOCK, blocks * BLOCK + 2 * shift
    low = jnp.bfloat16
    out_shape = [
        jax.ShapeDtypeStruct((blocks, HEAD_DIM, BLOCK), low),
        jax.ShapeDtypeStruct((1, tokens), jnp.float32),
    ]
    if shift:
        arrays, in_specs = [*made, window], [smem_spec()] * 2 + [vmem_spec()] * 2
    else:
        arrays, in_specs = [places, *made], [smem_spec()] * 3 + [vmem_spec()] * blocks
        out_shape.append(jax.ShapeDtypeStruct((blocks, 3 * HEAD_DIM, BLOCK), low))
    return pl.pallas_call(
        partial(forward_kernel, ends.shape[0], shift, blocks),
        out_shape=out_shape,
        in_specs=in_specs,
        out_specs=[vmem_spec()] * len(out_shape),
        scratch_shapes=[
            pltpu.VMEM((HEAD_DIM + 16, tokens), low),
            pltpu.VMEM((keys, HEAD_DIM + 16), low),
            pltpu.VMEM((HEAD_DIM + 16, keys), low),
            pltpu.VMEM((8, BLOCK), jnp.float32),
        ],
        compiler_params=pltpu.CompilerParams(vmem_limit_bytes=48 * 1024 * 1024),
        cost_estimate=pl.CostEstimate(
            flops=FORWARD_COST, bytes_accessed=tokens * 512, transcendentals=0
        ),
    )(ends, base, *arrays)


def attention_backward(ends, base, own, window, o, do, log, shift, first_block, chunk, carried):
    blocks = own.shape[0]
    tokens, keys = chunk * BLOCK, blocks * BLOCK + 2 * shift
    last = first_block + chunk == blocks
    low, f32 = jnp.bfloat16, jnp.float32
    arrays = [own] + ([window] if shift else []) + [o, do, log]
    in_specs = [smem_spec(), smem_spec()] + [vmem_spec()] * len(arrays)
    out_shape = [jax.ShapeDtypeStruct((blocks, HEAD_DIM if shift else 3 * HEAD_DIM, BLOCK), low)]
    out_specs = [any_spec()]
    aliases = {}
    if carried is not None:
        place_at = 2 + len(arrays)
        arrays += list(carried)
        in_specs += [any_spec(), any_spec()]
        aliases = {place_at + 1: 0}
        if not last:
            aliases[place_at] = 1
    if shift:
        out_shape.append(jax.ShapeDtypeStruct((keys // BLOCK, 2 * HEAD_DIM, BLOCK), f32))
        out_specs.append(vmem_spec())
    if not last:
        out_shape.append(jax.ShapeDtypeStruct((keys, 2 * HEAD_DIM), f32))
        out_specs.append(any_spec())
    scratch = [
        pltpu.VMEM((HEAD_DIM + 32, tokens), low),
        pltpu.VMEM((HEAD_DIM + 16, tokens), low),
        pltpu.VMEM((keys, HEAD_DIM + 32), low),
        pltpu.VMEM((keys, HEAD_DIM + 16), low),
        pltpu.VMEM((tokens, HEAD_DIM), low),
        pltpu.VMEM((tokens, HEAD_DIM), low),
        pltpu.VMEM((HEAD_DIM, keys), low),
        pltpu.VMEM((keys, 2 * HEAD_DIM), f32),
        pltpu.VMEM((chunk, HEAD_DIM, BLOCK), low),
        pltpu.SemaphoreType.DMA((keys // BLOCK,)),
        pltpu.SemaphoreType.DMA((chunk,)),
    ]
    if last and not shift:
        scratch += [
            pltpu.VMEM((blocks, 2 * HEAD_DIM, BLOCK), low),
            pltpu.SemaphoreType.DMA((blocks,)),
        ]
    return pl.pallas_call(
        partial(backward_kernel, ends.shape[0], shift, first_block, chunk, last),
        out_shape=out_shape,
        in_specs=in_specs,
        out_specs=out_specs,
        scratch_shapes=scratch,
        input_output_aliases=aliases,
        compiler_params=pltpu.CompilerParams(vmem_limit_bytes=50 * 1024 * 1024),
        cost_estimate=pl.CostEstimate(flops=BACKWARD_COST * chunk // blocks, bytes_accessed=tokens * 1024, transcendentals=0),
    )(ends, base, *arrays)


def any_spec():
    return pl.BlockSpec(memory_space=pl.ANY)


def block_rows(rows, cols):
    while rows * cols > 512 * 1024 and rows % 16 == 0:
        rows //= 2
    return rows


def take_kernel(at_ref, in_ref, out_ref):
    out_ref[...] = in_ref[...]


def take(x, index, count):
    rows, cols = x.shape[0] // count, x.shape[1]
    size = block_rows(rows, cols)
    steps = rows // size
    return pl.pallas_call(
        take_kernel,
        out_shape=jax.ShapeDtypeStruct((rows, cols), x.dtype),
        grid_spec=pltpu.PrefetchScalarGridSpec(
            num_scalar_prefetch=1,
            grid=(steps,),
            in_specs=[pl.BlockSpec((size, cols), lambda j, at_ref: (at_ref[0] * steps + j, 0))],
            out_specs=pl.BlockSpec((size, cols), lambda j, at_ref: (j, 0)),
        ),
        cost_estimate=pl.CostEstimate(flops=0, bytes_accessed=2 * rows * cols * x.dtype.itemsize, transcendentals=0),
    )(index.astype(jnp.int32).reshape(1), x)


def place_kernel(owner, row_ref, col_ref, *refs):
    out_ref = refs[-1]
    for i, piece in enumerate(owner):

        @pl.when(pl.program_id(0) == i)
        def _(piece=piece):
            out_ref[...] = refs[piece][...].astype(out_ref.dtype)


def place(pieces, row_at, col_at, dtype, rows, shape, cols=None, block=0):
    cols = cols or pieces[0].shape[1]
    owner = [n for n, piece in enumerate(pieces) for _ in range(piece.shape[0] // rows)]
    count = len(owner)
    size = block_rows(rows, cols)
    steps = rows // size

    def piece_map(piece):
        turns = [i for i in range(count) if owner[i] == piece]
        first, last = turns[0], turns[-1]

        def index(s, j, row_ref, col_ref):
            inside = j + (s - first) * steps
            end = (last - first + 1) * steps - 1
            return (jnp.where(s < first, 0, jnp.where(s > last, end, inside)), block)

        return index

    return pl.pallas_call(
        partial(place_kernel, owner),
        out_shape=jax.ShapeDtypeStruct(shape, dtype),
        grid_spec=pltpu.PrefetchScalarGridSpec(
            num_scalar_prefetch=2,
            grid=(count, steps),
            in_specs=[pl.BlockSpec((size, cols), piece_map(i)) for i in range(len(pieces))],
            out_specs=pl.BlockSpec(
                (size, cols), lambda s, j, row_ref, col_ref: (row_ref[s] * steps + j, col_ref[s])
            ),
        ),
        cost_estimate=pl.CostEstimate(
            flops=0,
            bytes_accessed=count * rows * cols * (2 + jnp.dtype(dtype).itemsize),
            transcendentals=0,
        ),
    )(row_at, col_at, *pieces)


def plane_columns_kernel(plane_ref, q_ref, k_ref, v_ref, out_ref):
    for part, ref in enumerate((q_ref, k_ref, v_ref)):
        cols = ref[...].astype(jnp.float32).T
        for j in range(4):
            at = (3 * j + part) * HEAD_DIM
            out_ref[at : at + HEAD_DIM] = cols[j * HEAD_DIM : (j + 1) * HEAD_DIM].astype(out_ref.dtype)


def plane_columns(w, plane):
    rows = w.shape[0]

    def spec(part):
        return pl.BlockSpec((rows, 4 * HEAD_DIM), lambda i, plane_ref: (0, part * (HEADS // 4) + plane_ref[0]))

    return pl.pallas_call(
        plane_columns_kernel,
        out_shape=jax.ShapeDtypeStruct((12 * HEAD_DIM, rows), w.dtype),
        grid_spec=pltpu.PrefetchScalarGridSpec(
            num_scalar_prefetch=1,
            grid=(1,),
            in_specs=[spec(part) for part in range(3)],
            out_specs=pl.BlockSpec((12 * HEAD_DIM, rows), lambda i, plane_ref: (0, 0)),
        ),
    )(plane.astype(jnp.int32).reshape(1), w, w, w)


def project_kernel(head_ref, w_ref, bias_ref, block_ref, *out_refs):
    size = w_ref.shape[2]
    rows = 3 * HEAD_DIM
    for i, out_ref in enumerate(out_refs):
        at = pl.ds(pl.multiple_of(head_ref[i] * rows, HEAD_DIM), rows)
        total = bias_ref[at, :]
        for f in range(w_ref.shape[0]):
            total += lax.dot_general(
                w_ref[f, at, :], block_ref[:, f * size : (f + 1) * size], (((1,), (1,)), ((), ())),
                preferred_element_type=jnp.float32,
            )
        out_ref[...] = total.astype(jnp.bfloat16)


def project(heads, w, bias, block):
    rows, width = block.shape
    count = heads.shape[0]
    shape = jax.ShapeDtypeStruct((3 * HEAD_DIM, rows), jnp.bfloat16)
    return pl.pallas_call(
        project_kernel,
        out_shape=[shape] * count,
        in_specs=[smem_spec()] + [vmem_spec()] * 3,
        out_specs=[vmem_spec()] * count,
        compiler_params=pltpu.CompilerParams(vmem_limit_bytes=24 * 1024 * 1024),
        cost_estimate=pl.CostEstimate(
            flops=6 * count * rows * width * 3 * HEAD_DIM, bytes_accessed=rows * width * 2, transcendentals=0
        ),
    )(heads, w, bias, block)


def assemble_kernel(count, place_ref, *refs):
    pieces, out_ref, sem = refs[:count], refs[count], refs[count + 1]

    def copy(i):
        return pltpu.make_async_copy(pieces[i], out_ref.at[place_ref[i]], sem.at[i])

    for i in range(count):
        copy(i).start()
    for i in range(count):
        copy(i).wait()


def assemble(pieces, places):
    count = len(pieces)
    return pl.pallas_call(
        partial(assemble_kernel, count),
        out_shape=jax.ShapeDtypeStruct((count,) + pieces[0].shape, pieces[0].dtype),
        in_specs=[smem_spec()] + [vmem_spec()] * count,
        out_specs=any_spec(),
        scratch_shapes=[pltpu.SemaphoreType.DMA((count,))],
        compiler_params=pltpu.CompilerParams(vmem_limit_bytes=16 * 1024 * 1024),
        cost_estimate=pl.CostEstimate(
            flops=0, bytes_accessed=4 * count * pieces[0].size, transcendentals=0
        ),
    )(places, *pieces)


SLOTS = 4


def head_weight_kernel(count, place_ref, grad_ref, *refs):
    blocks, (out_ref, held, sem) = refs[:count], refs[count:]

    def copy(b):
        return pltpu.make_async_copy(blocks[b], held.at[b % SLOTS], sem.at[b % SLOTS])

    for b in range(SLOTS - 1):
        copy(b).start()
    out_ref[...] = jnp.zeros_like(out_ref)

    @pl.loop(0, count)
    def _(i):
        slot = lax.rem(i, SLOTS)
        pltpu.make_async_copy(blocks[0], held.at[slot], sem.at[slot]).wait()
        for b in range(SLOTS - 1, count):

            @pl.when(i + SLOTS - 1 == b)
            def _(b=b):
                copy(b).start()

        out_ref[...] += rows_dot(grad_ref[place_ref[i]], held[slot])


def head_weight(places, grad, blocks):
    count = len(blocks)
    rows, width = blocks[0].shape
    cols = grad.shape[1]
    return pl.pallas_call(
        partial(head_weight_kernel, count),
        out_shape=jax.ShapeDtypeStruct((cols, width), jnp.float32),
        in_specs=[smem_spec(), vmem_spec()] + [any_spec()] * count,
        out_specs=vmem_spec(),
        scratch_shapes=[
            pltpu.VMEM((SLOTS, rows, width), jnp.bfloat16),
            pltpu.SemaphoreType.DMA((SLOTS,)),
        ],
        compiler_params=pltpu.CompilerParams(vmem_limit_bytes=24 * 1024 * 1024),
        cost_estimate=pl.CostEstimate(flops=4 * count * rows * width * cols, bytes_accessed=count * rows * width * 2, transcendentals=0),
    )(places, grad, *blocks)


def weave_kernel(count, at_ref, *refs):
    pieces, (out_ref, held) = refs[:count], refs[count:]
    for i in range(count):
        held[at_ref[i]] = pieces[i][...]
    for part in range(3):
        for pair in range(count // 2):
            rows = slice(part * HEAD_DIM, (part + 1) * HEAD_DIM)
            both = jnp.concatenate([held[2 * pair, rows], held[2 * pair + 1, rows]], axis=0)
            at = (part * count + 2 * pair) * HEAD_DIM
            out_ref[:, at : at + 2 * HEAD_DIM] = both.astype(jnp.float32).T


def weave(pieces, places):
    count = len(pieces)
    cols, rows = pieces[0].shape
    size = 128
    return pl.pallas_call(
        partial(weave_kernel, count),
        out_shape=jax.ShapeDtypeStruct((rows, count * cols), jnp.float32),
        grid_spec=pltpu.PrefetchScalarGridSpec(
            num_scalar_prefetch=1,
            grid=(rows // size,),
            in_specs=[pl.BlockSpec((cols, size), lambda i, at_ref: (0, i))] * count,
            out_specs=pl.BlockSpec((size, count * cols), lambda i, at_ref: (i, 0)),
            scratch_shapes=[pltpu.VMEM((count, cols, size), pieces[0].dtype)],
        ),
        cost_estimate=pl.CostEstimate(
            flops=0, bytes_accessed=6 * count * cols * rows, transcendentals=0
        ),
    )(places, *pieces)


SEQ = ("z", "y", "c")
SWAP = ((0, 1), (1, 0))


def norm_forward(hidden, gain_vec, offset_vec):
    centre = hidden - jnp.mean(hidden, axis=-1, keepdims=True)
    spread = jnp.mean(centre * centre, axis=-1, keepdims=True)
    inv_std = lax.rsqrt(spread + NORM_EPS)
    scaled = centre * inv_std
    return (scaled * gain_vec + offset_vec, scaled, inv_std)


def norm_backward(grad_out, scaled, inv_std, gain_vec):
    gain_grad = jnp.sum(grad_out * scaled, axis=0)
    offset_grad = jnp.sum(grad_out, axis=0)
    grad_scaled = grad_out * gain_vec
    grad_in = inv_std * (
        grad_scaled
        - jnp.mean(grad_scaled, axis=-1, keepdims=True)
        - scaled * jnp.mean(grad_scaled * scaled, axis=-1, keepdims=True)
    )
    return (gain_grad, offset_grad, grad_in)


def dot(a, b, a_dim, b_dim):
    return lax.dot_general(
        a, b, (((a_dim,), (b_dim,)), ((), ())), preferred_element_type=jnp.float32
    )


def tie(x, *others):
    others = [other for other in others if other is not None]
    return lax.optimization_barrier((x, *others))[0] if others else x


def linear(start, first, a, second, b):
    start, first, second = (jnp.array(x, jnp.int32) for x in (start, first, second))
    return start + first * a + second * b


def pick(x, i, axis=0):
    return lax.dynamic_index_in_dim(x, i, axis, keepdims=False)


def swap(x, axis):
    return lax.ppermute(x, axis, SWAP)


def in_order(own, other, position):
    return jnp.where(position == 0, jnp.stack([own, other]), jnp.stack([other, own]))


def fetch_fsdp(shard, pieces, *others):
    if lax.axis_size("f") != 2:
        return [], [lax.all_gather(shard, "f", axis=0, tiled=True)]
    first = lax.axis_index("c") * pieces
    shard = tie(shard, *others)
    taken = [take(shard, first + i, 2 * pieces) for i in range(pieces)]
    return taken, [swap(part, "f") for part in taken]


def share_cores(fetched, *others):
    if lax.axis_size("f") != 2:
        return fetched
    return fetched + [swap(tie(piece, *others), "c") for piece in fetched]


def join_fsdp(shard, pieces, *others):
    if lax.axis_size("f") != 2:
        return pieces[0]
    core, here = lax.axis_index("c"), lax.axis_index("f")
    count = len(pieces) // 2
    step = range(count)
    at = linear(
        (*range(2 * count), *(2 * count + i for i in step), *(3 * count + i for i in step)),
        (2 * count,) * (2 * count) + (-2 * count,) * (2 * count),
        here,
        (0,) * (2 * count) + (count,) * count + (-count,) * count,
        core,
    )
    rows, cols = shard.shape
    return place(
        [tie(shard, *others), *pieces], at, jnp.zeros_like(at), shard.dtype, rows // (2 * count), (2 * rows, cols)
    )


def join_small(shard):
    if lax.axis_size("f") != 2:
        return lax.all_gather(shard, "f", axis=0, tiled=False)
    return in_order(shard, swap(shard, "f"), lax.axis_index("f"))


def halve(x, axis, pairs=SWAP, here=None):
    here = lax.axis_index(axis) if here is None else here
    got = lax.ppermute(pick(x, 1 - here), axis, pairs)
    return pick(x, here).astype(jnp.float32) + got.astype(jnp.float32)


def plane_pairs(bit):
    return [(i, i ^ bit) for i in range(4)]


class WeightSum:
    def __init__(self, terms, scale):
        self.terms, self.scale = terms, scale
        self.widths = [right.shape[1] // 2 for _, right, _ in terms]
        self.cols = sum(self.widths)
        self.rows = terms[0][0].shape[1 - terms[0][2]] // lax.axis_size("f")

    def after(self, others):
        self.terms = [(left, tie(right, *others), dim) for left, right, dim in self.terms]

    def term(self, n, c, f, half=None):
        left, right, dim = self.terms[n]
        rows, start = self.rows, f * self.rows
        if half is not None:
            rows //= 2
            start = start + half * rows
        left = lax.dynamic_slice_in_dim(left, start, rows, 1 - dim)
        right = lax.dynamic_slice_in_dim(right, c * self.widths[n], self.widths[n], 1)
        return dot(left, right, dim, 0)

    def joined(self, parts):
        parts = [part.astype(jnp.bfloat16) for part in parts]
        return parts[0] if len(parts) == 1 else jnp.concatenate(parts, axis=1)

    def half_of(self, x, half):
        rows = x.shape[0] // 2
        return lax.dynamic_slice_in_dim(x, half * rows, rows, 0).astype(jnp.float32)

    def other_core(self, *others):
        self.after(others)
        core, parts, here = lax.axis_index("c"), lax.axis_size("f"), lax.axis_index("f")
        order = [1 - here, here] if parts == 2 else range(parts)
        self.got = []
        for f in order:
            sent = [self.term(n, 1 - core, f).astype(jnp.bfloat16) for n in range(len(self.terms))]
            self.got.append([swap(part, "c") for part in sent])
        return sent[-1]

    def other_f(self, *others):
        self.after(others)
        core, parts, here = lax.axis_index("c"), lax.axis_size("f"), lax.axis_index("f")
        y, count = lax.axis_index("y"), range(len(self.terms))
        if parts == 2:
            self.far = []
            for half in (1 - y, y):
                sent = self.joined(
                    [self.term(n, core, 1 - here, half) + self.half_of(self.got[0][n], half) for n in count]
                )
                self.far.append(swap(sent, "f"))
                self.after([sent])
            return sent
        total = [
            self.joined([self.term(n, core, f) + self.got[f][n].astype(jnp.float32) for n in count])
            for f in range(parts)
        ]
        self.far = []
        self.total = lax.psum_scatter(jnp.stack(total), "f", scatter_dimension=0, tiled=False)
        return self.total

    def here_half(self, k, half):
        core, parts, here = lax.axis_index("c"), lax.axis_size("f"), lax.axis_index("f")
        if parts != 2:
            return [self.half_of(self.total, half)]
        x, at = [], 0
        for n, width in enumerate(self.widths):
            total = self.term(n, core, here, half) + self.half_of(self.got[1][n], half)
            x.append(total + self.far[k][:, at : at + width].astype(jnp.float32))
            at += width
        return x

    def near_y(self, *others):
        self.after(others)
        sent = self.joined(self.here_half(0, 1 - lax.axis_index("y")))
        self.coming = lax.ppermute(sent, "y", SWAP)
        return sent

    def near_z(self, *others):
        self.coming = tie(self.coming, *others)
        self.after(others)
        x, at = [], 0
        for part in self.here_half(1, lax.axis_index("y")):
            width = part.shape[1]
            x.append(part + self.coming[:, at : at + width].astype(jnp.float32))
            at += width
        x = self.joined(x).reshape(2, -1, self.cols)
        low_z = lax.rem(lax.axis_index("z"), 2)
        sent = pick(x, 1 - low_z)
        self.kept, self.coming = pick(x, low_z), lax.ppermute(sent, "z", plane_pairs(1))
        return sent

    def added(self, x, others):
        return x.astype(jnp.float32) + tie(self.coming, *others).astype(jnp.float32)

    def far_z(self, *others):
        self.x = self.added(self.kept, others).astype(jnp.bfloat16)
        self.coming = lax.ppermute(self.x, "z", plane_pairs(2))
        return self.x

    def back_near_z(self, *others):
        x = self.added(self.x, others)
        if lax.axis_size("g") > 1:
            x = lax.psum(x, "g")
        self.x = (x * self.scale).astype(jnp.bfloat16)
        self.coming = lax.ppermute(self.x, "z", plane_pairs(1))
        return self.x

    def back_y(self, *others):
        coming = tie(self.coming, *others)
        x = in_order(self.x, coming, lax.rem(lax.axis_index("z"), 2)).reshape(-1, self.cols)
        self.near = lax.ppermute(x, "y", SWAP)
        self.x, self.across = x, swap(x, "c")
        return x

    def results(self, *others):
        y, c = lax.axis_index("y"), lax.axis_index("c")
        near = tie(self.near, *others)
        pieces = [self.x, near, self.across, swap(near, "c")]
        row_at = linear((0, 1, 0, 1), (1, -1, 1, -1), y, (0, 0, 0, 0), c)
        col_at = linear((0, 0, 1, 1), (0, 0, 0, 0), y, (1, 1, -1, -1), c)
        rows, at, results = pieces[0].shape[0], 0, []
        for width in self.widths:
            results.append(
                place(
                    pieces, row_at, col_at, jnp.float32, rows, (2 * rows, 2 * width), width, at // width
                )
            )
            at += width
        return results


class VectorSum:
    def __init__(self, vectors, scale):
        self.sizes = [vec.shape[0] // lax.axis_size("f") for vec in vectors]
        self.x = jnp.concatenate([vec.reshape(lax.axis_size("f"), -1) for vec in vectors], axis=1) * scale

    def core(self, *others):
        self.x = tie(self.x, *others)
        self.coming = swap(self.x, "c")
        return self.x

    def other_f(self, *others):
        x = self.x + tie(self.coming, *others)
        if lax.axis_size("f") == 2:
            here = lax.axis_index("f")
            self.x, sent = pick(x, here), pick(x, 1 - here)
            self.coming = swap(sent, "f")
            return sent
        self.x = lax.psum_scatter(x, "f", scatter_dimension=0, tiled=False)
        self.coming = jnp.zeros_like(self.x)
        return self.x

    def hop(self, axis, pairs, others):
        self.x = self.x + tie(self.coming, *others)
        self.coming = lax.ppermute(self.x, axis, pairs)
        return self.x

    def near_y(self, *others):
        return self.hop("y", SWAP, others)

    def near_z(self, *others):
        return self.hop("z", plane_pairs(1), others)

    def far_z(self, *others):
        return self.hop("z", plane_pairs(2), others)

    def result(self, *others):
        self.total = self.x + tie(self.coming, *others)
        if lax.axis_size("g") > 1:
            self.total = lax.psum(self.total, "g")
        return self.total

    def vectors(self):
        at = 0
        for size in self.sizes:
            yield self.total[at : at + size]
            at += size


def arrivals(count):
    table = []
    for z in range(count):
        hops = []
        for t in range(1, count):
            if z - t >= 0:
                hops.append(("up", t))
            if z + t < count:
                hops.append(("down", t))
        table.append(hops)
    return table


def gather_planes(x, use, beside, later):
    z = lax.axis_index("z")
    count = lax.axis_size("z")
    table = arrivals(count)
    up, down = x, x
    hops = {}
    blocks, planes, used = [x], [z], []
    for t in range(1, count):
        up = lax.ppermute(up, "z", [(i, i + 1) for i in range(t - 1, count - 1)])
        down = lax.ppermute(down, "z", [(i, i - 1) for i in range(1, count - t + 1)])
        made = use(blocks[-1])
        before = used.pop() if used else []
        up, down, before, made[0], extra, _ = lax.optimization_barrier(
            (up, down, before, made[0], later[t - 1](blocks), beside[t - 1])
        )
        later[t - 1](blocks, extra)
        used += [before] * (t > 1) + [made]
        hops["up", t], hops["down", t] = up, down
        names = sorted({table[i][t - 1] for i in range(count)})
        block, plane = None, z
        for name in names:
            here = [i for i in range(count) if table[i][t - 1] == name]
            chosen = (z >= here[0]) & (z <= here[-1])
            block = hops[name] if block is None else jnp.where(chosen, hops[name], block)
            plane = jnp.where(chosen, z + (-name[1] if name[0] == "up" else name[1]), plane)
        blocks.append(block)
        planes.append(plane)
    used.append(use(blocks[-1]))
    return blocks, planes, used


def body(
    patches, pos_embed, lengths, out_grad,
    ln1_gain, ln1_bias, w_qkv, b_qv, w_out, b_out,
    ln2_gain, ln2_bias, w_fc1, b_fc1, w_fc2, b_fc2,
):
    f32, low = jnp.float32, jnp.bfloat16
    rows, width = patches.shape[1:]
    groups, parts = lax.axis_size("g"), lax.axis_size("f")
    head = lax.axis_index(SEQ)
    group = lax.axis_index("g")
    shard_index = lax.axis_index("f")
    scale = 1.0 / (parts * math.sqrt(rows * HEADS * groups))

    gain_one, bias_one, qv_bias = (
        join_small(vec).reshape(-1).astype(f32) for vec in (ln1_gain, ln1_bias, b_qv)
    )
    hidden = patches[0].astype(f32) + pos_embed[0].astype(f32)
    normed_pre, scaled_one, inv_one = norm_forward(hidden, gain_one, bias_one)
    normed = normed_pre.astype(low)

    shard_rows = w_qkv.shape[0]
    z, y, c = (lax.axis_index(axis) for axis in SEQ)
    place_in_plane = 2 * y + c
    plane_weights = join_small(plane_columns(tie(w_qkv, gain_one, bias_one, qv_bias), z)).reshape(parts, 12 * HEAD_DIM, shard_rows)
    q_bias, v_bias = (
        lax.dynamic_slice_in_dim(qv_bias, at + z * 4 * HEAD_DIM, 4 * HEAD_DIM).reshape(4, HEAD_DIM)
        for at in (0, width)
    )
    plane_bias = jnp.concatenate([q_bias, jnp.zeros((4, HEAD_DIM), f32), v_bias], axis=1).reshape(-1, 1)
    others = jnp.array([0, 1, 2, 3], jnp.int32)
    heads_made = others ^ place_in_plane

    def heads_of(block):
        own, core, near, far = project(heads_made, plane_weights, plane_bias, block)
        return [
            own, swap(core, "c"), swap(near, "y"),
            lax.ppermute(far, ("y", "c"), [(i, 3 - i) for i in range(4)]),
        ]

    out_taken, out_part = fetch_fsdp(w_out, 1, normed)
    fc1_taken, fc1_part = fetch_fsdp(w_fc1, 2, normed)
    fc2_taken, fc2_part = fetch_fsdp(w_fc2, 2, normed)
    if parts == 2:
        fc2_part = [swap(tie(part, fc1_part[1]), "f") for part in fc2_taken]
    qkv_taken, qkv_part = fetch_fsdp(w_qkv, 2, normed)
    out_full = join_fsdp(w_out, share_cores(out_part))
    beside = [
        out_taken + fc1_taken + fc2_taken + qkv_taken, out_part, fc1_part[:1] + [out_full],
    ]
    near_blocks = []

    def swap_later(first):
        def step(blocks, done=None):
            if done is None:
                return [swap(blocks[first], "y")] if first is not None else []
            near_blocks.extend(done)

        return step

    later = [swap_later(None), swap_later(0), swap_later(1)]
    blocks, planes, made = gather_planes(normed, heads_of, beside, later)
    blocks_at = jnp.concatenate([plane * 4 + heads_made for plane in planes])
    made = [piece for round_made in made for piece in round_made]
    if groups > 1:
        qkv = assemble(made, blocks_at)
    ends = jnp.cumsum(lengths[0]).astype(jnp.int32)
    base = (group * (rows * HEADS)).astype(jnp.int32).reshape(1)
    shift, window = 0, None
    up = [(i, i + 1) for i in range(groups - 1)]
    down = [(i + 1, i) for i in range(groups - 1)]
    if groups > 1:
        margin = -(-LONG // rows)
        shift = margin * rows
        both = qkv[:, HEAD_DIM:]
        before = lax.ppermute(both[HEADS - margin :], "g", up)
        after = lax.ppermute(both[:margin], "g", down)
        window = jnp.concatenate([before, both, after], axis=0)
    if groups > 1:
        attended, log_total = attention_forward(ends, base, [qkv], None, window, shift)
    else:
        attended, log_total, qkv = attention_forward(ends, base, made, blocks_at, None, 0)
    attended, near_last = lax.optimization_barrier((attended, swap(blocks[2], "y")))
    near_blocks.append(near_last)
    fc2_part = share_cores(fc2_part, attended)
    fc1_full = join_fsdp(w_fc1, share_cores(fc1_part), attended)
    fc2_full = join_fsdp(w_fc2, fc2_part, attended)
    small = (b_out, ln2_gain, ln2_bias, b_fc1, b_fc2)
    packed, at, total = 0.0, 0, sum(vec.shape[0] for vec in small)
    for vec in small:
        packed += jnp.pad(vec, (at, total - at - vec.shape[0]))
        at += vec.shape[0]
    packed = join_small(tie(packed, normed))
    vectors, at = [], 0
    for vec in small:
        size = vec.shape[0]
        vectors.append(packed[:, at : at + size].reshape(-1).astype(f32))
        at += size
    out_bias, gain_two, bias_two, fc1_bias, fc2_bias = vectors
    mixed = lax.all_to_all(attended, SEQ, 0, 0, tiled=True).reshape(width, rows)

    branch = dot(mixed, out_full, 0, 0) + out_bias
    middle = hidden + tie(branch, fc2_full, qkv_part[0])
    normed_two_pre, scaled_two, inv_two = norm_forward(middle, gain_two, bias_two)
    normed_two = normed_two_pre.astype(low)
    inner_sum = dot(normed_two, fc1_full, 1, 0) + fc1_bias
    active, gelu_pull = jax.vjp(partial(jax.nn.gelu, approximate=True), inner_sum)
    active_low = active.astype(low)

    out_cot = out_grad[0]
    cot_full = out_cot.astype(f32)
    active_low, *qkv_part = lax.optimization_barrier((active_low, *qkv_part))
    qkv_part = share_cores(qkv_part)
    fc2_sum = WeightSum([(active_low, out_cot, 0)], scale)
    token = fc2_sum.other_core()
    active_grad = dot(tie(out_cot, token), fc2_full, 1, 1)
    inner_grad = gelu_pull(active_grad)[0].astype(low)
    near_blocks.append(swap(tie(blocks[3], fc2_full), "y"))
    token = fc2_sum.other_f(inner_grad, near_blocks[3])
    norm_two_grad = dot(tie(inner_grad, token), fc1_full, 1, 1)
    gain_two_grad, bias_two_grad, middle_from_norm = norm_backward(
        norm_two_grad, scaled_two, inv_two, gain_two
    )
    middle_grad = cot_full + middle_from_norm
    branch_grad = middle_grad.astype(low)
    mixed_grad = dot(out_full, branch_grad, 1, 1).astype(low)
    attended_grad = lax.all_to_all(
        mixed_grad.reshape(HEADS, HEAD_DIM, rows), SEQ, 0, 0, tiled=True
    )
    rest_sum = WeightSum([(normed_two, inner_grad, 0), (mixed, branch_grad, 1)], scale)
    token = rest_sum.other_core(mixed_grad)
    token = fc2_sum.near_y(token)
    token = rest_sum.other_f(token, *fc2_sum.far[1:])
    column = list(blocks)
    across = [swap(tie(block, mixed_grad), "c") for block in column + near_blocks]
    tokens = [token] + across

    plan = [
        [fc2_sum.near_z, rest_sum.near_y],
        [fc2_sum.far_z, rest_sum.near_z],
        [fc2_sum.back_near_z, rest_sum.far_z],
        [fc2_sum.back_y],
        [rest_sum.back_near_z, lambda *after: fc2_sum.near],
        [rest_sum.back_y],
    ]
    carried, first = None, 0
    for chunk in [HEADS] if groups > 1 else CHUNKS:
        results = attention_backward(
            ends, tie(base, *tokens), qkv, window, attended, attended_grad, log_total, shift,
            first, chunk, carried,
        )
        carried, first = results[::-1], first + chunk
        tokens = []
        for move in plan.pop(0):
            tokens.append(move(results[0], *tokens))
    for moves in plan:
        for move in moves:
            tokens.append(move(results[0]))
    head_grad, *window_grad = results
    if groups > 1:
        both = window_grad[0]
        inner = both[margin : margin + HEADS]
        before = lax.ppermute(both[:margin], "g", down)
        after = lax.ppermute(both[margin + HEADS :], "g", up)
        inner = inner.at[HEADS - margin :].add(before).at[:margin].add(after)
        head_grad = jnp.concatenate([head_grad, inner.astype(low)], axis=1)
    token_grad = lax.all_to_all(tie(head_grad, *tokens), SEQ, 0, 0, tiled=True)

    weight_part = head_weight(
        jnp.concatenate([jnp.stack(planes) * 4 + (place_in_plane ^ k) for k in (0, 2, 1, 3)]).astype(jnp.int32),
        head_grad,
        column + near_blocks + across,
    )
    block_out = dot(tie(active_low, weight_part), fc2_full, 1, 0) + fc2_bias
    block_out = (middle + block_out).astype(low)
    weight_part = weight_part.reshape(3 * HEAD_DIM, parts, shard_rows).transpose(1, 0, 2)
    if parts == 2:
        weight_part = halve(weight_part, "f")
    else:
        weight_part = lax.psum_scatter(weight_part, "f", scatter_dimension=0, tiled=False)
    if groups > 1:
        weight_part = lax.psum(weight_part, "g")

    weight_part = (weight_part * scale).astype(low)
    qkv_full = join_fsdp(w_qkv, qkv_part, weight_part, block_out)
    (fc2_grad,) = fc2_sum.results(qkv_full)
    fc1_grad, out_weight_grad = rest_sum.results(fc2_grad)
    hops = [weight_part] + [
        lax.ppermute(weight_part, "z", [(i, (i + k) % 4) for i in range(4)]) for k in range(1, 4)
    ]
    token_grad, fc1_grad, out_weight_grad, *hops = lax.optimization_barrier(
        (token_grad, fc1_grad, out_weight_grad, *hops)
    )

    token_grad = (
        tie(token_grad, fc2_grad).reshape(HEADS, 3, HEAD_DIM, rows).transpose(1, 0, 2, 3).reshape(3 * width, rows)
    )
    norm_one_grad = dot(token_grad, qkv_full, 0, 1)
    gain_one_grad, bias_one_grad, hidden_from_norm = norm_backward(
        norm_one_grad, scaled_one, inv_one, gain_one
    )
    patch_grad = middle_grad + hidden_from_norm

    head_sums = jnp.sum(head_grad.astype(f32), axis=(0, 2))
    qv_grad = jnp.zeros((2 * width,), f32)
    qv_grad = lax.dynamic_update_slice(qv_grad, head_sums[:HEAD_DIM], (head * HEAD_DIM,))
    qv_grad = lax.dynamic_update_slice(
        qv_grad, head_sums[2 * HEAD_DIM :], (width + head * HEAD_DIM,)
    )
    late = VectorSum(
        (
            gain_one_grad,
            bias_one_grad,
            qv_grad,
            jnp.sum(branch_grad.astype(f32), axis=0),
            gain_two_grad,
            bias_two_grad,
            jnp.sum(inner_grad.astype(f32), axis=0),
            jnp.sum(cot_full, axis=0),
        ),
        scale,
    )
    token = late.core()
    token = late.other_f(token)
    pieces = hops + [swap(piece, "y") for piece in hops]
    pieces += [swap(tie(piece, gain_one_grad), "c") for piece in pieces]
    token = late.near_y(token)
    token = late.near_z(token)
    late.far_z(token)
    firsts = lax.rem(z + 4 - jnp.arange(4, dtype=jnp.int32), 4) * 4
    near_places = [firsts + 2 * y + c, firsts + 2 * (1 - y) + c]
    places = jnp.concatenate(near_places + [place_at + 1 - 2 * c for place_at in near_places])
    qkv_weight_grad = weave(pieces, places)
    late.result()
    (
        ln1_gain_sum, ln1_bias_sum, qv_sum, out_bias_sum,
        ln2_gain_sum, ln2_bias_sum, fc1_bias_sum, fc2_bias_sum,
    ) = late.vectors()
    return (
        block_out[None],
        patch_grad[None],
        ln1_gain_sum,
        ln1_bias_sum,
        qkv_weight_grad,
        qv_sum,
        out_weight_grad,
        out_bias_sum,
        ln2_gain_sum,
        ln2_bias_sum,
        fc1_grad,
        fc1_bias_sum,
        fc2_grad,
        fc2_bias_sum,
    )


def solution(mesh):
    seq, parts = mesh.shape["seq"], mesh.shape["fsdp"]
    fine = Mesh(mesh.devices.reshape(seq // HEADS, HEADS // 4, 2, 2, parts), ("g", "z", "y", "c", "f"))
    rows = P("f", ("g",) + SEQ, None)
    vec, mat = P("f"), P("f", None)
    in_specs = (rows, rows, mat, rows, vec, vec, mat, vec, mat, vec, vec, vec, mat, vec, mat, vec)
    out_specs = (rows, rows, vec, vec, mat, vec, mat, vec, vec, vec, mat, vec, mat, vec)
    return jax.shard_map(body, mesh=fine, in_specs=in_specs, out_specs=out_specs, check_vma=False)
```

```python
import math
from functools import partial

import jax
import jax.numpy as jnp
from jax import lax
from jax.experimental import pallas as pl
from jax.experimental.pallas import tpu as pltpu
from jax.sharding import Mesh, PartitionSpec as P

HEADS = 16
LONG = 2304
NORM_EPS = 1e-06
CHUNKS = (3, 4, 4, 3, 2)
HEAD_DIM = 64
BLOCK = 512
FAR = 1e30
QB = 512
KB = 512
HALF = 256
CALM_SCORE = 60.0
FORWARD_COST = 50_000_000_000
BACKWARD_COST = 75_000_000_000


def rows_dot(a, b):
    return lax.dot_general(a, b, (((1,), (0,)), ((), ())), preferred_element_type=jnp.float32)


def membership(ends_ref, count, first, width):
    place = first + lax.broadcasted_iota(jnp.int32, (16, width), 1)
    row = lax.broadcasted_iota(jnp.int32, (16, width), 0)
    low = jnp.zeros((16, width), jnp.int32)
    high = jnp.zeros((16, width), jnp.int32)
    for i in range(count):
        begin = ends_ref[i - 1] if i > 0 else 0
        low = jnp.where(row == i, begin, low)
        high = jnp.where(row == i, ends_ref[i], high)
    return jnp.where((place >= low) & (place < high), 1.0, 0.0)


def image_span(ends_ref, count, first, last):
    low = jnp.int32(0)
    high = ends_ref[count - 1]
    for i in range(count - 1):
        end = ends_ref[i]
        low = jnp.where(end <= first, end, low)
    for i in range(count - 2, -1, -1):
        end = ends_ref[i]
        high = jnp.where(end > last, end, high)
    return low, high


def over_keys(low, high, step, carry):
    def whole(j, carry):
        return step(pl.ds(pl.multiple_of((low + 2 * j) * HALF, HALF), KB), carry)

    def half(j, carry):
        return step(pl.ds(pl.multiple_of(j * HALF, HALF), HALF), carry)

    pairs = (high - low) // 2
    carry = lax.fori_loop(0, pairs, whole, carry)
    return lax.fori_loop(low + 2 * pairs, high, half, carry)


def split3(x):
    top = x.astype(jnp.bfloat16)
    rest = x - top.astype(jnp.float32)
    mid = rest.astype(jnp.bfloat16)
    low = (rest - mid.astype(jnp.float32)).astype(jnp.bfloat16)
    return [top.astype(jnp.float32), mid.astype(jnp.float32), low.astype(jnp.float32)]


def parts_of(ref):
    return [ref.at[:, i * HEAD_DIM : (i + 1) * HEAD_DIM, :] for i in range(ref.shape[1] // HEAD_DIM)]


def forward_kernel(count, shift, pieces, ends_ref, base_ref, *refs):
    if shift:
        own_ref, window_ref, o_ref, log_ref, qa, kn, va, peak = refs
        q_ref = parts_of(own_ref)[0]
        k_ref, v_ref = parts_of(window_ref)
    else:
        place_ref, *refs = refs
        made, (o_ref, log_ref, own_ref, qa, kn, va, peak) = refs[:pieces], refs[pieces:]
        for i in range(pieces):
            own_ref[place_ref[i]] = made[i][...]
        q_ref, k_ref, v_ref = parts_of(own_ref)
    peak[...] = jnp.zeros_like(peak)
    q_blocks = q_ref.shape[0]
    k_blocks = k_ref.shape[0]
    key_count = k_blocks * BLOCK
    base = base_ref[0]

    @pl.loop(0, k_blocks)
    def _(i):
        at = pl.ds(pl.multiple_of(i * BLOCK, BLOCK), BLOCK)
        away = (membership(ends_ref, count, base - shift + i * BLOCK, BLOCK) - 1.0) * FAR
        keys = k_ref[i].astype(jnp.float32)
        peak[1:2] = jnp.maximum(peak[1:2], jnp.sum(keys * keys, axis=0, keepdims=True))
        both = jnp.concatenate([keys, away], axis=0)
        kn[at, :] = both.T.astype(jnp.bfloat16)
        va[:, at] = jnp.concatenate(
            [v_ref[i].astype(jnp.float32), jnp.ones((16, BLOCK), jnp.float32)], axis=0
        ).astype(jnp.bfloat16)

    @pl.loop(0, q_blocks)
    def _(i):
        at = pl.ds(pl.multiple_of(i * BLOCK, BLOCK), BLOCK)
        inside = membership(ends_ref, count, base + i * BLOCK, BLOCK)
        asked = q_ref[i].astype(jnp.float32)
        peak[0:1] = jnp.maximum(peak[0:1], jnp.sum(asked * asked, axis=0, keepdims=True))
        qa[:, at] = jnp.concatenate(
            [asked * (HEAD_DIM ** -0.5), inside], axis=0
        ).astype(jnp.bfloat16)

    per = BLOCK // QB
    calm = CALM_SCORE * HEAD_DIM ** 0.5
    peaks = [jnp.max(peak[i : i + 1]) for i in range(2)]

    def span(i):
        first = base + i * QB
        low, high = image_span(ends_ref, count, first, first + QB - 1)
        low = jnp.maximum(low - base + shift, 0) // HALF
        return low, jnp.minimum(high - base + shift + HALF - 1, key_count) // HALF

    def finish(i, top, acc):
        total = acc[HEAD_DIM : HEAD_DIM + 1]
        o_ref[i // per, :, pl.ds(pl.multiple_of((i % per) * QB, QB), QB)] = (
            acc[:HEAD_DIM] / total
        ).astype(jnp.bfloat16)
        log_ref[:, pl.ds(pl.multiple_of(i * QB, QB), QB)] = top + jnp.log(total)

    small = peaks[0] * peaks[1] <= calm * calm

    @pl.when(small)
    def _():
        @pl.loop(0, q_blocks * per)
        def _(i):
            q_part = qa[:, pl.ds(pl.multiple_of(i * QB, QB), QB)]

            def step(at, acc):
                weights = jnp.exp(rows_dot(kn[at, :], q_part)).astype(jnp.bfloat16)
                return acc + rows_dot(va[:, at], weights)

            finish(i, 0.0, over_keys(*span(i), step, jnp.zeros((HEAD_DIM + 16, QB), jnp.float32)))

    @pl.when(jnp.logical_not(small))
    def _():
        @pl.loop(0, q_blocks * per)
        def _(i):
            q_part = qa[:, pl.ds(pl.multiple_of(i * QB, QB), QB)]

            def step(at, carry):
                top, acc = carry
                scores = rows_dot(kn[at, :], q_part)
                new_top = jnp.maximum(top, jnp.max(scores, axis=0, keepdims=True))
                weights = jnp.exp(scores - new_top).astype(jnp.bfloat16)
                acc = acc * jnp.exp(top - new_top) + rows_dot(va[:, at], weights)
                return new_top, acc

            start = (
                jnp.full((1, QB), -3e38, jnp.float32),
                jnp.zeros((HEAD_DIM + 16, QB), jnp.float32),
            )
            finish(i, *over_keys(*span(i), step, start))


def backward_kernel(count, shift, first_block, chunk, last, ends_ref, base_ref, own_ref, *refs):
    q_ref, k_ref, v_ref = parts_of(own_ref)
    if shift:
        k_ref, v_ref = parts_of(refs[0])
        refs = refs[1:]
    o_ref, do_ref, log_ref, *refs = refs
    if first_block > 0:
        sums_in, _, *refs = refs
    grad_ref, *refs = refs
    sums_out = None
    if shift:
        window_ref, *refs = refs
    if not last:
        sums_out, *refs = refs
    qa, da, kn, vn, qn, dn, ks, sums, dq_part, sums_sem, dq_sem, *refs = refs
    k_blocks = k_ref.shape[0]
    key_count = k_blocks * BLOCK
    base = base_ref[0]
    scale = HEAD_DIM ** -0.5
    start = base + first_block * BLOCK
    low, high = image_span(ends_ref, count, start, start + chunk * BLOCK - 1)
    low = jnp.maximum(low - base + shift, 0) // BLOCK
    high = jnp.minimum(high - base + shift + BLOCK - 1, key_count) // BLOCK
    held_low, held_high = (0, k_blocks) if last or first_block == 0 else (low, high)

    def block_at(i):
        return pl.ds(pl.multiple_of(i * BLOCK, BLOCK), BLOCK)

    if first_block > 0:

        @pl.loop(held_low, held_high)
        def _(i):
            pltpu.make_async_copy(sums_in.at[block_at(i)], sums.at[block_at(i)], sums_sem.at[i]).start()

    else:
        sums[...] = jnp.zeros_like(sums)

    @pl.loop(low, high)
    def _(i):
        at = block_at(i)
        away = (membership(ends_ref, count, base - shift + i * BLOCK, BLOCK) - 1.0) * FAR
        ones = jnp.ones((16, BLOCK), jnp.float32)
        keys = k_ref[i].astype(jnp.float32)
        kn[at, :] = jnp.concatenate([keys, away, ones], axis=0).T.astype(jnp.bfloat16)
        vn[at, :] = jnp.concatenate([v_ref[i].astype(jnp.float32), ones], axis=0).T.astype(jnp.bfloat16)
        ks[:, at] = (keys * scale).astype(jnp.bfloat16)

    @pl.loop(0, chunk)
    def _(i):
        at = block_at(i)
        block = first_block + i
        inside = membership(ends_ref, count, base + block * BLOCK, BLOCK)
        pad = jnp.zeros((13, BLOCK), jnp.float32)
        scaled = q_ref[block].astype(jnp.float32) * scale
        qn[at, :] = scaled.T.astype(jnp.bfloat16)
        qa[:, at] = jnp.concatenate(
            [scaled, inside] + split3(-log_ref[:, block_at(block)]) + [pad], axis=0
        ).astype(jnp.bfloat16)
        grads = do_ref[block].astype(jnp.float32)
        row_dot = jnp.sum(grads * o_ref[block].astype(jnp.float32), axis=0, keepdims=True)
        dn[at, :] = grads.T.astype(jnp.bfloat16)
        da[:, at] = jnp.concatenate([grads] + split3(-row_dot) + [pad], axis=0).astype(jnp.bfloat16)

    if first_block > 0:

        @pl.loop(held_low, held_high)
        def _(i):
            pltpu.make_async_copy(sums_in.at[block_at(i)], sums.at[block_at(i)], sums_sem.at[i]).wait()

    @pl.loop(0, chunk)
    def _(i):
        q_at = block_at(i)
        q_part = qa[:, q_at]
        d_part = da[:, q_at]
        q_rows = qn[q_at, :]
        d_rows = dn[q_at, :]
        first = start + i * BLOCK
        key_low, key_high = image_span(ends_ref, count, first, first + BLOCK - 1)
        key_low = jnp.maximum(key_low - base + shift, 0) // HALF
        key_high = jnp.minimum(key_high - base + shift + HALF - 1, key_count) // HALF

        def step(at, dq):
            probs = jnp.exp(rows_dot(kn[at, :], q_part))
            score_grad = (probs * rows_dot(vn[at, :], d_part)).astype(jnp.bfloat16)
            sums[at, 0:HEAD_DIM] += rows_dot(score_grad, q_rows)
            sums[at, HEAD_DIM : 2 * HEAD_DIM] += rows_dot(probs.astype(jnp.bfloat16), d_rows)
            return dq + rows_dot(ks[:, at], score_grad)

        dq = over_keys(key_low, key_high, step, jnp.zeros((HEAD_DIM, BLOCK), jnp.float32))
        dq_part[i] = dq.astype(jnp.bfloat16)

    def query_copy(i):
        return pltpu.make_async_copy(
            dq_part.at[i], grad_ref.at[first_block + i, 0:HEAD_DIM], dq_sem.at[i]
        )

    for i in range(chunk):
        query_copy(i).start()
    if not last:

        @pl.loop(held_low, held_high)
        def _(i):
            pltpu.make_async_copy(sums.at[block_at(i)], sums_out.at[block_at(i)], sums_sem.at[i]).start()

        @pl.loop(held_low, held_high)
        def _(i):
            pltpu.make_async_copy(sums.at[block_at(i)], sums_out.at[block_at(i)], sums_sem.at[i]).wait()

    elif shift:

        @pl.loop(0, k_blocks)
        def _(i):
            window_ref[i] = sums[block_at(i), :].T

    else:
        kv_part, kv_sem = refs

        def key_copy(i):
            return pltpu.make_async_copy(
                kv_part.at[i], grad_ref.at[i, HEAD_DIM : 3 * HEAD_DIM], kv_sem.at[i]
            )

        @pl.loop(0, k_blocks)
        def _(i):
            kv_part[i] = sums[block_at(i), :].T.astype(jnp.bfloat16)
            key_copy(i).start()

        @pl.loop(0, k_blocks)
        def _(i):
            key_copy(i).wait()

    for i in range(chunk):
        query_copy(i).wait()


def vmem_spec():
    return pl.BlockSpec(memory_space=pltpu.VMEM)


def smem_spec():
    return pl.BlockSpec(memory_space=pltpu.SMEM)


def attention_forward(ends, base, made, places, window, shift):
    blocks = made[0].shape[0] if shift else len(made)
    tokens, keys = blocks * BLOCK, blocks * BLOCK + 2 * shift
    low = jnp.bfloat16
    out_shape = [
        jax.ShapeDtypeStruct((blocks, HEAD_DIM, BLOCK), low),
        jax.ShapeDtypeStruct((1, tokens), jnp.float32),
    ]
    if shift:
        arrays, in_specs = [*made, window], [smem_spec()] * 2 + [vmem_spec()] * 2
    else:
        arrays, in_specs = [places, *made], [smem_spec()] * 3 + [vmem_spec()] * blocks
        out_shape.append(jax.ShapeDtypeStruct((blocks, 3 * HEAD_DIM, BLOCK), low))
    return pl.pallas_call(
        partial(forward_kernel, ends.shape[0], shift, blocks),
        out_shape=out_shape,
        in_specs=in_specs,
        out_specs=[vmem_spec()] * len(out_shape),
        scratch_shapes=[
            pltpu.VMEM((HEAD_DIM + 16, tokens), low),
            pltpu.VMEM((keys, HEAD_DIM + 16), low),
            pltpu.VMEM((HEAD_DIM + 16, keys), low),
            pltpu.VMEM((8, BLOCK), jnp.float32),
        ],
        compiler_params=pltpu.CompilerParams(vmem_limit_bytes=48 * 1024 * 1024),
        cost_estimate=pl.CostEstimate(
            flops=FORWARD_COST, bytes_accessed=tokens * 512, transcendentals=0
        ),
    )(ends, base, *arrays)


def attention_backward(ends, base, own, window, o, do, log, shift, first_block, chunk, carried):
    blocks = own.shape[0]
    tokens, keys = chunk * BLOCK, blocks * BLOCK + 2 * shift
    last = first_block + chunk == blocks
    low, f32 = jnp.bfloat16, jnp.float32
    arrays = [own] + ([window] if shift else []) + [o, do, log]
    in_specs = [smem_spec(), smem_spec()] + [vmem_spec()] * len(arrays)
    out_shape = [jax.ShapeDtypeStruct((blocks, HEAD_DIM if shift else 3 * HEAD_DIM, BLOCK), low)]
    out_specs = [any_spec()]
    aliases = {}
    if carried is not None:
        place_at = 2 + len(arrays)
        arrays += list(carried)
        in_specs += [any_spec(), any_spec()]
        aliases = {place_at + 1: 0}
        if not last:
            aliases[place_at] = 1
    if shift:
        out_shape.append(jax.ShapeDtypeStruct((keys // BLOCK, 2 * HEAD_DIM, BLOCK), f32))
        out_specs.append(vmem_spec())
    if not last:
        out_shape.append(jax.ShapeDtypeStruct((keys, 2 * HEAD_DIM), f32))
        out_specs.append(any_spec())
    scratch = [
        pltpu.VMEM((HEAD_DIM + 32, tokens), low),
        pltpu.VMEM((HEAD_DIM + 16, tokens), low),
        pltpu.VMEM((keys, HEAD_DIM + 32), low),
        pltpu.VMEM((keys, HEAD_DIM + 16), low),
        pltpu.VMEM((tokens, HEAD_DIM), low),
        pltpu.VMEM((tokens, HEAD_DIM), low),
        pltpu.VMEM((HEAD_DIM, keys), low),
        pltpu.VMEM((keys, 2 * HEAD_DIM), f32),
        pltpu.VMEM((chunk, HEAD_DIM, BLOCK), low),
        pltpu.SemaphoreType.DMA((keys // BLOCK,)),
        pltpu.SemaphoreType.DMA((chunk,)),
    ]
    if last and not shift:
        scratch += [
            pltpu.VMEM((blocks, 2 * HEAD_DIM, BLOCK), low),
            pltpu.SemaphoreType.DMA((blocks,)),
        ]
    return pl.pallas_call(
        partial(backward_kernel, ends.shape[0], shift, first_block, chunk, last),
        out_shape=out_shape,
        in_specs=in_specs,
        out_specs=out_specs,
        scratch_shapes=scratch,
        input_output_aliases=aliases,
        compiler_params=pltpu.CompilerParams(vmem_limit_bytes=50 * 1024 * 1024),
        cost_estimate=pl.CostEstimate(flops=BACKWARD_COST * chunk // blocks, bytes_accessed=tokens * 1024, transcendentals=0),
    )(ends, base, *arrays)


def any_spec():
    return pl.BlockSpec(memory_space=pl.ANY)


def block_rows(rows, cols):
    while rows * cols > 512 * 1024 and rows % 16 == 0:
        rows //= 2
    return rows


def take_kernel(at_ref, in_ref, out_ref):
    out_ref[...] = in_ref[...]


def take(x, index, count):
    rows, cols = x.shape[0] // count, x.shape[1]
    size = block_rows(rows, cols)
    steps = rows // size
    return pl.pallas_call(
        take_kernel,
        out_shape=jax.ShapeDtypeStruct((rows, cols), x.dtype),
        grid_spec=pltpu.PrefetchScalarGridSpec(
            num_scalar_prefetch=1,
            grid=(steps,),
            in_specs=[pl.BlockSpec((size, cols), lambda j, at_ref: (at_ref[0] * steps + j, 0))],
            out_specs=pl.BlockSpec((size, cols), lambda j, at_ref: (j, 0)),
        ),
        cost_estimate=pl.CostEstimate(flops=0, bytes_accessed=2 * rows * cols * x.dtype.itemsize, transcendentals=0),
    )(index.astype(jnp.int32).reshape(1), x)


def place_kernel(owner, row_ref, col_ref, *refs):
    out_ref = refs[-1]
    for i, piece in enumerate(owner):

        @pl.when(pl.program_id(0) == i)
        def _(piece=piece):
            out_ref[...] = refs[piece][...].astype(out_ref.dtype)


def place(pieces, row_at, col_at, dtype, rows, shape, cols=None, block=0):
    cols = cols or pieces[0].shape[1]
    owner = [n for n, piece in enumerate(pieces) for _ in range(piece.shape[0] // rows)]
    count = len(owner)
    size = block_rows(rows, cols)
    steps = rows // size

    def piece_map(piece):
        turns = [i for i in range(count) if owner[i] == piece]
        first, last = turns[0], turns[-1]

        def index(s, j, row_ref, col_ref):
            inside = j + (s - first) * steps
            end = (last - first + 1) * steps - 1
            return (jnp.where(s < first, 0, jnp.where(s > last, end, inside)), block)

        return index

    return pl.pallas_call(
        partial(place_kernel, owner),
        out_shape=jax.ShapeDtypeStruct(shape, dtype),
        grid_spec=pltpu.PrefetchScalarGridSpec(
            num_scalar_prefetch=2,
            grid=(count, steps),
            in_specs=[pl.BlockSpec((size, cols), piece_map(i)) for i in range(len(pieces))],
            out_specs=pl.BlockSpec(
                (size, cols), lambda s, j, row_ref, col_ref: (row_ref[s] * steps + j, col_ref[s])
            ),
        ),
        cost_estimate=pl.CostEstimate(
            flops=0,
            bytes_accessed=count * rows * cols * (2 + jnp.dtype(dtype).itemsize),
            transcendentals=0,
        ),
    )(row_at, col_at, *pieces)


def plane_columns_kernel(plane_ref, q_ref, k_ref, v_ref, out_ref):
    for part, ref in enumerate((q_ref, k_ref, v_ref)):
        cols = ref[...].astype(jnp.float32).T
        for j in range(4):
            at = (3 * j + part) * HEAD_DIM
            out_ref[at : at + HEAD_DIM] = cols[j * HEAD_DIM : (j + 1) * HEAD_DIM].astype(out_ref.dtype)


def plane_columns(w, plane):
    rows = w.shape[0]

    def spec(part):
        return pl.BlockSpec((rows, 4 * HEAD_DIM), lambda i, plane_ref: (0, part * (HEADS // 4) + plane_ref[0]))

    return pl.pallas_call(
        plane_columns_kernel,
        out_shape=jax.ShapeDtypeStruct((12 * HEAD_DIM, rows), w.dtype),
        grid_spec=pltpu.PrefetchScalarGridSpec(
            num_scalar_prefetch=1,
            grid=(1,),
            in_specs=[spec(part) for part in range(3)],
            out_specs=pl.BlockSpec((12 * HEAD_DIM, rows), lambda i, plane_ref: (0, 0)),
        ),
    )(plane.astype(jnp.int32).reshape(1), w, w, w)


def project_kernel(head_ref, w_ref, bias_ref, block_ref, *out_refs):
    size = w_ref.shape[2]
    rows = 3 * HEAD_DIM
    for i, out_ref in enumerate(out_refs):
        at = pl.ds(pl.multiple_of(head_ref[i] * rows, HEAD_DIM), rows)
        total = bias_ref[at, :]
        for f in range(w_ref.shape[0]):
            total += lax.dot_general(
                w_ref[f, at, :], block_ref[:, f * size : (f + 1) * size], (((1,), (1,)), ((), ())),
                preferred_element_type=jnp.float32,
            )
        out_ref[...] = total.astype(jnp.bfloat16)


def project(heads, w, bias, block):
    rows, width = block.shape
    count = heads.shape[0]
    shape = jax.ShapeDtypeStruct((3 * HEAD_DIM, rows), jnp.bfloat16)
    return pl.pallas_call(
        project_kernel,
        out_shape=[shape] * count,
        in_specs=[smem_spec()] + [vmem_spec()] * 3,
        out_specs=[vmem_spec()] * count,
        compiler_params=pltpu.CompilerParams(vmem_limit_bytes=24 * 1024 * 1024),
        cost_estimate=pl.CostEstimate(
            flops=6 * count * rows * width * 3 * HEAD_DIM, bytes_accessed=rows * width * 2, transcendentals=0
        ),
    )(heads, w, bias, block)


def assemble_kernel(count, place_ref, *refs):
    pieces, out_ref, sem = refs[:count], refs[count], refs[count + 1]

    def copy(i):
        return pltpu.make_async_copy(pieces[i], out_ref.at[place_ref[i]], sem.at[i])

    for i in range(count):
        copy(i).start()
    for i in range(count):
        copy(i).wait()


def assemble(pieces, places):
    count = len(pieces)
    return pl.pallas_call(
        partial(assemble_kernel, count),
        out_shape=jax.ShapeDtypeStruct((count,) + pieces[0].shape, pieces[0].dtype),
        in_specs=[smem_spec()] + [vmem_spec()] * count,
        out_specs=any_spec(),
        scratch_shapes=[pltpu.SemaphoreType.DMA((count,))],
        compiler_params=pltpu.CompilerParams(vmem_limit_bytes=16 * 1024 * 1024),
        cost_estimate=pl.CostEstimate(
            flops=0, bytes_accessed=4 * count * pieces[0].size, transcendentals=0
        ),
    )(places, *pieces)


SLOTS = 4


def head_weight_kernel(count, place_ref, grad_ref, *refs):
    blocks, (out_ref, held, sem) = refs[:count], refs[count:]

    def copy(b):
        return pltpu.make_async_copy(blocks[b], held.at[b % SLOTS], sem.at[b % SLOTS])

    for b in range(SLOTS - 1):
        copy(b).start()
    out_ref[...] = jnp.zeros_like(out_ref)

    @pl.loop(0, count)
    def _(i):
        slot = lax.rem(i, SLOTS)
        pltpu.make_async_copy(blocks[0], held.at[slot], sem.at[slot]).wait()
        for b in range(SLOTS - 1, count):

            @pl.when(i + SLOTS - 1 == b)
            def _(b=b):
                copy(b).start()

        out_ref[...] += rows_dot(grad_ref[place_ref[i]], held[slot])


def head_weight(places, grad, blocks):
    count = len(blocks)
    rows, width = blocks[0].shape
    cols = grad.shape[1]
    return pl.pallas_call(
        partial(head_weight_kernel, count),
        out_shape=jax.ShapeDtypeStruct((cols, width), jnp.float32),
        in_specs=[smem_spec(), vmem_spec()] + [any_spec()] * count,
        out_specs=vmem_spec(),
        scratch_shapes=[
            pltpu.VMEM((SLOTS, rows, width), jnp.bfloat16),
            pltpu.SemaphoreType.DMA((SLOTS,)),
        ],
        compiler_params=pltpu.CompilerParams(vmem_limit_bytes=24 * 1024 * 1024),
        cost_estimate=pl.CostEstimate(flops=4 * count * rows * width * cols, bytes_accessed=count * rows * width * 2, transcendentals=0),
    )(places, grad, *blocks)


def weave_kernel(count, at_ref, *refs):
    pieces, (out_ref, held) = refs[:count], refs[count:]
    for i in range(count):
        held[at_ref[i]] = pieces[i][...]
    for part in range(3):
        for pair in range(count // 2):
            rows = slice(part * HEAD_DIM, (part + 1) * HEAD_DIM)
            both = jnp.concatenate([held[2 * pair, rows], held[2 * pair + 1, rows]], axis=0)
            at = (part * count + 2 * pair) * HEAD_DIM
            out_ref[:, at : at + 2 * HEAD_DIM] = both.astype(jnp.float32).T


def weave(pieces, places):
    count = len(pieces)
    cols, rows = pieces[0].shape
    size = 128
    return pl.pallas_call(
        partial(weave_kernel, count),
        out_shape=jax.ShapeDtypeStruct((rows, count * cols), jnp.float32),
        grid_spec=pltpu.PrefetchScalarGridSpec(
            num_scalar_prefetch=1,
            grid=(rows // size,),
            in_specs=[pl.BlockSpec((cols, size), lambda i, at_ref: (0, i))] * count,
            out_specs=pl.BlockSpec((size, count * cols), lambda i, at_ref: (i, 0)),
            scratch_shapes=[pltpu.VMEM((count, cols, size), pieces[0].dtype)],
        ),
        cost_estimate=pl.CostEstimate(
            flops=0, bytes_accessed=6 * count * cols * rows, transcendentals=0
        ),
    )(places, *pieces)


SEQ = ("z", "y", "c")
SWAP = ((0, 1), (1, 0))


def norm_forward(hidden, gain_vec, offset_vec):
    centre = hidden - jnp.mean(hidden, axis=-1, keepdims=True)
    spread = jnp.mean(centre * centre, axis=-1, keepdims=True)
    inv_std = lax.rsqrt(spread + NORM_EPS)
    scaled = centre * inv_std
    return (scaled * gain_vec + offset_vec, scaled, inv_std)


def norm_backward(grad_out, scaled, inv_std, gain_vec):
    gain_grad = jnp.sum(grad_out * scaled, axis=0)
    offset_grad = jnp.sum(grad_out, axis=0)
    grad_scaled = grad_out * gain_vec
    grad_in = inv_std * (
        grad_scaled
        - jnp.mean(grad_scaled, axis=-1, keepdims=True)
        - scaled * jnp.mean(grad_scaled * scaled, axis=-1, keepdims=True)
    )
    return (gain_grad, offset_grad, grad_in)


def dot(a, b, a_dim, b_dim):
    return lax.dot_general(
        a, b, (((a_dim,), (b_dim,)), ((), ())), preferred_element_type=jnp.float32
    )


def tie(x, *others):
    others = [other for other in others if other is not None]
    return lax.optimization_barrier((x, *others))[0] if others else x


def linear(start, first, a, second, b):
    start, first, second = (jnp.array(x, jnp.int32) for x in (start, first, second))
    return start + first * a + second * b


def pick(x, i, axis=0):
    return lax.dynamic_index_in_dim(x, i, axis, keepdims=False)


def swap(x, axis):
    return lax.ppermute(x, axis, SWAP)


def in_order(own, other, position):
    return jnp.where(position == 0, jnp.stack([own, other]), jnp.stack([other, own]))


def fetch_fsdp(shard, pieces, *others):
    if lax.axis_size("f") != 2:
        return [], [lax.all_gather(shard, "f", axis=0, tiled=True)]
    first = lax.axis_index("c") * pieces
    shard = tie(shard, *others)
    taken = [take(shard, first + i, 2 * pieces) for i in range(pieces)]
    return taken, [swap(part, "f") for part in taken]


def share_cores(fetched, *others):
    if lax.axis_size("f") != 2:
        return fetched
    return fetched + [swap(tie(piece, *others), "c") for piece in fetched]


def join_fsdp(shard, pieces, *others):
    if lax.axis_size("f") != 2:
        return pieces[0]
    core, here = lax.axis_index("c"), lax.axis_index("f")
    count = len(pieces) // 2
    step = range(count)
    at = linear(
        (*range(2 * count), *(2 * count + i for i in step), *(3 * count + i for i in step)),
        (2 * count,) * (2 * count) + (-2 * count,) * (2 * count),
        here,
        (0,) * (2 * count) + (count,) * count + (-count,) * count,
        core,
    )
    rows, cols = shard.shape
    return place(
        [tie(shard, *others), *pieces], at, jnp.zeros_like(at), shard.dtype, rows // (2 * count), (2 * rows, cols)
    )


def join_small(shard):
    if lax.axis_size("f") != 2:
        return lax.all_gather(shard, "f", axis=0, tiled=False)
    return in_order(shard, swap(shard, "f"), lax.axis_index("f"))


def halve(x, axis, pairs=SWAP, here=None):
    here = lax.axis_index(axis) if here is None else here
    got = lax.ppermute(pick(x, 1 - here), axis, pairs)
    return pick(x, here).astype(jnp.float32) + got.astype(jnp.float32)


def plane_pairs(bit):
    return [(i, i ^ bit) for i in range(4)]


class WeightSum:
    def __init__(self, terms, scale):
        self.terms, self.scale = terms, scale
        self.widths = [right.shape[1] // 2 for _, right, _ in terms]
        self.cols = sum(self.widths)
        self.rows = terms[0][0].shape[1 - terms[0][2]] // lax.axis_size("f")

    def after(self, others):
        self.terms = [(left, tie(right, *others), dim) for left, right, dim in self.terms]

    def term(self, n, c, f, half=None):
        left, right, dim = self.terms[n]
        rows, start = self.rows, f * self.rows
        if half is not None:
            rows //= 2
            start = start + half * rows
        left = lax.dynamic_slice_in_dim(left, start, rows, 1 - dim)
        right = lax.dynamic_slice_in_dim(right, c * self.widths[n], self.widths[n], 1)
        return dot(left, right, dim, 0)

    def joined(self, parts):
        parts = [part.astype(jnp.bfloat16) for part in parts]
        return parts[0] if len(parts) == 1 else jnp.concatenate(parts, axis=1)

    def half_of(self, x, half):
        rows = x.shape[0] // 2
        return lax.dynamic_slice_in_dim(x, half * rows, rows, 0).astype(jnp.float32)

    def other_core(self, *others):
        self.after(others)
        core, parts, here = lax.axis_index("c"), lax.axis_size("f"), lax.axis_index("f")
        order = [1 - here, here] if parts == 2 else range(parts)
        self.got = []
        for f in order:
            sent = [self.term(n, 1 - core, f).astype(jnp.bfloat16) for n in range(len(self.terms))]
            self.got.append([swap(part, "c") for part in sent])
        return sent[-1]

    def other_f(self, *others):
        self.after(others)
        core, parts, here = lax.axis_index("c"), lax.axis_size("f"), lax.axis_index("f")
        y, count = lax.axis_index("y"), range(len(self.terms))
        if parts == 2:
            self.far = []
            for half in (1 - y, y):
                sent = self.joined(
                    [self.term(n, core, 1 - here, half) + self.half_of(self.got[0][n], half) for n in count]
                )
                self.far.append(swap(sent, "f"))
                self.after([sent])
            return sent
        total = [
            self.joined([self.term(n, core, f) + self.got[f][n].astype(jnp.float32) for n in count])
            for f in range(parts)
        ]
        self.far = []
        self.total = lax.psum_scatter(jnp.stack(total), "f", scatter_dimension=0, tiled=False)
        return self.total

    def here_half(self, k, half):
        core, parts, here = lax.axis_index("c"), lax.axis_size("f"), lax.axis_index("f")
        if parts != 2:
            return [self.half_of(self.total, half)]
        x, at = [], 0
        for n, width in enumerate(self.widths):
            total = self.term(n, core, here, half) + self.half_of(self.got[1][n], half)
            x.append(total + self.far[k][:, at : at + width].astype(jnp.float32))
            at += width
        return x

    def near_y(self, *others):
        self.after(others)
        sent = self.joined(self.here_half(0, 1 - lax.axis_index("y")))
        self.coming = lax.ppermute(sent, "y", SWAP)
        return sent

    def near_z(self, *others):
        self.coming = tie(self.coming, *others)
        self.after(others)
        x, at = [], 0
        for part in self.here_half(1, lax.axis_index("y")):
            width = part.shape[1]
            x.append(part + self.coming[:, at : at + width].astype(jnp.float32))
            at += width
        x = self.joined(x).reshape(2, -1, self.cols)
        low_z = lax.rem(lax.axis_index("z"), 2)
        sent = pick(x, 1 - low_z)
        self.kept, self.coming = pick(x, low_z), lax.ppermute(sent, "z", plane_pairs(1))
        return sent

    def added(self, x, others):
        return x.astype(jnp.float32) + tie(self.coming, *others).astype(jnp.float32)

    def far_z(self, *others):
        self.x = self.added(self.kept, others).astype(jnp.bfloat16)
        self.coming = lax.ppermute(self.x, "z", plane_pairs(2))
        return self.x

    def back_near_z(self, *others):
        x = self.added(self.x, others)
        if lax.axis_size("g") > 1:
            x = lax.psum(x, "g")
        self.x = (x * self.scale).astype(jnp.bfloat16)
        self.coming = lax.ppermute(self.x, "z", plane_pairs(1))
        return self.x

    def back_y(self, *others):
        coming = tie(self.coming, *others)
        x = in_order(self.x, coming, lax.rem(lax.axis_index("z"), 2)).reshape(-1, self.cols)
        self.near = lax.ppermute(x, "y", SWAP)
        self.x, self.across = x, swap(x, "c")
        return x

    def results(self, *others):
        y, c = lax.axis_index("y"), lax.axis_index("c")
        near = tie(self.near, *others)
        pieces = [self.x, near, self.across, swap(near, "c")]
        row_at = linear((0, 1, 0, 1), (1, -1, 1, -1), y, (0, 0, 0, 0), c)
        col_at = linear((0, 0, 1, 1), (0, 0, 0, 0), y, (1, 1, -1, -1), c)
        rows, at, results = pieces[0].shape[0], 0, []
        for width in self.widths:
            results.append(
                place(
                    pieces, row_at, col_at, jnp.float32, rows, (2 * rows, 2 * width), width, at // width
                )
            )
            at += width
        return results


class VectorSum:
    def __init__(self, vectors, scale):
        self.sizes = [vec.shape[0] // lax.axis_size("f") for vec in vectors]
        self.x = jnp.concatenate([vec.reshape(lax.axis_size("f"), -1) for vec in vectors], axis=1) * scale

    def core(self, *others):
        self.x = tie(self.x, *others)
        self.coming = swap(self.x, "c")
        return self.x

    def other_f(self, *others):
        x = self.x + tie(self.coming, *others)
        if lax.axis_size("f") == 2:
            here = lax.axis_index("f")
            self.x, sent = pick(x, here), pick(x, 1 - here)
            self.coming = swap(sent, "f")
            return sent
        self.x = lax.psum_scatter(x, "f", scatter_dimension=0, tiled=False)
        self.coming = jnp.zeros_like(self.x)
        return self.x

    def hop(self, axis, pairs, others):
        self.x = self.x + tie(self.coming, *others)
        self.coming = lax.ppermute(self.x, axis, pairs)
        return self.x

    def near_y(self, *others):
        return self.hop("y", SWAP, others)

    def near_z(self, *others):
        return self.hop("z", plane_pairs(1), others)

    def far_z(self, *others):
        return self.hop("z", plane_pairs(2), others)

    def result(self, *others):
        self.total = self.x + tie(self.coming, *others)
        if lax.axis_size("g") > 1:
            self.total = lax.psum(self.total, "g")
        return self.total

    def vectors(self):
        at = 0
        for size in self.sizes:
            yield self.total[at : at + size]
            at += size


def arrivals(count):
    table = []
    for z in range(count):
        hops = []
        for t in range(1, count):
            if z - t >= 0:
                hops.append(("up", t))
            if z + t < count:
                hops.append(("down", t))
        table.append(hops)
    return table


def gather_planes(x, use, beside, later):
    z = lax.axis_index("z")
    count = lax.axis_size("z")
    table = arrivals(count)
    up, down = x, x
    hops = {}
    blocks, planes, used = [x], [z], []
    for t in range(1, count):
        up = lax.ppermute(up, "z", [(i, i + 1) for i in range(t - 1, count - 1)])
        down = lax.ppermute(down, "z", [(i, i - 1) for i in range(1, count - t + 1)])
        made = use(blocks[-1])
        before = used.pop() if used else []
        up, down, before, made[0], extra, _ = lax.optimization_barrier(
            (up, down, before, made[0], later[t - 1](blocks), beside[t - 1])
        )
        later[t - 1](blocks, extra)
        used += [before] * (t > 1) + [made]
        hops["up", t], hops["down", t] = up, down
        names = sorted({table[i][t - 1] for i in range(count)})
        block, plane = None, z
        for name in names:
            here = [i for i in range(count) if table[i][t - 1] == name]
            chosen = (z >= here[0]) & (z <= here[-1])
            block = hops[name] if block is None else jnp.where(chosen, hops[name], block)
            plane = jnp.where(chosen, z + (-name[1] if name[0] == "up" else name[1]), plane)
        blocks.append(block)
        planes.append(plane)
    used.append(use(blocks[-1]))
    return blocks, planes, used


def body(
    patches, pos_embed, lengths, out_grad,
    ln1_gain, ln1_bias, w_qkv, b_qv, w_out, b_out,
    ln2_gain, ln2_bias, w_fc1, b_fc1, w_fc2, b_fc2,
):
    f32, low = jnp.float32, jnp.bfloat16
    rows, width = patches.shape[1:]
    groups, parts = lax.axis_size("g"), lax.axis_size("f")
    head = lax.axis_index(SEQ)
    group = lax.axis_index("g")
    shard_index = lax.axis_index("f")
    scale = 1.0 / (parts * math.sqrt(rows * HEADS * groups))

    gain_one, bias_one, qv_bias = (
        join_small(vec).reshape(-1).astype(f32) for vec in (ln1_gain, ln1_bias, b_qv)
    )
    hidden = patches[0].astype(f32) + pos_embed[0].astype(f32)
    normed_pre, scaled_one, inv_one = norm_forward(hidden, gain_one, bias_one)
    normed = normed_pre.astype(low)

    shard_rows = w_qkv.shape[0]
    z, y, c = (lax.axis_index(axis) for axis in SEQ)
    place_in_plane = 2 * y + c
    plane_weights = join_small(plane_columns(tie(w_qkv, gain_one, bias_one, qv_bias), z)).reshape(parts, 12 * HEAD_DIM, shard_rows)
    q_bias, v_bias = (
        lax.dynamic_slice_in_dim(qv_bias, at + z * 4 * HEAD_DIM, 4 * HEAD_DIM).reshape(4, HEAD_DIM)
        for at in (0, width)
    )
    plane_bias = jnp.concatenate([q_bias, jnp.zeros((4, HEAD_DIM), f32), v_bias], axis=1).reshape(-1, 1)
    others = jnp.array([0, 1, 2, 3], jnp.int32)
    heads_made = others ^ place_in_plane

    def heads_of(block):
        own, core, near, far = project(heads_made, plane_weights, plane_bias, block)
        return [
            own, swap(core, "c"), swap(near, "y"),
            lax.ppermute(far, ("y", "c"), [(i, 3 - i) for i in range(4)]),
        ]

    out_taken, out_part = fetch_fsdp(w_out, 1, normed)
    fc1_taken, fc1_part = fetch_fsdp(w_fc1, 2, normed)
    fc2_taken, fc2_part = fetch_fsdp(w_fc2, 2, normed)
    if parts == 2:
        fc2_part = [swap(tie(part, fc1_part[1]), "f") for part in fc2_taken]
    qkv_taken, qkv_part = fetch_fsdp(w_qkv, 2, normed)
    out_full = join_fsdp(w_out, share_cores(out_part))
    beside = [
        out_taken + fc1_taken + fc2_taken + qkv_taken, out_part, fc1_part[:1] + [out_full],
    ]
    near_blocks = []

    def swap_later(first):
        def step(blocks, done=None):
            if done is None:
                return [swap(blocks[first], "y")] if first is not None else []
            near_blocks.extend(done)

        return step

    later = [swap_later(None), swap_later(0), swap_later(1)]
    blocks, planes, made = gather_planes(normed, heads_of, beside, later)
    blocks_at = jnp.concatenate([plane * 4 + heads_made for plane in planes])
    made = [piece for round_made in made for piece in round_made]
    if groups > 1:
        qkv = assemble(made, blocks_at)
    ends = jnp.cumsum(lengths[0]).astype(jnp.int32)
    base = (group * (rows * HEADS)).astype(jnp.int32).reshape(1)
    shift, window = 0, None
    up = [(i, i + 1) for i in range(groups - 1)]
    down = [(i + 1, i) for i in range(groups - 1)]
    if groups > 1:
        margin = -(-LONG // rows)
        shift = margin * rows
        both = qkv[:, HEAD_DIM:]
        before = lax.ppermute(both[HEADS - margin :], "g", up)
        after = lax.ppermute(both[:margin], "g", down)
        window = jnp.concatenate([before, both, after], axis=0)
    if groups > 1:
        attended, log_total = attention_forward(ends, base, [qkv], None, window, shift)
    else:
        attended, log_total, qkv = attention_forward(ends, base, made, blocks_at, None, 0)
    attended, near_last = lax.optimization_barrier((attended, swap(blocks[2], "y")))
    near_blocks.append(near_last)
    fc2_part = share_cores(fc2_part, attended)
    fc1_full = join_fsdp(w_fc1, share_cores(fc1_part), attended)
    fc2_full = join_fsdp(w_fc2, fc2_part, attended)
    small = (b_out, ln2_gain, ln2_bias, b_fc1, b_fc2)
    packed, at, total = 0.0, 0, sum(vec.shape[0] for vec in small)
    for vec in small:
        packed += jnp.pad(vec, (at, total - at - vec.shape[0]))
        at += vec.shape[0]
    packed = join_small(tie(packed, normed))
    vectors, at = [], 0
    for vec in small:
        size = vec.shape[0]
        vectors.append(packed[:, at : at + size].reshape(-1).astype(f32))
        at += size
    out_bias, gain_two, bias_two, fc1_bias, fc2_bias = vectors
    mixed = lax.all_to_all(attended, SEQ, 0, 0, tiled=True).reshape(width, rows)

    branch = dot(mixed, out_full, 0, 0) + out_bias
    middle = hidden + tie(branch, fc2_full, qkv_part[0])
    normed_two_pre, scaled_two, inv_two = norm_forward(middle, gain_two, bias_two)
    normed_two = normed_two_pre.astype(low)
    inner_sum = dot(normed_two, fc1_full, 1, 0) + fc1_bias
    active, gelu_pull = jax.vjp(partial(jax.nn.gelu, approximate=True), inner_sum)
    active_low = active.astype(low)

    out_cot = out_grad[0]
    cot_full = out_cot.astype(f32)
    active_low, *qkv_part = lax.optimization_barrier((active_low, *qkv_part))
    qkv_part = share_cores(qkv_part)
    fc2_sum = WeightSum([(active_low, out_cot, 0)], scale)
    token = fc2_sum.other_core()
    active_grad = dot(tie(out_cot, token), fc2_full, 1, 1)
    inner_grad = gelu_pull(active_grad)[0].astype(low)
    near_blocks.append(swap(tie(blocks[3], fc2_full), "y"))
    token = fc2_sum.other_f(inner_grad, near_blocks[3])
    norm_two_grad = dot(tie(inner_grad, token), fc1_full, 1, 1)
    gain_two_grad, bias_two_grad, middle_from_norm = norm_backward(
        norm_two_grad, scaled_two, inv_two, gain_two
    )
    middle_grad = cot_full + middle_from_norm
    branch_grad = middle_grad.astype(low)
    mixed_grad = dot(out_full, branch_grad, 1, 1).astype(low)
    attended_grad = lax.all_to_all(
        mixed_grad.reshape(HEADS, HEAD_DIM, rows), SEQ, 0, 0, tiled=True
    )
    rest_sum = WeightSum([(normed_two, inner_grad, 0), (mixed, branch_grad, 1)], scale)
    token = rest_sum.other_core(mixed_grad)
    token = fc2_sum.near_y(token)
    token = rest_sum.other_f(token, *fc2_sum.far[1:])
    column = list(blocks)
    across = [swap(tie(block, mixed_grad), "c") for block in column + near_blocks]
    tokens = [token] + across

    plan = [
        [fc2_sum.near_z, rest_sum.near_y],
        [fc2_sum.far_z, rest_sum.near_z],
        [fc2_sum.back_near_z, rest_sum.far_z],
        [fc2_sum.back_y],
        [rest_sum.back_near_z, lambda *after: fc2_sum.near],
        [rest_sum.back_y],
    ]
    carried, first = None, 0
    for chunk in [HEADS] if groups > 1 else CHUNKS:
        results = attention_backward(
            ends, tie(base, *tokens), qkv, window, attended, attended_grad, log_total, shift,
            first, chunk, carried,
        )
        carried, first = results[::-1], first + chunk
        tokens = []
        for move in plan.pop(0):
            tokens.append(move(results[0], *tokens))
    for moves in plan:
        for move in moves:
            tokens.append(move(results[0]))
    head_grad, *window_grad = results
    if groups > 1:
        both = window_grad[0]
        inner = both[margin : margin + HEADS]
        before = lax.ppermute(both[:margin], "g", down)
        after = lax.ppermute(both[margin + HEADS :], "g", up)
        inner = inner.at[HEADS - margin :].add(before).at[:margin].add(after)
        head_grad = jnp.concatenate([head_grad, inner.astype(low)], axis=1)
    token_grad = lax.all_to_all(tie(head_grad, *tokens), SEQ, 0, 0, tiled=True)

    weight_part = head_weight(
        jnp.concatenate([jnp.stack(planes) * 4 + (place_in_plane ^ k) for k in (0, 2, 1, 3)]).astype(jnp.int32),
        head_grad,
        column + near_blocks + across,
    )
    block_out = dot(tie(active_low, weight_part), fc2_full, 1, 0) + fc2_bias
    block_out = (middle + block_out).astype(low)
    weight_part = weight_part.reshape(3 * HEAD_DIM, parts, shard_rows).transpose(1, 0, 2)
    if parts == 2:
        weight_part = halve(weight_part, "f")
    else:
        weight_part = lax.psum_scatter(weight_part, "f", scatter_dimension=0, tiled=False)
    if groups > 1:
        weight_part = lax.psum(weight_part, "g")

    weight_part = (weight_part * scale).astype(low)
    qkv_full = join_fsdp(w_qkv, qkv_part, weight_part, block_out)
    (fc2_grad,) = fc2_sum.results(qkv_full)
    fc1_grad, out_weight_grad = rest_sum.results(fc2_grad)
    hops = [weight_part] + [
        lax.ppermute(weight_part, "z", [(i, (i + k) % 4) for i in range(4)]) for k in range(1, 4)
    ]
    token_grad, fc1_grad, out_weight_grad, *hops = lax.optimization_barrier(
        (token_grad, fc1_grad, out_weight_grad, *hops)
    )

    token_grad = (
        tie(token_grad, fc2_grad).reshape(HEADS, 3, HEAD_DIM, rows).transpose(1, 0, 2, 3).reshape(3 * width, rows)
    )
    norm_one_grad = dot(token_grad, qkv_full, 0, 1)
    gain_one_grad, bias_one_grad, hidden_from_norm = norm_backward(
        norm_one_grad, scaled_one, inv_one, gain_one
    )
    patch_grad = middle_grad + hidden_from_norm

    head_sums = jnp.sum(head_grad.astype(f32), axis=(0, 2))
    qv_grad = jnp.zeros((2 * width,), f32)
    qv_grad = lax.dynamic_update_slice(qv_grad, head_sums[:HEAD_DIM], (head * HEAD_DIM,))
    qv_grad = lax.dynamic_update_slice(
        qv_grad, head_sums[2 * HEAD_DIM :], (width + head * HEAD_DIM,)
    )
    late = VectorSum(
        (
            gain_one_grad,
            bias_one_grad,
            qv_grad,
            jnp.sum(branch_grad.astype(f32), axis=0),
            gain_two_grad,
            bias_two_grad,
            jnp.sum(inner_grad.astype(f32), axis=0),
            jnp.sum(cot_full, axis=0),
        ),
        scale,
    )
    token = late.core()
    token = late.other_f(token)
    pieces = hops + [swap(piece, "y") for piece in hops]
    pieces += [swap(tie(piece, gain_one_grad), "c") for piece in pieces]
    token = late.near_y(token)
    token = late.near_z(token)
    late.far_z(token)
    firsts = lax.rem(z + 4 - jnp.arange(4, dtype=jnp.int32), 4) * 4
    near_places = [firsts + 2 * y + c, firsts + 2 * (1 - y) + c]
    places = jnp.concatenate(near_places + [place_at + 1 - 2 * c for place_at in near_places])
    qkv_weight_grad = weave(pieces, places)
    late.result()
    (
        ln1_gain_sum, ln1_bias_sum, qv_sum, out_bias_sum,
        ln2_gain_sum, ln2_bias_sum, fc1_bias_sum, fc2_bias_sum,
    ) = late.vectors()
    return (
        block_out[None],
        patch_grad[None],
        ln1_gain_sum,
        ln1_bias_sum,
        qkv_weight_grad,
        qv_sum,
        out_weight_grad,
        out_bias_sum,
        ln2_gain_sum,
        ln2_bias_sum,
        fc1_grad,
        fc1_bias_sum,
        fc2_grad,
        fc2_bias_sum,
    )


def solution(mesh):
    seq, parts = mesh.shape["seq"], mesh.shape["fsdp"]
    fine = Mesh(mesh.devices.reshape(seq // HEADS, HEADS // 4, 2, 2, parts), ("g", "z", "y", "c", "f"))
    rows = P("f", ("g",) + SEQ, None)
    vec, mat = P("f"), P("f", None)
    in_specs = (rows, rows, mat, rows, vec, vec, mat, vec, mat, vec, vec, vec, mat, vec, mat, vec)
    out_specs = (rows, rows, vec, vec, mat, vec, mat, vec, vec, vec, mat, vec, mat, vec)
    return jax.shard_map(body, mesh=fine, in_specs=in_specs, out_specs=out_specs, check_vma=False)
```

```python
import math
from functools import partial

import jax
import jax.numpy as jnp
from jax import lax
from jax.experimental import pallas as pl
from jax.experimental.pallas import tpu as pltpu
from jax.sharding import Mesh, PartitionSpec as P

HEADS = 16
LONG = 2304
NORM_EPS = 1e-06
CHUNKS = (3, 4, 3, 3, 3)
HEAD_DIM = 64
BLOCK = 512
FAR = 1e30
QB = 512
KB = 512
HALF = 256
CALM_SCORE = 60.0
FORWARD_COST = 50_000_000_000
BACKWARD_COST = 75_000_000_000


def rows_dot(a, b):
    return lax.dot_general(a, b, (((1,), (0,)), ((), ())), preferred_element_type=jnp.float32)


def membership(ends_ref, count, first, width):
    place = first + lax.broadcasted_iota(jnp.int32, (16, width), 1)
    row = lax.broadcasted_iota(jnp.int32, (16, width), 0)
    low = jnp.zeros((16, width), jnp.int32)
    high = jnp.zeros((16, width), jnp.int32)
    for i in range(count):
        begin = ends_ref[i - 1] if i > 0 else 0
        low = jnp.where(row == i, begin, low)
        high = jnp.where(row == i, ends_ref[i], high)
    return jnp.where((place >= low) & (place < high), 1.0, 0.0)


def image_span(ends_ref, count, first, last):
    low = jnp.int32(0)
    high = ends_ref[count - 1]
    for i in range(count - 1):
        end = ends_ref[i]
        low = jnp.where(end <= first, end, low)
    for i in range(count - 2, -1, -1):
        end = ends_ref[i]
        high = jnp.where(end > last, end, high)
    return low, high


def over_keys(low, high, step, carry):
    def whole(j, carry):
        return step(pl.ds(pl.multiple_of((low + 2 * j) * HALF, HALF), KB), carry)

    def half(j, carry):
        return step(pl.ds(pl.multiple_of(j * HALF, HALF), HALF), carry)

    pairs = (high - low) // 2
    carry = lax.fori_loop(0, pairs, whole, carry)
    return lax.fori_loop(low + 2 * pairs, high, half, carry)


def split3(x):
    top = x.astype(jnp.bfloat16)
    rest = x - top.astype(jnp.float32)
    mid = rest.astype(jnp.bfloat16)
    low = (rest - mid.astype(jnp.float32)).astype(jnp.bfloat16)
    return [top.astype(jnp.float32), mid.astype(jnp.float32), low.astype(jnp.float32)]


def parts_of(ref):
    return [ref.at[:, i * HEAD_DIM : (i + 1) * HEAD_DIM, :] for i in range(ref.shape[1] // HEAD_DIM)]


def forward_kernel(count, shift, pieces, ends_ref, base_ref, *refs):
    if shift:
        own_ref, window_ref, o_ref, log_ref, qa, kn, va, peak = refs
        q_ref = parts_of(own_ref)[0]
        k_ref, v_ref = parts_of(window_ref)
    else:
        place_ref, *refs = refs
        made, (o_ref, log_ref, own_ref, qa, kn, va, peak) = refs[:pieces], refs[pieces:]
        for i in range(pieces):
            own_ref[place_ref[i]] = made[i][...]
        q_ref, k_ref, v_ref = parts_of(own_ref)
    peak[...] = jnp.zeros_like(peak)
    q_blocks = q_ref.shape[0]
    k_blocks = k_ref.shape[0]
    key_count = k_blocks * BLOCK
    base = base_ref[0]

    @pl.loop(0, k_blocks)
    def _(i):
        at = pl.ds(pl.multiple_of(i * BLOCK, BLOCK), BLOCK)
        away = (membership(ends_ref, count, base - shift + i * BLOCK, BLOCK) - 1.0) * FAR
        keys = k_ref[i].astype(jnp.float32)
        peak[1:2] = jnp.maximum(peak[1:2], jnp.sum(keys * keys, axis=0, keepdims=True))
        both = jnp.concatenate([keys, away], axis=0)
        kn[at, :] = both.T.astype(jnp.bfloat16)
        va[:, at] = jnp.concatenate(
            [v_ref[i].astype(jnp.float32), jnp.ones((16, BLOCK), jnp.float32)], axis=0
        ).astype(jnp.bfloat16)

    @pl.loop(0, q_blocks)
    def _(i):
        at = pl.ds(pl.multiple_of(i * BLOCK, BLOCK), BLOCK)
        inside = membership(ends_ref, count, base + i * BLOCK, BLOCK)
        asked = q_ref[i].astype(jnp.float32)
        peak[0:1] = jnp.maximum(peak[0:1], jnp.sum(asked * asked, axis=0, keepdims=True))
        qa[:, at] = jnp.concatenate(
            [asked * (HEAD_DIM ** -0.5), inside], axis=0
        ).astype(jnp.bfloat16)

    per = BLOCK // QB
    calm = CALM_SCORE * HEAD_DIM ** 0.5
    peaks = [jnp.max(peak[i : i + 1]) for i in range(2)]

    def span(i):
        first = base + i * QB
        low, high = image_span(ends_ref, count, first, first + QB - 1)
        low = jnp.maximum(low - base + shift, 0) // HALF
        return low, jnp.minimum(high - base + shift + HALF - 1, key_count) // HALF

    def finish(i, top, acc):
        total = acc[HEAD_DIM : HEAD_DIM + 1]
        o_ref[i // per, :, pl.ds(pl.multiple_of((i % per) * QB, QB), QB)] = (
            acc[:HEAD_DIM] / total
        ).astype(jnp.bfloat16)
        log_ref[:, pl.ds(pl.multiple_of(i * QB, QB), QB)] = top + jnp.log(total)

    small = peaks[0] * peaks[1] <= calm * calm

    @pl.when(small)
    def _():
        @pl.loop(0, q_blocks * per)
        def _(i):
            q_part = qa[:, pl.ds(pl.multiple_of(i * QB, QB), QB)]

            def step(at, acc):
                weights = jnp.exp(rows_dot(kn[at, :], q_part)).astype(jnp.bfloat16)
                return acc + rows_dot(va[:, at], weights)

            finish(i, 0.0, over_keys(*span(i), step, jnp.zeros((HEAD_DIM + 16, QB), jnp.float32)))

    @pl.when(jnp.logical_not(small))
    def _():
        @pl.loop(0, q_blocks * per)
        def _(i):
            q_part = qa[:, pl.ds(pl.multiple_of(i * QB, QB), QB)]

            def step(at, carry):
                top, acc = carry
                scores = rows_dot(kn[at, :], q_part)
                new_top = jnp.maximum(top, jnp.max(scores, axis=0, keepdims=True))
                weights = jnp.exp(scores - new_top).astype(jnp.bfloat16)
                acc = acc * jnp.exp(top - new_top) + rows_dot(va[:, at], weights)
                return new_top, acc

            start = (
                jnp.full((1, QB), -3e38, jnp.float32),
                jnp.zeros((HEAD_DIM + 16, QB), jnp.float32),
            )
            finish(i, *over_keys(*span(i), step, start))


def backward_kernel(count, shift, first_block, chunk, last, ends_ref, base_ref, own_ref, *refs):
    q_ref, k_ref, v_ref = parts_of(own_ref)
    if shift:
        k_ref, v_ref = parts_of(refs[0])
        refs = refs[1:]
    o_ref, do_ref, log_ref, *refs = refs
    if first_block > 0:
        sums_in, _, *refs = refs
    grad_ref, *refs = refs
    sums_out = None
    if shift:
        window_ref, *refs = refs
    if not last:
        sums_out, *refs = refs
    qa, da, kn, vn, qn, dn, ks, sums, dq_part, sums_sem, dq_sem, *refs = refs
    k_blocks = k_ref.shape[0]
    key_count = k_blocks * BLOCK
    base = base_ref[0]
    scale = HEAD_DIM ** -0.5
    start = base + first_block * BLOCK
    low, high = image_span(ends_ref, count, start, start + chunk * BLOCK - 1)
    low = jnp.maximum(low - base + shift, 0) // BLOCK
    high = jnp.minimum(high - base + shift + BLOCK - 1, key_count) // BLOCK
    held_low, held_high = (0, k_blocks) if last or first_block == 0 else (low, high)

    def block_at(i):
        return pl.ds(pl.multiple_of(i * BLOCK, BLOCK), BLOCK)

    if first_block > 0:

        @pl.loop(held_low, held_high)
        def _(i):
            pltpu.make_async_copy(sums_in.at[block_at(i)], sums.at[block_at(i)], sums_sem.at[i]).start()

    else:
        sums[...] = jnp.zeros_like(sums)

    @pl.loop(low, high)
    def _(i):
        at = block_at(i)
        away = (membership(ends_ref, count, base - shift + i * BLOCK, BLOCK) - 1.0) * FAR
        ones = jnp.ones((16, BLOCK), jnp.float32)
        keys = k_ref[i].astype(jnp.float32)
        kn[at, :] = jnp.concatenate([keys, away, ones], axis=0).T.astype(jnp.bfloat16)
        vn[at, :] = jnp.concatenate([v_ref[i].astype(jnp.float32), ones], axis=0).T.astype(jnp.bfloat16)
        ks[:, at] = (keys * scale).astype(jnp.bfloat16)

    @pl.loop(0, chunk)
    def _(i):
        at = block_at(i)
        block = first_block + i
        inside = membership(ends_ref, count, base + block * BLOCK, BLOCK)
        pad = jnp.zeros((13, BLOCK), jnp.float32)
        scaled = q_ref[block].astype(jnp.float32) * scale
        qn[at, :] = scaled.T.astype(jnp.bfloat16)
        qa[:, at] = jnp.concatenate(
            [scaled, inside] + split3(-log_ref[:, block_at(block)]) + [pad], axis=0
        ).astype(jnp.bfloat16)
        grads = do_ref[block].astype(jnp.float32)
        row_dot = jnp.sum(grads * o_ref[block].astype(jnp.float32), axis=0, keepdims=True)
        dn[at, :] = grads.T.astype(jnp.bfloat16)
        da[:, at] = jnp.concatenate([grads] + split3(-row_dot) + [pad], axis=0).astype(jnp.bfloat16)

    if first_block > 0:

        @pl.loop(held_low, held_high)
        def _(i):
            pltpu.make_async_copy(sums_in.at[block_at(i)], sums.at[block_at(i)], sums_sem.at[i]).wait()

    @pl.loop(0, chunk)
    def _(i):
        q_at = block_at(i)
        q_part = qa[:, q_at]
        d_part = da[:, q_at]
        q_rows = qn[q_at, :]
        d_rows = dn[q_at, :]
        first = start + i * BLOCK
        key_low, key_high = image_span(ends_ref, count, first, first + BLOCK - 1)
        key_low = jnp.maximum(key_low - base + shift, 0) // HALF
        key_high = jnp.minimum(key_high - base + shift + HALF - 1, key_count) // HALF

        def step(at, dq):
            probs = jnp.exp(rows_dot(kn[at, :], q_part))
            score_grad = (probs * rows_dot(vn[at, :], d_part)).astype(jnp.bfloat16)
            sums[at, 0:HEAD_DIM] += rows_dot(score_grad, q_rows)
            sums[at, HEAD_DIM : 2 * HEAD_DIM] += rows_dot(probs.astype(jnp.bfloat16), d_rows)
            return dq + rows_dot(ks[:, at], score_grad)

        dq = over_keys(key_low, key_high, step, jnp.zeros((HEAD_DIM, BLOCK), jnp.float32))
        dq_part[i] = dq.astype(jnp.bfloat16)

    def query_copy(i):
        return pltpu.make_async_copy(
            dq_part.at[i], grad_ref.at[first_block + i, 0:HEAD_DIM], dq_sem.at[i]
        )

    for i in range(chunk):
        query_copy(i).start()
    if not last:

        @pl.loop(held_low, held_high)
        def _(i):
            pltpu.make_async_copy(sums.at[block_at(i)], sums_out.at[block_at(i)], sums_sem.at[i]).start()

        @pl.loop(held_low, held_high)
        def _(i):
            pltpu.make_async_copy(sums.at[block_at(i)], sums_out.at[block_at(i)], sums_sem.at[i]).wait()

    elif shift:

        @pl.loop(0, k_blocks)
        def _(i):
            window_ref[i] = sums[block_at(i), :].T

    else:
        kv_part, kv_sem = refs

        def key_copy(i):
            return pltpu.make_async_copy(
                kv_part.at[i], grad_ref.at[i, HEAD_DIM : 3 * HEAD_DIM], kv_sem.at[i]
            )

        @pl.loop(0, k_blocks)
        def _(i):
            kv_part[i] = sums[block_at(i), :].T.astype(jnp.bfloat16)
            key_copy(i).start()

        @pl.loop(0, k_blocks)
        def _(i):
            key_copy(i).wait()

    for i in range(chunk):
        query_copy(i).wait()


def vmem_spec():
    return pl.BlockSpec(memory_space=pltpu.VMEM)


def smem_spec():
    return pl.BlockSpec(memory_space=pltpu.SMEM)


def attention_forward(ends, base, made, places, window, shift):
    blocks = made[0].shape[0] if shift else len(made)
    tokens, keys = blocks * BLOCK, blocks * BLOCK + 2 * shift
    low = jnp.bfloat16
    out_shape = [
        jax.ShapeDtypeStruct((blocks, HEAD_DIM, BLOCK), low),
        jax.ShapeDtypeStruct((1, tokens), jnp.float32),
    ]
    if shift:
        arrays, in_specs = [*made, window], [smem_spec()] * 2 + [vmem_spec()] * 2
    else:
        arrays, in_specs = [places, *made], [smem_spec()] * 3 + [vmem_spec()] * blocks
        out_shape.append(jax.ShapeDtypeStruct((blocks, 3 * HEAD_DIM, BLOCK), low))
    return pl.pallas_call(
        partial(forward_kernel, ends.shape[0], shift, blocks),
        out_shape=out_shape,
        in_specs=in_specs,
        out_specs=[vmem_spec()] * len(out_shape),
        scratch_shapes=[
            pltpu.VMEM((HEAD_DIM + 16, tokens), low),
            pltpu.VMEM((keys, HEAD_DIM + 16), low),
            pltpu.VMEM((HEAD_DIM + 16, keys), low),
            pltpu.VMEM((8, BLOCK), jnp.float32),
        ],
        compiler_params=pltpu.CompilerParams(vmem_limit_bytes=48 * 1024 * 1024),
        cost_estimate=pl.CostEstimate(
            flops=FORWARD_COST, bytes_accessed=tokens * 512, transcendentals=0
        ),
    )(ends, base, *arrays)


def attention_backward(ends, base, own, window, o, do, log, shift, first_block, chunk, carried):
    blocks = own.shape[0]
    tokens, keys = chunk * BLOCK, blocks * BLOCK + 2 * shift
    last = first_block + chunk == blocks
    low, f32 = jnp.bfloat16, jnp.float32
    arrays = [own] + ([window] if shift else []) + [o, do, log]
    in_specs = [smem_spec(), smem_spec()] + [vmem_spec()] * len(arrays)
    out_shape = [jax.ShapeDtypeStruct((blocks, HEAD_DIM if shift else 3 * HEAD_DIM, BLOCK), low)]
    out_specs = [any_spec()]
    aliases = {}
    if carried is not None:
        place_at = 2 + len(arrays)
        arrays += list(carried)
        in_specs += [any_spec(), any_spec()]
        aliases = {place_at + 1: 0}
        if not last:
            aliases[place_at] = 1
    if shift:
        out_shape.append(jax.ShapeDtypeStruct((keys // BLOCK, 2 * HEAD_DIM, BLOCK), f32))
        out_specs.append(vmem_spec())
    if not last:
        out_shape.append(jax.ShapeDtypeStruct((keys, 2 * HEAD_DIM), f32))
        out_specs.append(any_spec())
    scratch = [
        pltpu.VMEM((HEAD_DIM + 32, tokens), low),
        pltpu.VMEM((HEAD_DIM + 16, tokens), low),
        pltpu.VMEM((keys, HEAD_DIM + 32), low),
        pltpu.VMEM((keys, HEAD_DIM + 16), low),
        pltpu.VMEM((tokens, HEAD_DIM), low),
        pltpu.VMEM((tokens, HEAD_DIM), low),
        pltpu.VMEM((HEAD_DIM, keys), low),
        pltpu.VMEM((keys, 2 * HEAD_DIM), f32),
        pltpu.VMEM((chunk, HEAD_DIM, BLOCK), low),
        pltpu.SemaphoreType.DMA((keys // BLOCK,)),
        pltpu.SemaphoreType.DMA((chunk,)),
    ]
    if last and not shift:
        scratch += [
            pltpu.VMEM((blocks, 2 * HEAD_DIM, BLOCK), low),
            pltpu.SemaphoreType.DMA((blocks,)),
        ]
    return pl.pallas_call(
        partial(backward_kernel, ends.shape[0], shift, first_block, chunk, last),
        out_shape=out_shape,
        in_specs=in_specs,
        out_specs=out_specs,
        scratch_shapes=scratch,
        input_output_aliases=aliases,
        compiler_params=pltpu.CompilerParams(vmem_limit_bytes=50 * 1024 * 1024),
        cost_estimate=pl.CostEstimate(flops=BACKWARD_COST * chunk // blocks, bytes_accessed=tokens * 1024, transcendentals=0),
    )(ends, base, *arrays)


def any_spec():
    return pl.BlockSpec(memory_space=pl.ANY)


def block_rows(rows, cols):
    while rows * cols > 512 * 1024 and rows % 16 == 0:
        rows //= 2
    return rows


def take_kernel(at_ref, in_ref, out_ref):
    out_ref[...] = in_ref[...]


def take(x, index, count):
    rows, cols = x.shape[0] // count, x.shape[1]
    size = block_rows(rows, cols)
    steps = rows // size
    return pl.pallas_call(
        take_kernel,
        out_shape=jax.ShapeDtypeStruct((rows, cols), x.dtype),
        grid_spec=pltpu.PrefetchScalarGridSpec(
            num_scalar_prefetch=1,
            grid=(steps,),
            in_specs=[pl.BlockSpec((size, cols), lambda j, at_ref: (at_ref[0] * steps + j, 0))],
            out_specs=pl.BlockSpec((size, cols), lambda j, at_ref: (j, 0)),
        ),
        cost_estimate=pl.CostEstimate(flops=0, bytes_accessed=2 * rows * cols * x.dtype.itemsize, transcendentals=0),
    )(index.astype(jnp.int32).reshape(1), x)


def place_kernel(owner, row_ref, col_ref, *refs):
    out_ref = refs[-1]
    for i, piece in enumerate(owner):

        @pl.when(pl.program_id(0) == i)
        def _(piece=piece):
            out_ref[...] = refs[piece][...].astype(out_ref.dtype)


def place(pieces, row_at, col_at, dtype, rows, shape, cols=None, block=0):
    cols = cols or pieces[0].shape[1]
    owner = [n for n, piece in enumerate(pieces) for _ in range(piece.shape[0] // rows)]
    count = len(owner)
    size = block_rows(rows, cols)
    steps = rows // size

    def piece_map(piece):
        turns = [i for i in range(count) if owner[i] == piece]
        first, last = turns[0], turns[-1]

        def index(s, j, row_ref, col_ref):
            inside = j + (s - first) * steps
            end = (last - first + 1) * steps - 1
            return (jnp.where(s < first, 0, jnp.where(s > last, end, inside)), block)

        return index

    return pl.pallas_call(
        partial(place_kernel, owner),
        out_shape=jax.ShapeDtypeStruct(shape, dtype),
        grid_spec=pltpu.PrefetchScalarGridSpec(
            num_scalar_prefetch=2,
            grid=(count, steps),
            in_specs=[pl.BlockSpec((size, cols), piece_map(i)) for i in range(len(pieces))],
            out_specs=pl.BlockSpec(
                (size, cols), lambda s, j, row_ref, col_ref: (row_ref[s] * steps + j, col_ref[s])
            ),
        ),
        cost_estimate=pl.CostEstimate(
            flops=0,
            bytes_accessed=count * rows * cols * (2 + jnp.dtype(dtype).itemsize),
            transcendentals=0,
        ),
    )(row_at, col_at, *pieces)


def plane_columns_kernel(plane_ref, q_ref, k_ref, v_ref, out_ref):
    for part, ref in enumerate((q_ref, k_ref, v_ref)):
        cols = ref[...].astype(jnp.float32).T
        for j in range(4):
            at = (3 * j + part) * HEAD_DIM
            out_ref[at : at + HEAD_DIM] = cols[j * HEAD_DIM : (j + 1) * HEAD_DIM].astype(out_ref.dtype)


def plane_columns(w, plane):
    rows = w.shape[0]

    def spec(part):
        return pl.BlockSpec((rows, 4 * HEAD_DIM), lambda i, plane_ref: (0, part * (HEADS // 4) + plane_ref[0]))

    return pl.pallas_call(
        plane_columns_kernel,
        out_shape=jax.ShapeDtypeStruct((12 * HEAD_DIM, rows), w.dtype),
        grid_spec=pltpu.PrefetchScalarGridSpec(
            num_scalar_prefetch=1,
            grid=(1,),
            in_specs=[spec(part) for part in range(3)],
            out_specs=pl.BlockSpec((12 * HEAD_DIM, rows), lambda i, plane_ref: (0, 0)),
        ),
    )(plane.astype(jnp.int32).reshape(1), w, w, w)


def project_kernel(head_ref, w_ref, bias_ref, block_ref, *out_refs):
    size = w_ref.shape[2]
    rows = 3 * HEAD_DIM
    for i, out_ref in enumerate(out_refs):
        at = pl.ds(pl.multiple_of(head_ref[i] * rows, HEAD_DIM), rows)
        total = bias_ref[at, :]
        for f in range(w_ref.shape[0]):
            total += lax.dot_general(
                w_ref[f, at, :], block_ref[:, f * size : (f + 1) * size], (((1,), (1,)), ((), ())),
                preferred_element_type=jnp.float32,
            )
        out_ref[...] = total.astype(jnp.bfloat16)


def project(heads, w, bias, block):
    rows, width = block.shape
    count = heads.shape[0]
    shape = jax.ShapeDtypeStruct((3 * HEAD_DIM, rows), jnp.bfloat16)
    return pl.pallas_call(
        project_kernel,
        out_shape=[shape] * count,
        in_specs=[smem_spec()] + [vmem_spec()] * 3,
        out_specs=[vmem_spec()] * count,
        compiler_params=pltpu.CompilerParams(vmem_limit_bytes=24 * 1024 * 1024),
        cost_estimate=pl.CostEstimate(
            flops=6 * count * rows * width * 3 * HEAD_DIM, bytes_accessed=rows * width * 2, transcendentals=0
        ),
    )(heads, w, bias, block)


def assemble_kernel(count, place_ref, *refs):
    pieces, out_ref, sem = refs[:count], refs[count], refs[count + 1]

    def copy(i):
        return pltpu.make_async_copy(pieces[i], out_ref.at[place_ref[i]], sem.at[i])

    for i in range(count):
        copy(i).start()
    for i in range(count):
        copy(i).wait()


def assemble(pieces, places):
    count = len(pieces)
    return pl.pallas_call(
        partial(assemble_kernel, count),
        out_shape=jax.ShapeDtypeStruct((count,) + pieces[0].shape, pieces[0].dtype),
        in_specs=[smem_spec()] + [vmem_spec()] * count,
        out_specs=any_spec(),
        scratch_shapes=[pltpu.SemaphoreType.DMA((count,))],
        compiler_params=pltpu.CompilerParams(vmem_limit_bytes=16 * 1024 * 1024),
        cost_estimate=pl.CostEstimate(
            flops=0, bytes_accessed=4 * count * pieces[0].size, transcendentals=0
        ),
    )(places, *pieces)


SLOTS = 4


def head_weight_kernel(count, place_ref, grad_ref, *refs):
    blocks, (out_ref, held, sem) = refs[:count], refs[count:]

    def copy(b):
        return pltpu.make_async_copy(blocks[b], held.at[b % SLOTS], sem.at[b % SLOTS])

    for b in range(SLOTS - 1):
        copy(b).start()
    out_ref[...] = jnp.zeros_like(out_ref)

    @pl.loop(0, count)
    def _(i):
        slot = lax.rem(i, SLOTS)
        pltpu.make_async_copy(blocks[0], held.at[slot], sem.at[slot]).wait()
        for b in range(SLOTS - 1, count):

            @pl.when(i + SLOTS - 1 == b)
            def _(b=b):
                copy(b).start()

        out_ref[...] += rows_dot(grad_ref[place_ref[i]], held[slot])


def head_weight(places, grad, blocks):
    count = len(blocks)
    rows, width = blocks[0].shape
    cols = grad.shape[1]
    return pl.pallas_call(
        partial(head_weight_kernel, count),
        out_shape=jax.ShapeDtypeStruct((cols, width), jnp.float32),
        in_specs=[smem_spec(), vmem_spec()] + [any_spec()] * count,
        out_specs=vmem_spec(),
        scratch_shapes=[
            pltpu.VMEM((SLOTS, rows, width), jnp.bfloat16),
            pltpu.SemaphoreType.DMA((SLOTS,)),
        ],
        compiler_params=pltpu.CompilerParams(vmem_limit_bytes=24 * 1024 * 1024),
        cost_estimate=pl.CostEstimate(flops=4 * count * rows * width * cols, bytes_accessed=count * rows * width * 2, transcendentals=0),
    )(places, grad, *blocks)


def weave_kernel(count, at_ref, *refs):
    pieces, (out_ref, held) = refs[:count], refs[count:]
    for i in range(count):
        held[at_ref[i]] = pieces[i][...]
    for part in range(3):
        for pair in range(count // 2):
            rows = slice(part * HEAD_DIM, (part + 1) * HEAD_DIM)
            both = jnp.concatenate([held[2 * pair, rows], held[2 * pair + 1, rows]], axis=0)
            at = (part * count + 2 * pair) * HEAD_DIM
            out_ref[:, at : at + 2 * HEAD_DIM] = both.astype(jnp.float32).T


def weave(pieces, places):
    count = len(pieces)
    cols, rows = pieces[0].shape
    size = 128
    return pl.pallas_call(
        partial(weave_kernel, count),
        out_shape=jax.ShapeDtypeStruct((rows, count * cols), jnp.float32),
        grid_spec=pltpu.PrefetchScalarGridSpec(
            num_scalar_prefetch=1,
            grid=(rows // size,),
            in_specs=[pl.BlockSpec((cols, size), lambda i, at_ref: (0, i))] * count,
            out_specs=pl.BlockSpec((size, count * cols), lambda i, at_ref: (i, 0)),
            scratch_shapes=[pltpu.VMEM((count, cols, size), pieces[0].dtype)],
        ),
        cost_estimate=pl.CostEstimate(
            flops=0, bytes_accessed=6 * count * cols * rows, transcendentals=0
        ),
    )(places, *pieces)


SEQ = ("z", "y", "c")
SWAP = ((0, 1), (1, 0))


def norm_forward(hidden, gain_vec, offset_vec):
    centre = hidden - jnp.mean(hidden, axis=-1, keepdims=True)
    spread = jnp.mean(centre * centre, axis=-1, keepdims=True)
    inv_std = lax.rsqrt(spread + NORM_EPS)
    scaled = centre * inv_std
    return (scaled * gain_vec + offset_vec, scaled, inv_std)


def norm_backward(grad_out, scaled, inv_std, gain_vec):
    gain_grad = jnp.sum(grad_out * scaled, axis=0)
    offset_grad = jnp.sum(grad_out, axis=0)
    grad_scaled = grad_out * gain_vec
    grad_in = inv_std * (
        grad_scaled
        - jnp.mean(grad_scaled, axis=-1, keepdims=True)
        - scaled * jnp.mean(grad_scaled * scaled, axis=-1, keepdims=True)
    )
    return (gain_grad, offset_grad, grad_in)


def dot(a, b, a_dim, b_dim):
    return lax.dot_general(
        a, b, (((a_dim,), (b_dim,)), ((), ())), preferred_element_type=jnp.float32
    )


def tie(x, *others):
    others = [other for other in others if other is not None]
    return lax.optimization_barrier((x, *others))[0] if others else x


def linear(start, first, a, second, b):
    start, first, second = (jnp.array(x, jnp.int32) for x in (start, first, second))
    return start + first * a + second * b


def pick(x, i, axis=0):
    return lax.dynamic_index_in_dim(x, i, axis, keepdims=False)


def swap(x, axis):
    return lax.ppermute(x, axis, SWAP)


def in_order(own, other, position):
    return jnp.where(position == 0, jnp.stack([own, other]), jnp.stack([other, own]))


def fetch_fsdp(shard, pieces, *others):
    if lax.axis_size("f") != 2:
        return [], [lax.all_gather(shard, "f", axis=0, tiled=True)]
    first = lax.axis_index("c") * pieces
    shard = tie(shard, *others)
    taken = [take(shard, first + i, 2 * pieces) for i in range(pieces)]
    return taken, [swap(part, "f") for part in taken]


def share_cores(fetched, *others):
    if lax.axis_size("f") != 2:
        return fetched
    return fetched + [swap(tie(piece, *others), "c") for piece in fetched]


def join_fsdp(shard, pieces, *others):
    if lax.axis_size("f") != 2:
        return pieces[0]
    core, here = lax.axis_index("c"), lax.axis_index("f")
    count = len(pieces) // 2
    step = range(count)
    at = linear(
        (*range(2 * count), *(2 * count + i for i in step), *(3 * count + i for i in step)),
        (2 * count,) * (2 * count) + (-2 * count,) * (2 * count),
        here,
        (0,) * (2 * count) + (count,) * count + (-count,) * count,
        core,
    )
    rows, cols = shard.shape
    return place(
        [tie(shard, *others), *pieces], at, jnp.zeros_like(at), shard.dtype, rows // (2 * count), (2 * rows, cols)
    )


def join_small(shard):
    if lax.axis_size("f") != 2:
        return lax.all_gather(shard, "f", axis=0, tiled=False)
    return in_order(shard, swap(shard, "f"), lax.axis_index("f"))


def halve(x, axis, pairs=SWAP, here=None):
    here = lax.axis_index(axis) if here is None else here
    got = lax.ppermute(pick(x, 1 - here), axis, pairs)
    return pick(x, here).astype(jnp.float32) + got.astype(jnp.float32)


def plane_pairs(bit):
    return [(i, i ^ bit) for i in range(4)]


class WeightSum:
    def __init__(self, terms, scale):
        self.terms, self.scale = terms, scale
        self.widths = [right.shape[1] // 2 for _, right, _ in terms]
        self.cols = sum(self.widths)
        self.rows = terms[0][0].shape[1 - terms[0][2]] // lax.axis_size("f")

    def after(self, others):
        self.terms = [(left, tie(right, *others), dim) for left, right, dim in self.terms]

    def term(self, n, c, f, half=None):
        left, right, dim = self.terms[n]
        rows, start = self.rows, f * self.rows
        if half is not None:
            rows //= 2
            start = start + half * rows
        left = lax.dynamic_slice_in_dim(left, start, rows, 1 - dim)
        right = lax.dynamic_slice_in_dim(right, c * self.widths[n], self.widths[n], 1)
        return dot(left, right, dim, 0)

    def joined(self, parts):
        parts = [part.astype(jnp.bfloat16) for part in parts]
        return parts[0] if len(parts) == 1 else jnp.concatenate(parts, axis=1)

    def half_of(self, x, half):
        rows = x.shape[0] // 2
        return lax.dynamic_slice_in_dim(x, half * rows, rows, 0).astype(jnp.float32)

    def other_core(self, *others):
        self.after(others)
        core, parts, here = lax.axis_index("c"), lax.axis_size("f"), lax.axis_index("f")
        order = [1 - here, here] if parts == 2 else range(parts)
        self.got = []
        for f in order:
            sent = [self.term(n, 1 - core, f).astype(jnp.bfloat16) for n in range(len(self.terms))]
            self.got.append([swap(part, "c") for part in sent])
        return sent[-1]

    def other_f(self, *others):
        self.after(others)
        core, parts, here = lax.axis_index("c"), lax.axis_size("f"), lax.axis_index("f")
        y, count = lax.axis_index("y"), range(len(self.terms))
        if parts == 2:
            self.far = []
            for half in (1 - y, y):
                sent = self.joined(
                    [self.term(n, core, 1 - here, half) + self.half_of(self.got[0][n], half) for n in count]
                )
                self.far.append(swap(sent, "f"))
                self.after([sent])
            return sent
        total = [
            self.joined([self.term(n, core, f) + self.got[f][n].astype(jnp.float32) for n in count])
            for f in range(parts)
        ]
        self.far = []
        self.total = lax.psum_scatter(jnp.stack(total), "f", scatter_dimension=0, tiled=False)
        return self.total

    def here_half(self, k, half):
        core, parts, here = lax.axis_index("c"), lax.axis_size("f"), lax.axis_index("f")
        if parts != 2:
            return [self.half_of(self.total, half)]
        x, at = [], 0
        for n, width in enumerate(self.widths):
            total = self.term(n, core, here, half) + self.half_of(self.got[1][n], half)
            x.append(total + self.far[k][:, at : at + width].astype(jnp.float32))
            at += width
        return x

    def near_y(self, *others):
        self.after(others)
        sent = self.joined(self.here_half(0, 1 - lax.axis_index("y")))
        self.coming = lax.ppermute(sent, "y", SWAP)
        return sent

    def near_z(self, *others):
        self.coming = tie(self.coming, *others)
        self.after(others)
        x, at = [], 0
        for part in self.here_half(1, lax.axis_index("y")):
            width = part.shape[1]
            x.append(part + self.coming[:, at : at + width].astype(jnp.float32))
            at += width
        x = self.joined(x).reshape(2, -1, self.cols)
        low_z = lax.rem(lax.axis_index("z"), 2)
        sent = pick(x, 1 - low_z)
        self.kept, self.coming = pick(x, low_z), lax.ppermute(sent, "z", plane_pairs(1))
        return sent

    def added(self, x, others):
        return x.astype(jnp.float32) + tie(self.coming, *others).astype(jnp.float32)

    def far_z(self, *others):
        self.x = self.added(self.kept, others).astype(jnp.bfloat16)
        self.coming = lax.ppermute(self.x, "z", plane_pairs(2))
        return self.x

    def back_near_z(self, *others):
        x = self.added(self.x, others)
        if lax.axis_size("g") > 1:
            x = lax.psum(x, "g")
        self.x = (x * self.scale).astype(jnp.bfloat16)
        self.coming = lax.ppermute(self.x, "z", plane_pairs(1))
        return self.x

    def back_y(self, *others):
        coming = tie(self.coming, *others)
        x = in_order(self.x, coming, lax.rem(lax.axis_index("z"), 2)).reshape(-1, self.cols)
        self.near = lax.ppermute(x, "y", SWAP)
        self.x, self.across = x, swap(x, "c")
        return x

    def results(self, *others):
        y, c = lax.axis_index("y"), lax.axis_index("c")
        near = tie(self.near, *others)
        pieces = [self.x, near, self.across, swap(near, "c")]
        row_at = linear((0, 1, 0, 1), (1, -1, 1, -1), y, (0, 0, 0, 0), c)
        col_at = linear((0, 0, 1, 1), (0, 0, 0, 0), y, (1, 1, -1, -1), c)
        rows, at, results = pieces[0].shape[0], 0, []
        for width in self.widths:
            results.append(
                place(
                    pieces, row_at, col_at, jnp.float32, rows, (2 * rows, 2 * width), width, at // width
                )
            )
            at += width
        return results


class VectorSum:
    def __init__(self, vectors, scale):
        self.sizes = [vec.shape[0] // lax.axis_size("f") for vec in vectors]
        self.x = jnp.concatenate([vec.reshape(lax.axis_size("f"), -1) for vec in vectors], axis=1) * scale

    def core(self, *others):
        self.x = tie(self.x, *others)
        self.coming = swap(self.x, "c")
        return self.x

    def other_f(self, *others):
        x = self.x + tie(self.coming, *others)
        if lax.axis_size("f") == 2:
            here = lax.axis_index("f")
            self.x, sent = pick(x, here), pick(x, 1 - here)
            self.coming = swap(sent, "f")
            return sent
        self.x = lax.psum_scatter(x, "f", scatter_dimension=0, tiled=False)
        self.coming = jnp.zeros_like(self.x)
        return self.x

    def hop(self, axis, pairs, others):
        self.x = self.x + tie(self.coming, *others)
        self.coming = lax.ppermute(self.x, axis, pairs)
        return self.x

    def near_y(self, *others):
        return self.hop("y", SWAP, others)

    def near_z(self, *others):
        return self.hop("z", plane_pairs(1), others)

    def far_z(self, *others):
        return self.hop("z", plane_pairs(2), others)

    def result(self, *others):
        self.total = self.x + tie(self.coming, *others)
        if lax.axis_size("g") > 1:
            self.total = lax.psum(self.total, "g")
        return self.total

    def vectors(self):
        at = 0
        for size in self.sizes:
            yield self.total[at : at + size]
            at += size


def arrivals(count):
    table = []
    for z in range(count):
        hops = []
        for t in range(1, count):
            if z - t >= 0:
                hops.append(("up", t))
            if z + t < count:
                hops.append(("down", t))
        table.append(hops)
    return table


def gather_planes(x, use, beside, later):
    z = lax.axis_index("z")
    count = lax.axis_size("z")
    table = arrivals(count)
    up, down = x, x
    hops = {}
    blocks, planes, used = [x], [z], []
    for t in range(1, count):
        up = lax.ppermute(up, "z", [(i, i + 1) for i in range(t - 1, count - 1)])
        down = lax.ppermute(down, "z", [(i, i - 1) for i in range(1, count - t + 1)])
        made = use(blocks[-1])
        before = used.pop() if used else []
        up, down, before, made[0], extra, _ = lax.optimization_barrier(
            (up, down, before, made[0], later[t - 1](blocks), beside[t - 1])
        )
        later[t - 1](blocks, extra)
        used += [before] * (t > 1) + [made]
        hops["up", t], hops["down", t] = up, down
        names = sorted({table[i][t - 1] for i in range(count)})
        block, plane = None, z
        for name in names:
            here = [i for i in range(count) if table[i][t - 1] == name]
            chosen = (z >= here[0]) & (z <= here[-1])
            block = hops[name] if block is None else jnp.where(chosen, hops[name], block)
            plane = jnp.where(chosen, z + (-name[1] if name[0] == "up" else name[1]), plane)
        blocks.append(block)
        planes.append(plane)
    used.append(use(blocks[-1]))
    return blocks, planes, used


def body(
    patches, pos_embed, lengths, out_grad,
    ln1_gain, ln1_bias, w_qkv, b_qv, w_out, b_out,
    ln2_gain, ln2_bias, w_fc1, b_fc1, w_fc2, b_fc2,
):
    f32, low = jnp.float32, jnp.bfloat16
    rows, width = patches.shape[1:]
    groups, parts = lax.axis_size("g"), lax.axis_size("f")
    head = lax.axis_index(SEQ)
    group = lax.axis_index("g")
    shard_index = lax.axis_index("f")
    scale = 1.0 / (parts * math.sqrt(rows * HEADS * groups))

    gain_one, bias_one, qv_bias = (
        join_small(vec).reshape(-1).astype(f32) for vec in (ln1_gain, ln1_bias, b_qv)
    )
    hidden = patches[0].astype(f32) + pos_embed[0].astype(f32)
    normed_pre, scaled_one, inv_one = norm_forward(hidden, gain_one, bias_one)
    normed = normed_pre.astype(low)

    shard_rows = w_qkv.shape[0]
    z, y, c = (lax.axis_index(axis) for axis in SEQ)
    place_in_plane = 2 * y + c
    plane_weights = join_small(plane_columns(tie(w_qkv, gain_one, bias_one, qv_bias), z)).reshape(parts, 12 * HEAD_DIM, shard_rows)
    q_bias, v_bias = (
        lax.dynamic_slice_in_dim(qv_bias, at + z * 4 * HEAD_DIM, 4 * HEAD_DIM).reshape(4, HEAD_DIM)
        for at in (0, width)
    )
    plane_bias = jnp.concatenate([q_bias, jnp.zeros((4, HEAD_DIM), f32), v_bias], axis=1).reshape(-1, 1)
    others = jnp.array([0, 1, 2, 3], jnp.int32)
    heads_made = others ^ place_in_plane

    def heads_of(block):
        own, core, near, far = project(heads_made, plane_weights, plane_bias, block)
        return [
            own, swap(core, "c"), swap(near, "y"),
            lax.ppermute(far, ("y", "c"), [(i, 3 - i) for i in range(4)]),
        ]

    out_taken, out_part = fetch_fsdp(w_out, 1, normed)
    fc1_taken, fc1_part = fetch_fsdp(w_fc1, 2, normed)
    fc2_taken, fc2_part = fetch_fsdp(w_fc2, 2, normed)
    if parts == 2:
        fc2_part = [swap(tie(part, fc1_part[1]), "f") for part in fc2_taken]
    qkv_taken, qkv_part = fetch_fsdp(w_qkv, 2, normed)
    out_full = join_fsdp(w_out, share_cores(out_part))
    beside = [
        out_taken + fc1_taken + fc2_taken + qkv_taken, out_part, fc1_part[:1] + [out_full],
    ]
    near_blocks = []

    def swap_later(first):
        def step(blocks, done=None):
            if done is None:
                return [swap(blocks[first], "y")] if first is not None else []
            near_blocks.extend(done)

        return step

    later = [swap_later(None), swap_later(0), swap_later(1)]
    blocks, planes, made = gather_planes(normed, heads_of, beside, later)
    blocks_at = jnp.concatenate([plane * 4 + heads_made for plane in planes])
    made = [piece for round_made in made for piece in round_made]
    if groups > 1:
        qkv = assemble(made, blocks_at)
    ends = jnp.cumsum(lengths[0]).astype(jnp.int32)
    base = (group * (rows * HEADS)).astype(jnp.int32).reshape(1)
    shift, window = 0, None
    up = [(i, i + 1) for i in range(groups - 1)]
    down = [(i + 1, i) for i in range(groups - 1)]
    if groups > 1:
        margin = -(-LONG // rows)
        shift = margin * rows
        both = qkv[:, HEAD_DIM:]
        before = lax.ppermute(both[HEADS - margin :], "g", up)
        after = lax.ppermute(both[:margin], "g", down)
        window = jnp.concatenate([before, both, after], axis=0)
    if groups > 1:
        attended, log_total = attention_forward(ends, base, [qkv], None, window, shift)
    else:
        attended, log_total, qkv = attention_forward(ends, base, made, blocks_at, None, 0)
    attended, near_last = lax.optimization_barrier((attended, swap(blocks[2], "y")))
    near_blocks.append(near_last)
    fc2_part = share_cores(fc2_part, attended)
    fc1_full = join_fsdp(w_fc1, share_cores(fc1_part), attended)
    fc2_full = join_fsdp(w_fc2, fc2_part, attended)
    small = (b_out, ln2_gain, ln2_bias, b_fc1, b_fc2)
    packed, at, total = 0.0, 0, sum(vec.shape[0] for vec in small)
    for vec in small:
        packed += jnp.pad(vec, (at, total - at - vec.shape[0]))
        at += vec.shape[0]
    packed = join_small(tie(packed, normed))
    vectors, at = [], 0
    for vec in small:
        size = vec.shape[0]
        vectors.append(packed[:, at : at + size].reshape(-1).astype(f32))
        at += size
    out_bias, gain_two, bias_two, fc1_bias, fc2_bias = vectors
    mixed = lax.all_to_all(attended, SEQ, 0, 0, tiled=True).reshape(width, rows)

    branch = dot(mixed, out_full, 0, 0) + out_bias
    middle = hidden + tie(branch, fc2_full, qkv_part[0])
    normed_two_pre, scaled_two, inv_two = norm_forward(middle, gain_two, bias_two)
    normed_two = normed_two_pre.astype(low)
    inner_sum = dot(normed_two, fc1_full, 1, 0) + fc1_bias
    active, gelu_pull = jax.vjp(partial(jax.nn.gelu, approximate=True), inner_sum)
    active_low = active.astype(low)

    out_cot = out_grad[0]
    cot_full = out_cot.astype(f32)
    active_low, *qkv_part = lax.optimization_barrier((active_low, *qkv_part))
    qkv_part = share_cores(qkv_part)
    fc2_sum = WeightSum([(active_low, out_cot, 0)], scale)
    token = fc2_sum.other_core()
    active_grad = dot(tie(out_cot, token), fc2_full, 1, 1)
    inner_grad = gelu_pull(active_grad)[0].astype(low)
    near_blocks.append(swap(tie(blocks[3], fc2_full), "y"))
    token = fc2_sum.other_f(inner_grad, near_blocks[3])
    norm_two_grad = dot(tie(inner_grad, token), fc1_full, 1, 1)
    gain_two_grad, bias_two_grad, middle_from_norm = norm_backward(
        norm_two_grad, scaled_two, inv_two, gain_two
    )
    middle_grad = cot_full + middle_from_norm
    branch_grad = middle_grad.astype(low)
    mixed_grad = dot(out_full, branch_grad, 1, 1).astype(low)
    attended_grad = lax.all_to_all(
        mixed_grad.reshape(HEADS, HEAD_DIM, rows), SEQ, 0, 0, tiled=True
    )
    rest_sum = WeightSum([(normed_two, inner_grad, 0), (mixed, branch_grad, 1)], scale)
    token = rest_sum.other_core(mixed_grad)
    token = fc2_sum.near_y(token)
    token = rest_sum.other_f(token, *fc2_sum.far[1:])
    column = list(blocks)
    across = [swap(tie(block, mixed_grad), "c") for block in column + near_blocks]
    tokens = [token] + across

    plan = [
        [fc2_sum.near_z, rest_sum.near_y],
        [fc2_sum.far_z, rest_sum.near_z],
        [fc2_sum.back_near_z, rest_sum.far_z],
        [fc2_sum.back_y],
        [rest_sum.back_near_z, lambda *after: fc2_sum.near],
        [rest_sum.back_y],
    ]
    carried, first = None, 0
    for chunk in [HEADS] if groups > 1 else CHUNKS:
        results = attention_backward(
            ends, tie(base, *tokens), qkv, window, attended, attended_grad, log_total, shift,
            first, chunk, carried,
        )
        carried, first = results[::-1], first + chunk
        tokens = []
        for move in plan.pop(0):
            tokens.append(move(results[0], *tokens))
    for moves in plan:
        for move in moves:
            tokens.append(move(results[0]))
    head_grad, *window_grad = results
    if groups > 1:
        both = window_grad[0]
        inner = both[margin : margin + HEADS]
        before = lax.ppermute(both[:margin], "g", down)
        after = lax.ppermute(both[margin + HEADS :], "g", up)
        inner = inner.at[HEADS - margin :].add(before).at[:margin].add(after)
        head_grad = jnp.concatenate([head_grad, inner.astype(low)], axis=1)
    token_grad = lax.all_to_all(tie(head_grad, *tokens), SEQ, 0, 0, tiled=True)

    weight_part = head_weight(
        jnp.concatenate([jnp.stack(planes) * 4 + (place_in_plane ^ k) for k in (0, 2, 1, 3)]).astype(jnp.int32),
        head_grad,
        column + near_blocks + across,
    )
    block_out = dot(tie(active_low, weight_part), fc2_full, 1, 0) + fc2_bias
    block_out = (middle + block_out).astype(low)
    weight_part = weight_part.reshape(3 * HEAD_DIM, parts, shard_rows).transpose(1, 0, 2)
    if parts == 2:
        weight_part = halve(weight_part, "f")
    else:
        weight_part = lax.psum_scatter(weight_part, "f", scatter_dimension=0, tiled=False)
    if groups > 1:
        weight_part = lax.psum(weight_part, "g")

    weight_part = (weight_part * scale).astype(low)
    qkv_full = join_fsdp(w_qkv, qkv_part, weight_part, block_out)
    (fc2_grad,) = fc2_sum.results(qkv_full)
    fc1_grad, out_weight_grad = rest_sum.results(fc2_grad)
    hops = [weight_part] + [
        lax.ppermute(weight_part, "z", [(i, (i + k) % 4) for i in range(4)]) for k in range(1, 4)
    ]
    token_grad, fc1_grad, out_weight_grad, *hops = lax.optimization_barrier(
        (token_grad, fc1_grad, out_weight_grad, *hops)
    )

    token_grad = (
        tie(token_grad, fc2_grad).reshape(HEADS, 3, HEAD_DIM, rows).transpose(1, 0, 2, 3).reshape(3 * width, rows)
    )
    norm_one_grad = dot(token_grad, qkv_full, 0, 1)
    gain_one_grad, bias_one_grad, hidden_from_norm = norm_backward(
        norm_one_grad, scaled_one, inv_one, gain_one
    )
    patch_grad = middle_grad + hidden_from_norm

    head_sums = jnp.sum(head_grad.astype(f32), axis=(0, 2))
    qv_grad = jnp.zeros((2 * width,), f32)
    qv_grad = lax.dynamic_update_slice(qv_grad, head_sums[:HEAD_DIM], (head * HEAD_DIM,))
    qv_grad = lax.dynamic_update_slice(
        qv_grad, head_sums[2 * HEAD_DIM :], (width + head * HEAD_DIM,)
    )
    late = VectorSum(
        (
            gain_one_grad,
            bias_one_grad,
            qv_grad,
            jnp.sum(branch_grad.astype(f32), axis=0),
            gain_two_grad,
            bias_two_grad,
            jnp.sum(inner_grad.astype(f32), axis=0),
            jnp.sum(cot_full, axis=0),
        ),
        scale,
    )
    token = late.core()
    token = late.other_f(token)
    pieces = hops + [swap(piece, "y") for piece in hops]
    pieces += [swap(tie(piece, gain_one_grad), "c") for piece in pieces]
    token = late.near_y(token)
    token = late.near_z(token)
    late.far_z(token)
    firsts = lax.rem(z + 4 - jnp.arange(4, dtype=jnp.int32), 4) * 4
    near_places = [firsts + 2 * y + c, firsts + 2 * (1 - y) + c]
    places = jnp.concatenate(near_places + [place_at + 1 - 2 * c for place_at in near_places])
    qkv_weight_grad = weave(pieces, places)
    late.result()
    (
        ln1_gain_sum, ln1_bias_sum, qv_sum, out_bias_sum,
        ln2_gain_sum, ln2_bias_sum, fc1_bias_sum, fc2_bias_sum,
    ) = late.vectors()
    return (
        block_out[None],
        patch_grad[None],
        ln1_gain_sum,
        ln1_bias_sum,
        qkv_weight_grad,
        qv_sum,
        out_weight_grad,
        out_bias_sum,
        ln2_gain_sum,
        ln2_bias_sum,
        fc1_grad,
        fc1_bias_sum,
        fc2_grad,
        fc2_bias_sum,
    )


def solution(mesh):
    seq, parts = mesh.shape["seq"], mesh.shape["fsdp"]
    fine = Mesh(mesh.devices.reshape(seq // HEADS, HEADS // 4, 2, 2, parts), ("g", "z", "y", "c", "f"))
    rows = P("f", ("g",) + SEQ, None)
    vec, mat = P("f"), P("f", None)
    in_specs = (rows, rows, mat, rows, vec, vec, mat, vec, mat, vec, vec, vec, mat, vec, mat, vec)
    out_specs = (rows, rows, vec, vec, mat, vec, mat, vec, vec, vec, mat, vec, mat, vec)
    return jax.shard_map(body, mesh=fine, in_specs=in_specs, out_specs=out_specs, check_vma=False)
```
